512 devices in a mesh: dom: 128 (over z, y, core), rep: 4 (over x).
Axes of the slice: x: 4, y: 4, z: 16, core: 2. Of those that a mesh axis runs over, the one named last changes fastest.
Arguments:
- node_feats: bfloat16 [4, 16384, 256], P('rep', 'dom'), may hold values from -6 to 6
- out_grad: bfloat16 [4, 16384, 256], P('rep', 'dom'), may hold values from -24 to 24
- norm1_gain: float32 [256], replicated, may hold values from 0.1 to 1.9
- w_query: bfloat16 [256, 256], replicated, may hold values from -0.375 to 0.375
- w_key: bfloat16 [256, 256], replicated, may hold values from -0.375 to 0.375
- w_value: bfloat16 [256, 256], replicated, may hold values from -0.375 to 0.375
- w_out: bfloat16 [256, 256], replicated, may hold values from -0.375 to 0.375
- norm2_gain: float32 [256], replicated, may hold values from 0.1 to 1.9
- w_up: bfloat16 [256, 512], replicated, may hold values from -0.375 to 0.375
- w_down: bfloat16 [512, 256], replicated, may hold values from -0.25 to 0.25
- local_gain: float32 [4], replicated, may hold values from 0.5 to 2
- expander_gain: float32 [4], replicated, may hold values from 2 to 8
- partner_perm: int32 [4, 4, 128, 128], P('rep', None, 'dom'), may hold values from 0 to 127, each once within a row
- block_pairs: int32 [4, 128, 1], P('rep', 'dom'), may hold values from 0 to 0, as said below
- pair_count: int32 [4, 128], P('rep', 'dom'), may hold values from 1 to 1, as said below
Outputs:
- node_out: bfloat16 [4, 16384, 256], P('rep', 'dom')
- grad_feats: bfloat16 [4, 16384, 256], P('rep', 'dom')
- grad_norm1_gain: float32 [256], replicated
- grad_w_query: float32 [256, 256], replicated
- grad_w_key: float32 [256, 256], replicated
- grad_w_value: float32 [256, 256], replicated
- grad_w_out: float32 [256, 256], replicated
- grad_norm2_gain: float32 [256], replicated
- grad_w_up: float32 [256, 512], replicated
- grad_w_down: float32 [512, 256], replicated
- grad_local_gain: float32 [4], replicated
- grad_expander_gain: float32 [4], replicated
The draws below stay inside these ranges and needn't reach their ends.
Inputs may be any that keep to these rules, and one draw needn't show every extreme that they name: `partner_perm`: each row is a permutation of the 128 local node indices. `block_pairs`: an entry e names query block e // 1 and key block e % 1 of the same partition; the first pair_count entries of a partition are distinct, the rest are not edges. `pair_count`: in every cluster some partition has exactly 1 pairs and another exactly 1.
All inputs are finite; a program needn't handle non-finite values.
Results may differ from the reference program's by a relative error of at most 0.029.
Values may be sent and summed in bfloat16 or wider, within the bound.
A program may use at most 64 MiB of HBM per device.

```python
import math
import jax
import jax.numpy as jnp
from jax import lax

D = 256
H = 4
FF = 512
BLK = 128
MATCH = 4
NODE_DEV = 128
HD = 64
NB = 1
MAXP = 1
NODES = 16384
CLUSTERS = 4
N_DOM = 128


def pair_tables(key):
    folded = jax.random.fold_in(key, 11)
    rolled_key, busy_key, drawn_key, order_key = jax.random.split(folded, 4)
    spread = 64
    rolled = jax.random.randint(rolled_key, (CLUSTERS, N_DOM), 0, spread + 1)
    headroom = MAXP - NB
    surplus = headroom * rolled * rolled * rolled // (spread * spread * spread)
    busiest = jax.random.randint(busy_key, (CLUSTERS, 1), 0, N_DOM)
    calmest = (busiest + jax.random.randint(drawn_key, (CLUSTERS, 1), 1, N_DOM)) % N_DOM
    columns = jnp.arange(N_DOM)[None, :]
    surplus = jnp.where(columns == busiest, headroom, surplus)
    surplus = jnp.where(columns == calmest, 0, surplus)
    counted = (NB + surplus).astype(jnp.int32)
    candidates = NB * NB
    jitter = jax.random.randint(order_key, (CLUSTERS, N_DOM, candidates), 0, 1 << 20)
    ranked = jitter * candidates + jnp.arange(candidates)[None, None, :]
    ordering = jnp.argsort(ranked, axis=-1)
    return (ordering[:, :, :MAXP].astype(jnp.int32), counted)


def draw_block_pairs(key, part):
    return pair_tables(key)[0]


def draw_pair_count(key, part):
    return pair_tables(key)[1]


def strengthened(values, rng, source, target, parts, factor):
    def block_of(axis_at):
        return (jnp.arange(values.shape[axis_at]) // (values.shape[axis_at] // parts)).reshape((-1,) + (1,) * (values.ndim - 1 - axis_at))

    one_side = jax.random.permutation(rng, parts)[block_of(target)]
    other_side = (block_of(target) + parts // 2) % parts
    return jnp.where((block_of(source) == one_side) | (block_of(source) == other_side), factor * values, values)


def level_of(stream_key, dims, pieces, least, largest):
    level = 1.0
    for position, parts in pieces:
        steps = jax.random.uniform(jax.random.fold_in(jax.random.fold_in(stream_key, 6), position), (parts,), jnp.float32, least / len(pieces), largest / len(pieces))
        level = level * jnp.repeat(jnp.exp(steps), dims[position] // parts).reshape((-1,) + (1,) * (len(dims) - 1 - position))
    return level


def centred(key, extent, deviation, reach, cuts=(), kind=jnp.bfloat16):
    array = jax.random.normal(key, extent, jnp.float32) * deviation
    if len(cuts) > 0:
        array = level_of(key, extent, cuts, -0.22, 0.18) * array
    return jnp.clip(array, min=-reach, max=reach).astype(kind)


def heavy_noise(rng, extent, scale, most, pieces, heavy, held_as=jnp.bfloat16):
    values = scale * jax.random.normal(rng, extent, jnp.float32)
    if pieces:
        values = values * level_of(rng, extent, pieces, -0.22, 0.18)
    return jnp.clip(strengthened(values, jax.random.fold_in(rng, 3), *heavy), -most, most).astype(held_as)


def setup_inputs(seed: int = 0) -> dict:
    arg_keys = jax.random.split(jax.random.key(seed), 16)
    return {
        "node_feats": centred(arg_keys[0], (CLUSTERS, NODES, D), 1.0, 6.0, ((0, 4), (1, 128))),
        "out_grad": heavy_noise(arg_keys[1], (CLUSTERS, NODES, D), 1.0, 24.0, ((0, 4), (1, 128)), (1, 2, 128, 5.5)),
        "norm1_gain": jnp.clip(1.0 + 0.18 * jax.random.normal(arg_keys[2], (D,), jnp.float32), 0.1, 1.9),
        "w_query": centred(arg_keys[3], (D, D), D ** -0.5, 0.375),
        "w_key": centred(arg_keys[4], (D, D), D ** -0.5, 0.375),
        "w_value": centred(arg_keys[5], (D, D), D ** -0.5, 0.375),
        "w_out": centred(arg_keys[6], (D, D), D ** -0.5, 0.375),
        "norm2_gain": jnp.clip(1.0 + 0.18 * jax.random.normal(arg_keys[7], (D,), jnp.float32), 0.1, 1.9),
        "w_up": centred(arg_keys[8], (D, FF), D ** -0.5, 0.375),
        "w_down": centred(arg_keys[9], (FF, D), FF ** -0.5, 0.25),
        "local_gain": jnp.clip(jnp.exp(jax.random.uniform(arg_keys[10], (H,), jnp.float32, math.log(0.5), math.log(2.0))), 0.5, 2.0),
        "expander_gain": jnp.clip(jnp.exp(jax.random.uniform(arg_keys[11], (H,), jnp.float32, math.log(2.0), math.log(8.0))), 2.0, 8.0),
        "partner_perm": jax.vmap(lambda own: jax.random.permutation(own, NODE_DEV))(jax.random.split(arg_keys[12], CLUSTERS * MATCH * N_DOM)).reshape((CLUSTERS, MATCH, N_DOM, NODE_DEV)).astype(jnp.int32),
        "block_pairs": draw_block_pairs(jax.random.fold_in(arg_keys[15], 71), 0),
        "pair_count": draw_pair_count(jax.random.fold_in(arg_keys[15], 71), 0),
    }


EPSILON = 1e-05
SCORE_CAP = 5.0
GELU_ROOT = 0.7978845608028654
GELU_CUBIC = 0.044715

def rounded(matrix):
    return lax.optimization_barrier(matrix.astype(jnp.bfloat16)).astype(jnp.float32)

def gelu_parts(preact):
    tangent = jnp.tanh(GELU_ROOT * (preact + GELU_CUBIC * preact * preact * preact))
    result = 0.5 * preact * (1.0 + tangent)
    derivative = 0.5 * (1.0 + tangent) + 0.5 * preact * (1.0 - tangent * tangent) * GELU_ROOT * (1.0 + 3.0 * GELU_CUBIC * preact * preact)
    return (result, derivative)

def norm_forward(matrix):
    center = lax.optimization_barrier(jnp.mean(matrix, axis=-1, keepdims=True))
    shifted = matrix - center
    inverse = lax.rsqrt(lax.optimization_barrier(jnp.mean(shifted * shifted, axis=-1, keepdims=True)) + EPSILON)
    return (shifted * inverse, inverse)

def norm_backward(upstream, normed, inverse, gain):
    scaled_up = upstream * gain
    return inverse * (scaled_up - lax.optimization_barrier(jnp.mean(scaled_up, axis=-1, keepdims=True)) - normed * lax.optimization_barrier(jnp.mean(scaled_up * normed, axis=-1, keepdims=True)))

def project(first_op, second_op):
    return jnp.dot(first_op, second_op, preferred_element_type=jnp.float32)

def project_back(first_op, second_op):
    return lax.dot_general(first_op, second_op, (((1,), (1,)), ((), ())), preferred_element_type=jnp.float32)

def project_outer(first_op, second_op):
    return lax.dot_general(first_op, second_op, (((0,), (0,)), ((), ())), preferred_element_type=jnp.float32)

def block_mask(pair_list, listed):
    active = (jnp.arange(MAXP) < listed).astype(jnp.float32)
    hits = (pair_list[:, None] == jnp.arange(NB * NB, dtype=jnp.int32)[None, :]).astype(jnp.float32)
    blocks = lax.optimization_barrier(jnp.sum(hits * active[:, None], axis=0)).reshape(NB, NB)
    return jnp.repeat(jnp.repeat(blocks, BLK, axis=0), BLK, axis=1)

def reference(node_feats, out_grad, norm1_gain, w_query, w_key, w_value, w_out, norm2_gain, w_up, w_down, local_gain, expander_gain, partner_perm, block_pairs, pair_count):
    levels = N_DOM.bit_length() - 1
    flip_bits = [(levels - 1 - matching) % levels for matching in range(MATCH)]
    score_scale = float(HD) ** 0.5
    devices = jnp.arange(N_DOM, dtype=jnp.int32)
    local_col = local_gain[:, None, None]
    far_col = expander_gain[None, :, None]
    node_outs = []
    feat_grads = []
    grad_totals = None
    for cluster in range(CLUSTERS):
        features = node_feats[cluster].astype(jnp.float32)
        normed1, inverse1 = norm_forward(features)
        hidden = (normed1 * norm1_gain).astype(jnp.bfloat16)
        queries = project(hidden, w_query).astype(jnp.bfloat16).reshape(N_DOM, NODE_DEV, D)
        key_rows = project(hidden, w_key).astype(jnp.bfloat16).reshape(N_DOM, NODE_DEV, D)
        value_rows = project(hidden, w_value).astype(jnp.bfloat16).reshape(N_DOM, NODE_DEV, D)
        partners = partner_perm[cluster]
        pair_lists = block_pairs[cluster]
        pair_totals = pair_count[cluster]

        def attend(device):
            own_query = queries[device].astype(jnp.float32).reshape(NODE_DEV, H, HD)
            own_key = key_rows[device].astype(jnp.float32).reshape(NODE_DEV, H, HD)
            own_value = value_rows[device].astype(jnp.float32).reshape(NODE_DEV, H, HD)
            nodemask = block_mask(pair_lists[device], pair_totals[device])
            raw_local = jnp.einsum('ihd,jhd->hij', own_query, own_key) / score_scale
            tanh_local = jnp.tanh(local_col * raw_local / SCORE_CAP)
            exp_local = jnp.exp(SCORE_CAP * tanh_local) * nodemask[None]
            far_keys = []
            far_values = []
            for matching in range(MATCH):
                source = jnp.bitwise_xor(device, 1 << flip_bits[matching])
                picked = partners[matching][device]
                far_keys.append(key_rows[source][picked])
                far_values.append(value_rows[source][picked])
            far_key = jnp.stack(far_keys).astype(jnp.float32).reshape(MATCH, NODE_DEV, H, HD)
            far_value = jnp.stack(far_values).astype(jnp.float32).reshape(MATCH, NODE_DEV, H, HD)
            raw_far = jnp.einsum('ihd,mihd->mhi', own_query, far_key) / score_scale
            tanh_far = jnp.tanh(far_col * raw_far / SCORE_CAP)
            exp_far = jnp.exp(SCORE_CAP * tanh_far)
            denominator = lax.optimization_barrier(jnp.sum(exp_local, axis=-1)) + lax.optimization_barrier(jnp.sum(exp_far, axis=0))
            weight_local = rounded(exp_local / denominator[:, :, None])
            weight_far = rounded(exp_far / denominator[None])
            attended = jnp.einsum('hij,jhd->ihd', weight_local, own_value) + jnp.einsum('mhi,mihd->ihd', weight_far, far_value)
            saved = (own_query, own_key, own_value, far_key, far_value, raw_local, tanh_local, weight_local, raw_far, tanh_far, weight_far)
            return (attended.reshape(NODE_DEV, D), saved)
        attended32 = lax.map(lambda device: attend(device)[0], devices)
        attended = attended32.reshape(NODES, D).astype(jnp.bfloat16)
        mixed = (features + project(attended, w_out)).astype(jnp.bfloat16)
        normed2, inverse2 = norm_forward(mixed.astype(jnp.float32))
        hidden2 = (normed2 * norm2_gain).astype(jnp.bfloat16)
        preact = project(hidden2, w_up)
        activ, derivative = gelu_parts(preact)
        activ = activ.astype(jnp.bfloat16)
        node_outs.append((mixed.astype(jnp.float32) + project(activ, w_down)).astype(jnp.bfloat16))
        upstream = out_grad[cluster]
        grad_down = project_outer(activ, upstream)
        grad_pre = (project_back(upstream, w_down) * derivative).astype(jnp.bfloat16)
        grad_up = project_outer(hidden2, grad_pre)
        grad_hidden2 = project_back(grad_pre, w_up)
        grad_gain2 = lax.optimization_barrier(jnp.sum(grad_hidden2 * normed2, axis=0))
        grad_mixed = upstream.astype(jnp.float32) + norm_backward(grad_hidden2, normed2, inverse2, norm2_gain)
        grad_mixed16 = grad_mixed.astype(jnp.bfloat16)
        grad_wout = project_outer(attended, grad_mixed16)
        grad_att = project_back(grad_mixed16, w_out).astype(jnp.bfloat16).reshape(N_DOM, NODE_DEV, D)

        def backward_rows(device):
            _, saved = attend(device)
            own_query, own_key, own_value, far_key, far_value, raw_local, tanh_local, weight_local, raw_far, tanh_far, weight_far = saved
            grad_out = grad_att[device].astype(jnp.float32).reshape(NODE_DEV, H, HD)
            delta = jnp.einsum('ihd,ihd->hi', grad_out, attended32[device].reshape(NODE_DEV, H, HD))
            dots_local = jnp.einsum('ihd,jhd->hij', grad_out, own_value)
            dlogit_local = weight_local * (dots_local - delta[:, :, None])
            slope_local = 1.0 - tanh_local * tanh_local
            gain_local_term = lax.optimization_barrier(jnp.sum(dlogit_local * raw_local * slope_local, axis=(1, 2)))
            dscore_local = rounded(dlogit_local * local_col * slope_local / score_scale)
            dots_far = jnp.einsum('ihd,mihd->mhi', grad_out, far_value)
            dlogit_far = weight_far * (dots_far - delta[None])
            slope_far = 1.0 - tanh_far * tanh_far
            gain_far_term = lax.optimization_barrier(jnp.sum(dlogit_far * raw_far * slope_far, axis=(0, 2)))
            dscore_far = rounded(dlogit_far * far_col * slope_far / score_scale)
            grad_query = jnp.einsum('hij,jhd->ihd', dscore_local, own_key) + jnp.einsum('mhi,mihd->ihd', dscore_far, far_key)
            grad_key = jnp.einsum('hij,ihd->jhd', dscore_local, own_query)
            grad_value = jnp.einsum('hij,ihd->jhd', weight_local, grad_out)
            return (grad_query.reshape(NODE_DEV, D), grad_key.reshape(NODE_DEV, D), grad_value.reshape(NODE_DEV, D), dscore_far, weight_far, gain_local_term, gain_far_term)
        grad_query, key_local, value_local, dscore_far, weight_far, gain_local_terms, gain_far_terms = lax.map(backward_rows, devices)

        def receive_rows(device):
            key_total = key_local[device]
            value_total = value_local[device]
            for matching in range(MATCH):
                source = jnp.bitwise_xor(device, 1 << flip_bits[matching])
                source_query = queries[source].astype(jnp.float32).reshape(NODE_DEV, H, HD)
                source_grad = grad_att[source].astype(jnp.float32).reshape(NODE_DEV, H, HD)
                key_term = rounded(jnp.einsum('hi,ihd->ihd', dscore_far[source, matching], source_query).reshape(NODE_DEV, D))
                value_term = rounded(jnp.einsum('hi,ihd->ihd', weight_far[source, matching], source_grad).reshape(NODE_DEV, D))
                placed = partners[matching][source]
                key_total = key_total + jnp.zeros((NODE_DEV, D), jnp.float32).at[placed].set(key_term)
                value_total = value_total + jnp.zeros((NODE_DEV, D), jnp.float32).at[placed].set(value_term)
            return (key_total, value_total)
        key_total, value_total = lax.map(receive_rows, devices)
        grad_query16 = grad_query.reshape(NODES, D).astype(jnp.bfloat16)
        grad_key16 = key_total.reshape(NODES, D).astype(jnp.bfloat16)
        grad_value16 = value_total.reshape(NODES, D).astype(jnp.bfloat16)
        grad_wq = project_outer(hidden, grad_query16)
        grad_wk = project_outer(hidden, grad_key16)
        grad_wv = project_outer(hidden, grad_value16)
        grad_hidden = project_back(grad_query16, w_query) + project_back(grad_key16, w_key) + project_back(grad_value16, w_value)
        grad_gain1 = lax.optimization_barrier(jnp.sum(grad_hidden * normed1, axis=0))
        feat_grads.append((grad_mixed + norm_backward(grad_hidden, normed1, inverse1, norm1_gain)).astype(jnp.bfloat16))
        cluster_grads = (grad_gain1, grad_wq, grad_wk, grad_wv, grad_wout, grad_gain2, grad_up, grad_down, lax.optimization_barrier(jnp.sum(gain_local_terms, axis=0)), lax.optimization_barrier(jnp.sum(gain_far_terms, axis=0)))
        if grad_totals is None:
            grad_totals = cluster_grads
        else:
            grad_totals = tuple((former + latter for former, latter in zip(grad_totals, cluster_grads)))
    return (jnp.stack(node_outs), jnp.stack(feat_grads), grad_totals[0], grad_totals[1], grad_totals[2], grad_totals[3], grad_totals[4], grad_totals[5], grad_totals[6], grad_totals[7], grad_totals[8], grad_totals[9])
```

```python
import jax
import jax.numpy as jnp
from jax import lax
from jax.experimental import pallas as pl
from jax.experimental.pallas import tpu as pltpu
from jax.sharding import PartitionSpec as P

BLK = 128


EPSILON = 1e-05
SCORE_CAP = 5.0
GELU_ROOT = 0.7978845608028654
GELU_CUBIC = 0.044715


def swapped(x, axis, bit):
    return lax.ppermute(x, axis, [(i, i ^ 1 << bit) for i in range(lax.axis_size(axis))])


def gelu_parts(preact):
    tangent = jnp.tanh(GELU_ROOT * (preact + GELU_CUBIC * preact * preact * preact))
    result = 0.5 * preact * (1.0 + tangent)
    derivative = 0.5 * (1.0 + tangent) + 0.5 * preact * (1.0 - tangent * tangent) * GELU_ROOT * (
        1.0 + 3.0 * GELU_CUBIC * preact * preact
    )
    return (result, derivative)


def norm_forward(matrix):
    center = jnp.mean(matrix, axis=-1, keepdims=True)
    shifted = matrix - center
    inverse = lax.rsqrt(jnp.mean(shifted * shifted, axis=-1, keepdims=True) + EPSILON)
    return (shifted * inverse, inverse)


def norm_backward(upstream, normed, inverse, gain):
    scaled_up = upstream * gain
    return inverse * (
        scaled_up
        - jnp.mean(scaled_up, axis=-1, keepdims=True)
        - normed * jnp.mean(scaled_up * normed, axis=-1, keepdims=True)
    )


def project(first_op, second_op):
    return jnp.dot(first_op, second_op, preferred_element_type=jnp.float32)


def project_back(first_op, second_op):
    return lax.dot_general(
        first_op, second_op, (((1,), (1,)), ((), ())), preferred_element_type=jnp.float32
    )


def project_outer(first_op, second_op):
    return lax.dot_general(
        first_op, second_op, (((0,), (0,)), ((), ())), preferred_element_type=jnp.float32
    )


def soft_scores(query_tile, key_tile, gain_col, score_scale):
    raw_scores = (
        jnp.einsum("ihd,jhd->hij", query_tile, key_tile, preferred_element_type=jnp.float32)
        / score_scale
    )
    tangent = jnp.tanh(gain_col * raw_scores / SCORE_CAP)
    return (raw_scores, tangent, jnp.exp(SCORE_CAP * tangent))


def add_block(running, addend):
    return running + addend


XY = 16
ZS = 16
PIECE = 16
MESH = pl.DeviceIdType.MESH


def place():
    dom = lax.axis_index("dom")
    rep = lax.axis_index("rep")
    return dom // 8, (dom // 2) % 4, dom % 2, rep


def device(z, y, c, x):
    return {"dom": (z * 4 + y) * 2 + c, "rep": x}


def plane_peer(step):
    z, y, c, x = place()
    far_x = (x + step // 4) % 4
    far_y = (y + step % 4) % 4
    return far_x * 4 + far_y, device(z, far_y, c, far_x)


def column_peer(step):
    z, y, c, x = place()
    far_z = (z + step) % 16
    return far_z, device(far_z, y, c, x)


def enter():
    z, y, c, x = place()
    barrier = pltpu.get_barrier_semaphore()

    def greet(peer):
        pl.semaphore_signal(barrier, inc=1, device_id=peer, device_id_type=MESH)

    greet(device(z, y, 1 - c, x))

    def plane(step, carry):
        greet(plane_peer(step)[1])
        return carry

    def column(step, carry):
        greet(column_peer(step)[1])
        return carry

    lax.fori_loop(1, XY, plane, 0)
    lax.fori_loop(1, ZS, column, 0)
    pl.semaphore_wait(barrier, 1 + (XY - 1) + (ZS - 1))


def remote(src, dst, sems, at, peer):
    return pltpu.make_async_remote_copy(
        src_ref=src,
        dst_ref=dst,
        send_sem=sems.at[0, at],
        recv_sem=sems.at[1, at],
        device_id=peer,
        device_id_type=MESH,
    )


def each(first, last, body):
    def step(index, carry):
        body(index)
        return carry

    lax.fori_loop(first, last, step, 0)


def spread_small(total):
    row = lax.broadcasted_iota(jnp.int32, (8, 128), 0)
    high = total.astype(jnp.bfloat16).astype(jnp.float32)
    low = pltpu.roll(total - high, 1, 0)
    return jnp.where(row == 5, low, total).astype(jnp.bfloat16)


def join_small(parts):
    row = lax.broadcasted_iota(jnp.int32, (8, 128), 0)
    low = pltpu.roll(parts, 7, 0)
    return jnp.where(row == 4, parts + low, parts)


def sum_all(stage, core_in, mid, plane_in, column_out, column_in, last, full, sems):
    z, y, c, x = place()
    sibling = device(z, y, 1 - c, x)
    mine = x * 4 + y
    f32 = jnp.float32
    core_copy = remote(stage.at[1 - c], core_in, sems, 0, sibling)
    core_copy.start()
    core_copy.wait()
    small = join_small(stage[0, 256].astype(f32) + core_in[256].astype(f32))
    small16 = spread_small(small)

    def add_pair(piece):
        rows = pl.ds(piece * PIECE, PIECE)
        mid[piece, 0:PIECE] = (
            stage[c, rows].astype(f32) + core_in[rows].astype(f32)
        ).astype(jnp.bfloat16)
        mid[piece, PIECE] = small16

    each(0, XY, add_pair)

    def plane_copy(step):
        peer, where = plane_peer(step)
        return remote(mid.at[peer], plane_in.at[step], sems, step, where)

    each(1, XY, lambda step: plane_copy(step).start())
    each(1, XY, lambda step: plane_copy(step).wait_recv())
    total = mid[mine].astype(f32)
    for step in range(1, XY):
        total = total + plane_in[step].astype(f32)
    small16 = spread_small(join_small(total[PIECE]))
    column_out[:, 0] = total[0:PIECE].astype(jnp.bfloat16)
    for unit in range(ZS):
        column_out[unit, 1] = small16

    def column_copy(step):
        peer, where = column_peer(step)
        return remote(column_out.at[peer], column_in.at[step], sems, 16 + step, where)

    each(1, ZS, lambda step: column_copy(step).start())
    each(1, ZS, lambda step: column_copy(step).wait_recv())
    total = column_out[z].astype(f32)
    for step in range(1, ZS):
        total = total + column_in[step].astype(f32)
    small = join_small(total[1])
    last[z] = total[0].astype(jnp.bfloat16)

    def column_back(step):
        peer, where = column_peer(step)
        return remote(last.at[z], last.at[z], sems, 32 + step, where)

    each(1, ZS, lambda step: column_back(step).start())
    each(1, ZS, lambda step: column_back(step).wait_recv())
    full[c, mine] = last[...]

    def plane_back(step):
        peer, where = plane_peer(step)
        return remote(full.at[c, mine], full.at[c, mine], sems, 48 + step, where)

    def core_back(step):
        origin = ((x + 4 - step // 4) % 4) * 4 + (y + 4 - step % 4) % 4
        return remote(full.at[c, origin], full.at[c, origin], sems, 64 + step, sibling)

    each(1, XY, lambda step: plane_back(step).start())
    core_back(0).start()

    def pass_on(step):
        plane_back(step).wait_recv()
        core_back(step).start()

    each(1, XY, pass_on)
    each(0, XY, lambda step: core_back(step).wait())
    each(1, XY, lambda step: plane_copy(step).wait_send())
    each(1, ZS, lambda step: column_copy(step).wait_send())
    each(1, ZS, lambda step: column_back(step).wait_send())
    each(1, XY, lambda step: plane_back(step).wait_send())
    return small


def to_units(matrix):
    rows = matrix.shape[0]
    return [
        matrix[:, at : at + 128].reshape(rows // 8, 8, 128).astype(jnp.bfloat16)
        for at in range(0, matrix.shape[1], 128)
    ]


def sum_kernel(*refs):
    grads, small_ref, outs, small_out = refs[0:6], refs[6], refs[7:13], refs[13]
    stage, core_in, mid, plane_in, column_out, column_in, last, full, sems = refs[14:]
    spots = []
    counts = [0, 0]
    for number, ref in enumerate(grads):
        half = 0 if number < 4 else 1
        for column in range(0, ref.shape[1], 128):
            spots.append((number, column, half, counts[half]))
            counts[half] += ref.shape[0] // 8
    for number, column, half, at in spots:
        ref = grads[number]
        units = ref.shape[0] // 8
        stage[half, at : at + units] = (
            ref[:, column : column + 128].reshape(units, 8, 128).astype(jnp.bfloat16)
        )
    small16 = spread_small(small_ref[...])
    stage[0, 256] = small16
    stage[1, 256] = small16
    enter()
    small_out[...] = sum_all(
        stage, core_in, mid, plane_in, column_out, column_in, last, full, sems
    )
    for number, column, half, at in spots:
        ref = outs[number]
        units = ref.shape[0] // 8
        got = full[half, at // PIECE : (at + units) // PIECE].astype(jnp.float32)
        ref[:, column : column + 128] = got.reshape(units * 8, 128)


def sum_scratch():
    b16 = jnp.bfloat16
    return [
        pltpu.VMEM((2, 257, 8, 128), b16),
        pltpu.VMEM((257, 8, 128), b16),
        pltpu.VMEM((XY, PIECE + 1, 8, 128), b16),
        pltpu.VMEM((XY, PIECE + 1, 8, 128), b16),
        pltpu.VMEM((ZS, 2, 8, 128), b16),
        pltpu.VMEM((ZS, 2, 8, 128), b16),
        pltpu.VMEM((ZS, 8, 128), b16),
        pltpu.VMEM((2, XY, PIECE, 8, 128), b16),
        pltpu.SemaphoreType.DMA((2, 80)),
    ]


def sum_grads(grads, small):
    vmem = pl.BlockSpec(memory_space=pltpu.VMEM)
    shapes = [jax.ShapeDtypeStruct(g.shape, jnp.float32) for g in (*grads, small)]
    return pl.pallas_call(
        sum_kernel,
        out_shape=shapes,
        in_specs=[vmem] * 7,
        out_specs=[vmem] * 7,
        scratch_shapes=sum_scratch(),
        compiler_params=pltpu.CompilerParams(
            collective_id=0, has_side_effects=True, vmem_limit_bytes=40 * 1024 * 1024
        ),
    )(*grads, small)


def local(
    node_feats,
    out_grad,
    norm1_gain,
    w_query,
    w_key,
    w_value,
    w_out,
    norm2_gain,
    w_up,
    w_down,
    local_gain,
    expander_gain,
    partner_perm,
    block_pairs,
    pair_count,
):
    node_rows = node_feats[0]
    upstream = out_grad[0]
    partners = partner_perm[0, :, 0, :]
    listed = pair_count[0, 0]
    count_rows = node_rows.shape[0]
    width = node_rows.shape[1]
    heads = local_gain.shape[0]
    head_dim = width // heads
    matchings = partners.shape[0]
    levels = lax.axis_size("dom").bit_length() - 1
    score_scale = float(head_dim) ** 0.5
    local_col = local_gain[:, None, None]
    far_col = expander_gain[None, :, None]
    features = node_rows.astype(jnp.float32)
    normed1, inverse1 = norm_forward(features)
    hidden = (normed1 * norm1_gain).astype(jnp.bfloat16)
    queries = project(hidden, w_query).astype(jnp.bfloat16)
    key_rows = project(hidden, w_key).astype(jnp.bfloat16)
    value_rows = project(hidden, w_value).astype(jnp.bfloat16)
    far_keys = []
    far_values = []
    for matching in range(matchings):
        flip_bit = (levels - 1 - matching) % levels
        picked = partners[matching]
        their_keys, their_values = swapped((key_rows, value_rows), "dom", flip_bit)
        far_keys.append(their_keys[picked])
        far_values.append(their_values[picked])
    query_heads = queries.reshape(count_rows, heads, head_dim)
    far_key_heads = jnp.stack(far_keys).reshape(matchings, count_rows, heads, head_dim)
    far_value_heads = jnp.stack(far_values).reshape(matchings, count_rows, heads, head_dim)
    raw_far = (
        jnp.einsum("ihd,mihd->mhi", query_heads, far_key_heads, preferred_element_type=jnp.float32)
        / score_scale
    )
    tanh_far = jnp.tanh(far_col * raw_far / SCORE_CAP)
    exp_far = jnp.exp(SCORE_CAP * tanh_far)
    far_total = jnp.sum(exp_far, axis=0)

    def slice_heads(matrix):
        return matrix.reshape(BLK, heads, head_dim)

    def add_total(position, running):
        _, _, exp_tile = soft_scores(
            slice_heads(queries), slice_heads(key_rows), local_col, score_scale
        )
        return add_block(running, jnp.sum(exp_tile, axis=-1))

    denominator = lax.fori_loop(0, listed, add_total, far_total)
    weight_far = (exp_far / denominator[None]).astype(jnp.bfloat16)
    far_part = jnp.einsum(
        "mhi,mihd->ihd", weight_far, far_value_heads, preferred_element_type=jnp.float32
    ).reshape(count_rows, width)

    def add_rows(position, running):
        _, _, exp_tile = soft_scores(
            slice_heads(queries), slice_heads(key_rows), local_col, score_scale
        )
        weight_tile = (exp_tile / denominator[:, :, None]).astype(jnp.bfloat16)
        addend = jnp.einsum(
            "hij,jhd->ihd", weight_tile, slice_heads(value_rows), preferred_element_type=jnp.float32
        ).reshape(BLK, width)
        return add_block(running, addend)

    attended32 = lax.fori_loop(0, listed, add_rows, far_part)
    attended = attended32.astype(jnp.bfloat16)
    mixed = (features + project(attended, w_out)).astype(jnp.bfloat16)
    normed2, inverse2 = norm_forward(mixed.astype(jnp.float32))
    hidden2 = (normed2 * norm2_gain).astype(jnp.bfloat16)
    preact = project(hidden2, w_up)
    activ, derivative = gelu_parts(preact)
    activ = activ.astype(jnp.bfloat16)
    node_out = (mixed.astype(jnp.float32) + project(activ, w_down)).astype(jnp.bfloat16)
    grad_down = project_outer(activ, upstream)
    grad_pre = (project_back(upstream, w_down) * derivative).astype(jnp.bfloat16)
    grad_up = project_outer(hidden2, grad_pre)
    grad_hidden2 = project_back(grad_pre, w_up)
    grad_gain2 = jnp.sum(grad_hidden2 * normed2, axis=0)
    grad_mixed = upstream.astype(jnp.float32) + norm_backward(
        grad_hidden2, normed2, inverse2, norm2_gain
    )
    grad_mixed16 = grad_mixed.astype(jnp.bfloat16)
    grad_wout = project_outer(attended, grad_mixed16)
    grad_att = project_back(grad_mixed16, w_out).astype(jnp.bfloat16)
    grad_heads = grad_att.reshape(count_rows, heads, head_dim)
    delta = jnp.sum(
        (grad_att.astype(jnp.float32) * attended32).reshape(count_rows, heads, head_dim), axis=-1
    ).T
    dots_far = jnp.einsum(
        "ihd,mihd->mhi", grad_heads, far_value_heads, preferred_element_type=jnp.float32
    )
    dlogit_far = weight_far.astype(jnp.float32) * (dots_far - delta[None])
    slope_far = 1.0 - tanh_far * tanh_far
    far_gain_grad = jnp.sum(dlogit_far * raw_far * slope_far, axis=(0, 2))
    dscore_far = (dlogit_far * far_col * slope_far / score_scale).astype(jnp.bfloat16)
    grad_query32 = jnp.einsum(
        "mhi,mihd->ihd", dscore_far, far_key_heads, preferred_element_type=jnp.float32
    ).reshape(count_rows, width)
    key_terms = (
        jnp.einsum("mhi,ihd->mihd", dscore_far, query_heads, preferred_element_type=jnp.float32)
        .astype(jnp.bfloat16)
        .reshape(matchings, count_rows, width)
    )
    value_terms = (
        jnp.einsum("mhi,ihd->mihd", weight_far, grad_heads, preferred_element_type=jnp.float32)
        .astype(jnp.bfloat16)
        .reshape(matchings, count_rows, width)
    )
    returned = []
    for matching in range(matchings):
        flip_bit = (levels - 1 - matching) % levels
        placed_keys = (
            jnp.zeros((count_rows, width), jnp.bfloat16)
            .at[partners[matching]]
            .set(key_terms[matching])
        )
        placed_values = (
            jnp.zeros((count_rows, width), jnp.bfloat16)
            .at[partners[matching]]
            .set(value_terms[matching])
        )
        returned.append(swapped((placed_keys, placed_values), "dom", flip_bit))
    zero_rows = jnp.zeros((count_rows, width), jnp.float32)
    zero_gain = jnp.zeros((heads,), jnp.float32)

    def add_grads(position, running):
        query_acc, key_acc, value_acc, gain_acc = running
        query_tile = slice_heads(queries)
        key_tile = slice_heads(key_rows)
        value_tile = slice_heads(value_rows)
        grad_tile = slice_heads(grad_att)
        raw_tile, tanh_tile, exp_tile = soft_scores(query_tile, key_tile, local_col, score_scale)
        weight_tile = (exp_tile / denominator[:, :, None]).astype(jnp.bfloat16)
        dots_tile = jnp.einsum(
            "ihd,jhd->hij", grad_tile, value_tile, preferred_element_type=jnp.float32
        )
        dlogit_tile = weight_tile.astype(jnp.float32) * (dots_tile - delta[:, :, None])
        slope_tile = 1.0 - tanh_tile * tanh_tile
        gain_acc = gain_acc + jnp.sum(dlogit_tile * raw_tile * slope_tile, axis=(1, 2))
        dscore_tile = (dlogit_tile * local_col * slope_tile / score_scale).astype(jnp.bfloat16)
        query_acc = add_block(
            query_acc,
            jnp.einsum(
                "hij,jhd->ihd", dscore_tile, key_tile, preferred_element_type=jnp.float32
            ).reshape(BLK, width),
        )
        key_acc = add_block(
            key_acc,
            jnp.einsum(
                "hij,ihd->jhd", dscore_tile, query_tile, preferred_element_type=jnp.float32
            ).reshape(BLK, width),
        )
        value_acc = add_block(
            value_acc,
            jnp.einsum(
                "hij,ihd->jhd", weight_tile, grad_tile, preferred_element_type=jnp.float32
            ).reshape(BLK, width),
        )
        return (query_acc, key_acc, value_acc, gain_acc)

    grad_query32, grad_key32, grad_value32, local_gain_grad = lax.fori_loop(
        0, listed, add_grads, (grad_query32, zero_rows, zero_rows, zero_gain)
    )
    for back_keys, back_values in returned:
        grad_key32 = grad_key32 + back_keys.astype(jnp.float32)
        grad_value32 = grad_value32 + back_values.astype(jnp.float32)
    grad_query16 = grad_query32.astype(jnp.bfloat16)
    grad_key16 = grad_key32.astype(jnp.bfloat16)
    grad_value16 = grad_value32.astype(jnp.bfloat16)
    grad_wq = project_outer(hidden, grad_query16)
    grad_wk = project_outer(hidden, grad_key16)
    grad_wv = project_outer(hidden, grad_value16)
    grad_hidden = (
        project_back(grad_query16, w_query)
        + project_back(grad_key16, w_key)
        + project_back(grad_value16, w_value)
    )
    grad_gain1 = jnp.sum(grad_hidden * normed1, axis=0)
    grad_feats = (grad_mixed + norm_backward(grad_hidden, normed1, inverse1, norm1_gain)).astype(
        jnp.bfloat16
    )
    gain_row = jnp.concatenate([local_gain_grad, far_gain_grad])
    gain_row = jnp.pad(gain_row, (0, 128 - gain_row.shape[0]))
    small = jnp.concatenate(
        [
            grad_gain1.reshape(2, 128),
            grad_gain2.reshape(2, 128),
            gain_row[None],
            jnp.zeros((3, 128), jnp.float32),
        ]
    )
    grad_wq, grad_wk, grad_wv, grad_wout, grad_up, grad_down, small = sum_grads(
        (grad_wq, grad_wk, grad_wv, grad_wout, grad_up, grad_down), small
    )
    grad_gain1 = small[0:2].reshape(256)
    grad_gain2 = small[2:4].reshape(256)
    local_gain_grad = small[4, 0:heads]
    far_gain_grad = small[4, heads : 2 * heads]
    return (
        node_out[None],
        grad_feats[None],
        grad_gain1,
        grad_wq,
        grad_wk,
        grad_wv,
        grad_wout,
        grad_gain2,
        grad_up,
        grad_down,
        local_gain_grad,
        far_gain_grad,
    )


def solution(mesh):
    return jax.shard_map(
        local,
        mesh=mesh,
        in_specs=(
            P("rep", "dom", None),
            P("rep", "dom", None),
            P(),
            P(),
            P(),
            P(),
            P(),
            P(),
            P(),
            P(),
            P(),
            P(),
            P("rep", None, "dom", None),
            P("rep", "dom", None),
            P("rep", "dom"),
        ),
        out_specs=(
            P("rep", "dom", None),
            P("rep", "dom", None),
            P(),
            P(),
            P(),
            P(),
            P(),
            P(),
            P(),
            P(),
            P(),
            P(),
        ),
        check_vma=False,
    )
```

```python
import jax
import jax.numpy as jnp
from jax import lax
from jax.experimental import pallas as pl
from jax.experimental.pallas import tpu as pltpu
from jax.sharding import PartitionSpec as P

EPSILON = 1e-05
SCORE_CAP = 5.0
GELU_ROOT = 0.7978845608028654
GELU_CUBIC = 0.044715

ROWS = 128
WIDTH = 256
HEADS = 4
HEAD_DIM = 64
MATCH = 4
XY = 16
ZS = 16
EARLY = 10
LATE = 6
PIECE = EARLY + LATE
MESH = pl.DeviceIdType.MESH
F32 = jnp.float32
B16 = jnp.bfloat16

CORE_EARLY = 0
CORE_LATE = 1
PLANE_EARLY = 16
PLANE_LATE = 32
COLUMN_OUT = 48
COLUMN_BACK = 64
PLANE_BACK = 80
CORE_BACK = 96
FAR_OUT = 112
FAR_BACK = 116
SEMS = 120


def place():
    dom = lax.axis_index("dom")
    rep = lax.axis_index("rep")
    return dom // 8, (dom // 2) % 4, dom % 2, rep


def device(z, y, c, x):
    return {"dom": (z * 4 + y) * 2 + c, "rep": x}


def plane_peer(step):
    z, y, c, x = place()
    far_x = (x + step // 4) % 4
    far_y = (y + step % 4) % 4
    return far_x * 4 + far_y, device(z, far_y, c, far_x)


def column_peer(step):
    z, y, c, x = place()
    far_z = (z + step) % ZS
    return far_z, device(far_z, y, c, x)


def partner(matching):
    z, y, c, x = place()
    reach = 8 >> matching
    return device(z + reach - 2 * reach * ((z // reach) % 2), y, c, x)


def each(first, last, body):
    def step(index, carry):
        body(index)
        return carry

    lax.fori_loop(first, last, step, 0)


def enter():
    z, y, c, x = place()
    barrier = pltpu.get_barrier_semaphore()

    def greet(peer):
        pl.semaphore_signal(barrier, inc=1, device_id=peer, device_id_type=MESH)

    greet(device(z, y, 1 - c, x))
    each(1, ZS, lambda step: greet(column_peer(step)[1]))
    each(1, XY, lambda step: greet(plane_peer(step)[1]))
    pl.semaphore_wait(barrier, 1 + (XY - 1) + (ZS - 1))


def remote(src, dst, sems, at, peer):
    return pltpu.make_async_remote_copy(
        src_ref=src,
        dst_ref=dst,
        send_sem=sems.at[0, at],
        recv_sem=sems.at[1, at],
        device_id=peer,
        device_id_type=MESH,
    )


def spread_small(total):
    row = lax.broadcasted_iota(jnp.int32, (8, 128), 0)
    high = total.astype(B16).astype(F32)
    low = pltpu.roll(total - high, 1, 0)
    return jnp.where(row == 5, low, total).astype(B16)


def join_small(parts):
    row = lax.broadcasted_iota(jnp.int32, (8, 128), 0)
    low = pltpu.roll(parts, 7, 0)
    return jnp.where(row == 4, parts + low, parts)


def dot(left, right):
    return jnp.dot(left, right, preferred_element_type=F32)


def dot_back(left, right):
    return lax.dot_general(left, right, (((1,), (1,)), ((), ())), preferred_element_type=F32)


def dot_outer(left, right):
    return lax.dot_general(left, right, (((0,), (0,)), ((), ())), preferred_element_type=F32)


def gelu_parts(preact):
    square = preact * preact
    tangent = jnp.tanh(GELU_ROOT * (preact + GELU_CUBIC * square * preact))
    half = 0.5 * (1.0 + tangent)
    result = preact * half
    derivative = half + 0.5 * preact * (1.0 - tangent * tangent) * (
        GELU_ROOT + 3.0 * GELU_ROOT * GELU_CUBIC * square
    )
    return (result, derivative)


def norm_forward(matrix):
    center = jnp.mean(matrix, axis=-1, keepdims=True)
    shifted = matrix - center
    inverse = lax.rsqrt(jnp.mean(shifted * shifted, axis=-1, keepdims=True) + EPSILON)
    return (shifted * inverse, inverse)


def norm_backward(upstream, normed, inverse, gain):
    scaled_up = upstream * gain
    return inverse * (
        scaled_up
        - jnp.mean(scaled_up, axis=-1, keepdims=True)
        - normed * jnp.mean(scaled_up * normed, axis=-1, keepdims=True)
    )


def head_of_lane(shape, axis):
    return lax.broadcasted_iota(jnp.int32, shape, axis) >> 6


def head_sum(products, block_ones):
    high = products.astype(B16)
    low = (products - high.astype(F32)).astype(B16)
    return dot(high, block_ones) + dot(low, block_ones)


def put_units(stage, half, at, matrix):
    units = matrix.shape[0] // 8
    stage[half, at : at + units] = matrix.reshape(units, 8, 128).astype(B16)


def layer_kernel(
    feats_ref,
    up_ref,
    gain1_ref,
    wq_ref,
    wk_ref,
    wv_ref,
    wo_ref,
    gain2_ref,
    wup_ref,
    wdn_ref,
    local_ref,
    far_ref,
    perm_ref,
    node_out_ref,
    grad_feats_ref,
    full,
    small_ref,
    far_in,
    back_out,
    back_in,
    early_stage,
    early_in,
    early_mid,
    early_plane,
    late_stage,
    late_in,
    late_mid,
    late_plane,
    column_out,
    column_in,
    last,
    sems,
):
    z, y, c, x = place()
    sibling = device(z, y, 1 - c, x)
    mine = x * 4 + y
    enter()

    def far_out(matching):
        return remote(
            feats_ref, far_in.at[matching], sems, FAR_OUT + matching, partner(matching)
        )

    def far_back(matching):
        return remote(
            back_out.at[matching],
            back_in.at[matching],
            sems,
            FAR_BACK + matching,
            partner(matching),
        )

    for matching in range(MATCH):
        far_out(matching).start()

    lane_head = head_of_lane((1, WIDTH), 1)
    masks = [jnp.where(lane_head == head, 1.0, 0.0) for head in range(HEADS)]
    masks16 = [mask.astype(B16) for mask in masks]
    ones_rows = head_of_lane((WIDTH, WIDTH), 0)
    ones_lanes = head_of_lane((WIDTH, WIDTH), 1)
    block_ones = jnp.where(ones_rows == ones_lanes, 1.0, 0.0).astype(B16)
    far_gain = sum(masks[head] * far_ref[head] for head in range(HEADS))

    def stacked(matrix):
        return jnp.concatenate([matrix * mask for mask in masks16], axis=0)

    gain1 = gain1_ref[...]
    gain2 = gain2_ref[...]
    wk = wk_ref[...]
    wv = wv_ref[...]
    features = feats_ref[...].astype(F32)
    normed1, inverse1 = norm_forward(features)
    hidden = (normed1 * gain1).astype(B16)
    query = dot(hidden, wq_ref[...]).astype(B16)
    key = dot(hidden, wk).astype(B16)
    value = dot(hidden, wv).astype(B16)
    query32 = query.astype(F32)
    query_stack = stacked(query)
    raw_all = dot_back(query_stack, key) * (1.0 / 8.0)
    raws, tangents, exps = [], [], []
    denominator = jnp.zeros((ROWS, WIDTH), F32)
    for head in range(HEADS):
        raw = raw_all[head * ROWS : (head + 1) * ROWS]
        tangent = jnp.tanh(raw * (local_ref[head] / SCORE_CAP))
        exped = jnp.exp(SCORE_CAP * tangent)
        denominator = denominator + masks[head] * jnp.sum(exped, axis=1, keepdims=True)
        raws.append(raw)
        tangents.append(tangent)
        exps.append(exped)
    upstream = up_ref[...]
    grad_act = dot_back(upstream, wdn_ref[...])

    one_hots, far_norms, far_hiddens, far_keys, far_values = {}, {}, {}, {}, {}
    far_raws, far_tangents, far_exps = {}, {}, {}
    rows = lax.broadcasted_iota(jnp.int32, (ROWS, ROWS), 0)
    for matching in reversed(range(MATCH)):
        one_hot = jnp.where(rows == perm_ref[matching : matching + 1, :], 1.0, 0.0)
        one_hots[matching] = one_hot.astype(B16)
        far_out(matching).wait_recv()
        picked = dot_outer(one_hots[matching], far_in[matching])
        normed, _ = norm_forward(picked)
        far_norms[matching] = normed
        far_hiddens[matching] = (normed * gain1).astype(B16)
        far_keys[matching] = dot(far_hiddens[matching], wk).astype(B16)
        far_values[matching] = dot(far_hiddens[matching], wv).astype(B16)
        raw = head_sum(query32 * far_keys[matching].astype(F32), block_ones) * (1.0 / 8.0)
        tangent = jnp.tanh(raw * (far_gain * (1.0 / SCORE_CAP)))
        exped = jnp.exp(SCORE_CAP * tangent)
        denominator = denominator + exped
        far_raws[matching] = raw
        far_tangents[matching] = tangent
        far_exps[matching] = exped

    inverse_den = 1.0 / denominator
    weights = [
        (exps[head] * inverse_den[:, head * HEAD_DIM : head * HEAD_DIM + 1]).astype(B16)
        for head in range(HEADS)
    ]
    weight_lanes = jnp.concatenate(weights, axis=1)
    attended32 = dot(weight_lanes, stacked(value))
    far_weights = {}
    for matching in range(MATCH):
        weight = (far_exps[matching] * inverse_den).astype(B16).astype(F32)
        far_weights[matching] = weight
        attended32 = attended32 + weight * far_values[matching].astype(F32)
    attended = attended32.astype(B16)

    mixed = (features + dot(attended, wo_ref[...])).astype(B16).astype(F32)
    normed2, inverse2 = norm_forward(mixed)
    hidden2 = (normed2 * gain2).astype(B16)
    activ, derivative = gelu_parts(dot(hidden2, wup_ref[...]))
    activ = activ.astype(B16)
    grad_pre = (grad_act * derivative).astype(B16)
    grad_hidden2 = dot_back(grad_pre, wup_ref[...])
    grad_mixed = upstream.astype(F32) + norm_backward(grad_hidden2, normed2, inverse2, gain2)
    grad_mixed16 = grad_mixed.astype(B16)
    grad_att = dot_back(grad_mixed16, wo_ref[...]).astype(B16)
    node_out_ref[...] = (mixed + dot(activ, wdn_ref[...])).astype(B16)
    grad_gain2 = jnp.sum(grad_hidden2 * normed2, axis=0, keepdims=True)

    grad_down = dot_outer(activ, upstream)
    grad_up = dot_outer(hidden2, grad_pre)
    grad_wout = dot_outer(attended, grad_mixed16)
    for part in range(2):
        put_units(early_stage, 0, part * 64, grad_down[:, part * 128 : part * 128 + 128])
        put_units(early_stage, part, 128, grad_wout[:, part * 128 : part * 128 + 128])
    for part in range(4):
        put_units(early_stage, 1, part * 32, grad_up[:, part * 128 : part * 128 + 128])
    core_early = remote(early_stage.at[1 - c], early_in, sems, CORE_EARLY, sibling)
    core_early.start()

    grad_att32 = grad_att.astype(F32)
    grad_stack = stacked(grad_att)
    delta = head_sum(grad_att32 * attended32, block_ones)
    far_gain_row = jnp.zeros((1, WIDTH), F32)
    grad_query32 = jnp.zeros((ROWS, WIDTH), F32)
    grad_gain1 = jnp.zeros((1, WIDTH), F32)
    key_terms, value_terms = {}, {}
    for matching in range(MATCH):
        weight = far_weights[matching]
        dots = head_sum(grad_att32 * far_values[matching].astype(F32), block_ones)
        dlogit = weight * (dots - delta)
        sloped = dlogit * (1.0 - far_tangents[matching] * far_tangents[matching])
        far_gain_row = far_gain_row + jnp.sum(
            sloped * far_raws[matching], axis=0, keepdims=True
        )
        dscore = (sloped * (far_gain * (1.0 / 8.0))).astype(B16).astype(F32)
        grad_query32 = grad_query32 + dscore * far_keys[matching].astype(F32)
        key_terms[matching] = (dscore * query32).astype(B16)
        value_terms[matching] = (weight * grad_att32).astype(B16)
        returned = dot_back(key_terms[matching], wk) + dot_back(value_terms[matching], wv)
        grad_gain1 = grad_gain1 + jnp.sum(
            returned * far_norms[matching], axis=0, keepdims=True
        )
        back_out[matching] = dot(one_hots[matching], returned.astype(B16)).astype(B16)
        far_back(matching).start()

    def plane_early(step):
        peer, where = plane_peer(step)
        return remote(early_mid.at[peer], early_plane.at[step], sems, PLANE_EARLY + step, where)

    def plane_late(step):
        peer, where = plane_peer(step)
        return remote(late_mid.at[peer], late_plane.at[step], sems, PLANE_LATE + step, where)

    core_early.wait()

    def add_early(piece):
        units = pl.ds(piece * EARLY, EARLY)
        early_mid[piece] = (
            early_stage[c, units].astype(F32) + early_in[units].astype(F32)
        ).astype(B16)

    each(0, XY, add_early)
    each(1, XY, lambda step: plane_early(step).start())

    dots_all = dot_back(grad_stack, value)
    lane = lax.broadcasted_iota(jnp.int32, (1, 128), 1)
    gain_row = jnp.zeros((1, 128), F32)
    dscores = []
    for head in range(HEADS):
        dots = dots_all[head * ROWS : (head + 1) * ROWS]
        delta_column = delta[:, head * HEAD_DIM : head * HEAD_DIM + 1]
        dlogit = weights[head].astype(F32) * (dots - delta_column)
        sloped = dlogit * (1.0 - tangents[head] * tangents[head])
        local_sum = jnp.sum(
            jnp.sum(sloped * raws[head], axis=0, keepdims=True), axis=1, keepdims=True
        )
        far_sum = far_gain_row[:, head * HEAD_DIM : head * HEAD_DIM + 1]
        gain_row = jnp.where(lane == head, local_sum, gain_row)
        gain_row = jnp.where(lane == HEADS + head, far_sum, gain_row)
        dscores.append((sloped * (local_ref[head] / 8.0)).astype(B16))
    grad_query = (
        grad_query32 + dot(jnp.concatenate(dscores, axis=1), stacked(key))
    ).astype(B16)
    grad_key = dot_outer(jnp.concatenate(dscores, axis=0), query_stack).astype(B16)
    grad_value = dot_outer(jnp.concatenate(weights, axis=0), grad_stack).astype(B16)
    order = list(range(MATCH))
    all_hidden = jnp.concatenate([hidden] + [far_hiddens[m] for m in order], axis=0)
    grad_wq = dot_outer(hidden, grad_query)
    grad_wk = dot_outer(
        all_hidden, jnp.concatenate([grad_key] + [key_terms[m] for m in order], axis=0)
    )
    grad_wv = dot_outer(
        all_hidden, jnp.concatenate([grad_value] + [value_terms[m] for m in order], axis=0)
    )
    grad_hidden = (
        dot_back(grad_query, wq_ref[...]) + dot_back(grad_key, wk) + dot_back(grad_value, wv)
    )
    grad_gain1 = grad_gain1 + jnp.sum(grad_hidden * normed1, axis=0, keepdims=True)
    for number, grad in enumerate((grad_wq, grad_wk, grad_wv)):
        for part in range(2):
            put_units(late_stage, part, number * 32, grad[:, part * 128 : part * 128 + 128])
    small = jnp.concatenate(
        [
            grad_gain1[:, 0:128],
            grad_gain1[:, 128:256],
            grad_gain2[:, 0:128],
            grad_gain2[:, 128:256],
            gain_row,
            jnp.zeros((3, 128), F32),
        ],
        axis=0,
    )
    small16 = spread_small(small)
    late_stage[0, XY * LATE] = small16
    late_stage[1, XY * LATE] = small16
    core_late = remote(late_stage.at[1 - c], late_in, sems, CORE_LATE, sibling)
    core_late.start()
    core_late.wait()
    small = late_stage[0, XY * LATE].astype(F32) + late_in[XY * LATE].astype(F32)
    small16 = spread_small(join_small(small))

    def add_late(piece):
        units = pl.ds(piece * LATE, LATE)
        late_mid[piece, 0:LATE] = (
            late_stage[c, units].astype(F32) + late_in[units].astype(F32)
        ).astype(B16)
        late_mid[piece, LATE] = small16

    each(0, XY, add_late)
    each(1, XY, lambda step: plane_late(step).start())

    each(1, XY, lambda step: plane_early(step).wait_recv())
    total = early_mid[mine].astype(F32)
    for step in range(1, XY):
        total = total + early_plane[step].astype(F32)
    column_out[0:EARLY, 0] = total.astype(B16)
    each(1, XY, lambda step: plane_late(step).wait_recv())
    total = late_mid[mine].astype(F32)
    for step in range(1, XY):
        total = total + late_plane[step].astype(F32)
    small16 = spread_small(join_small(total[LATE]))
    column_out[EARLY:PIECE, 0] = total[0:LATE].astype(B16)
    for unit in range(ZS):
        column_out[unit, 1] = small16

    def column_copy(step):
        peer, where = column_peer(step)
        return remote(column_out.at[peer], column_in.at[step], sems, COLUMN_OUT + step, where)

    each(1, ZS, lambda step: column_copy(step).start())

    for matching in reversed(range(MATCH)):
        far_back(matching).wait_recv()
        grad_hidden = grad_hidden + back_in[matching].astype(F32)
    grad_feats_ref[...] = (
        grad_mixed + norm_backward(grad_hidden, normed1, inverse1, gain1)
    ).astype(B16)

    each(1, ZS, lambda step: column_copy(step).wait_recv())
    total = column_out[z].astype(F32)
    for step in range(1, ZS):
        total = total + column_in[step].astype(F32)
    small_ref[...] = join_small(total[1])
    last[z] = total[0].astype(B16)

    def column_back(step):
        return remote(last.at[z], last.at[z], sems, COLUMN_BACK + step, column_peer(step)[1])

    each(1, ZS, lambda step: column_back(step).start())
    each(1, ZS, lambda step: column_back(step).wait_recv())
    full[c, mine] = last[...]

    def plane_back(step):
        return remote(
            full.at[c, mine], full.at[c, mine], sems, PLANE_BACK + step, plane_peer(step)[1]
        )

    def core_back(step):
        origin = ((x + 4 - step // 4) % 4) * 4 + (y + 4 - step % 4) % 4
        return remote(full.at[c, origin], full.at[c, origin], sems, CORE_BACK + step, sibling)

    each(1, XY, lambda step: plane_back(step).start())
    core_back(0).start()

    def pass_on(step):
        plane_back(step).wait_recv()
        core_back(step).start()

    each(1, XY, pass_on)
    each(0, XY, lambda step: core_back(step).wait())
    each(1, XY, lambda step: plane_early(step).wait_send())
    each(1, XY, lambda step: plane_late(step).wait_send())
    each(1, ZS, lambda step: column_copy(step).wait_send())
    each(1, ZS, lambda step: column_back(step).wait_send())
    each(1, XY, lambda step: plane_back(step).wait_send())
    for matching in range(MATCH):
        far_out(matching).wait_send()
        far_back(matching).wait_send()


def layer(*args):
    vmem = pl.BlockSpec(memory_space=pltpu.VMEM)
    smem = pl.BlockSpec(memory_space=pltpu.SMEM)
    return pl.pallas_call(
        layer_kernel,
        out_shape=[
            jax.ShapeDtypeStruct((ROWS, WIDTH), B16),
            jax.ShapeDtypeStruct((ROWS, WIDTH), B16),
            jax.ShapeDtypeStruct((2, XY, PIECE, 8, 128), B16),
            jax.ShapeDtypeStruct((8, 128), F32),
        ],
        in_specs=[vmem] * 10 + [smem] * 2 + [vmem],
        out_specs=[vmem] * 4,
        scratch_shapes=[
            pltpu.VMEM((MATCH, ROWS, WIDTH), B16),
            pltpu.VMEM((MATCH, ROWS, WIDTH), B16),
            pltpu.VMEM((MATCH, ROWS, WIDTH), B16),
            pltpu.VMEM((2, XY * EARLY, 8, 128), B16),
            pltpu.VMEM((XY * EARLY, 8, 128), B16),
            pltpu.VMEM((XY, EARLY, 8, 128), B16),
            pltpu.VMEM((XY, EARLY, 8, 128), B16),
            pltpu.VMEM((2, XY * LATE + 1, 8, 128), B16),
            pltpu.VMEM((XY * LATE + 1, 8, 128), B16),
            pltpu.VMEM((XY, LATE + 1, 8, 128), B16),
            pltpu.VMEM((XY, LATE + 1, 8, 128), B16),
            pltpu.VMEM((ZS, 2, 8, 128), B16),
            pltpu.VMEM((ZS, 2, 8, 128), B16),
            pltpu.VMEM((ZS, 8, 128), B16),
            pltpu.SemaphoreType.DMA((2, SEMS)),
        ],
        compiler_params=pltpu.CompilerParams(
            collective_id=0, has_side_effects=True, vmem_limit_bytes=48 * 1024 * 1024
        ),
    )(*args)


def write_kernel(node_ref, feats_ref, full, small, node_out, feats_out, *outs):
    node_out[...] = node_ref[...]
    feats_out[...] = feats_ref[...]
    gain1, wq, wk, wv, wout, gain2, up, down, gains = outs
    for half in range(2):
        early = full[half, :, 0:EARLY].reshape(XY * EARLY, 8, 128)
        late = full[half, :, EARLY:PIECE].reshape(XY * LATE, 8, 128)

        def take(units, at, count):
            return units[at : at + count].astype(F32).reshape(count * 8, 128)

        lanes = slice(half * 128, half * 128 + 128)
        for number, ref in enumerate((wq, wk, wv)):
            ref[:, lanes] = take(late, number * 32, 32)
        wout[:, lanes] = take(early, 128, 32)
        if half == 0:
            for part in range(2):
                down[:, part * 128 : part * 128 + 128] = take(early, part * 64, 64)
        else:
            for part in range(4):
                up[:, part * 128 : part * 128 + 128] = take(early, part * 32, 32)
    gain1[:, 0:128] = small[0:1, :]
    gain1[:, 128:256] = small[1:2, :]
    gain2[:, 0:128] = small[2:3, :]
    gain2[:, 128:256] = small[3:4, :]
    gains[...] = small[4:5, :]


def write_out(*args):
    vmem = pl.BlockSpec(memory_space=pltpu.VMEM)
    shapes = [
        ((ROWS, WIDTH), B16),
        ((ROWS, WIDTH), B16),
        ((1, WIDTH), F32),
        ((WIDTH, WIDTH), F32),
        ((WIDTH, WIDTH), F32),
        ((WIDTH, WIDTH), F32),
        ((WIDTH, WIDTH), F32),
        ((1, WIDTH), F32),
        ((WIDTH, 2 * WIDTH), F32),
        ((2 * WIDTH, WIDTH), F32),
        ((1, 128), F32),
    ]
    return pl.pallas_call(
        write_kernel,
        out_shape=[jax.ShapeDtypeStruct(*shape) for shape in shapes],
        in_specs=[vmem] * 4,
        out_specs=[vmem] * len(shapes),
        compiler_params=pltpu.CompilerParams(vmem_limit_bytes=48 * 1024 * 1024),
    )(*args)


def local(
    node_feats,
    out_grad,
    norm1_gain,
    w_query,
    w_key,
    w_value,
    w_out,
    norm2_gain,
    w_up,
    w_down,
    local_gain,
    expander_gain,
    partner_perm,
    block_pairs,
    pair_count,
):
    summed = layer(
        node_feats[0],
        out_grad[0],
        norm1_gain[None],
        w_query,
        w_key,
        w_value,
        w_out,
        norm2_gain[None],
        w_up,
        w_down,
        local_gain,
        expander_gain,
        partner_perm[0, :, 0, :],
    )
    node_out, grad_feats, gain1, wq, wk, wv, wout, gain2, up, down, gains = write_out(*summed)
    return (
        node_out[None],
        grad_feats[None],
        gain1[0],
        wq,
        wk,
        wv,
        wout,
        gain2[0],
        up,
        down,
        gains[0, 0:HEADS],
        gains[0, HEADS : 2 * HEADS],
    )


def solution(mesh):
    return jax.shard_map(
        local,
        mesh=mesh,
        in_specs=(
            P("rep", "dom", None),
            P("rep", "dom", None),
            P(),
            P(),
            P(),
            P(),
            P(),
            P(),
            P(),
            P(),
            P(),
            P(),
            P("rep", None, "dom", None),
            P("rep", "dom", None),
            P("rep", "dom"),
        ),
        out_specs=(
            P("rep", "dom", None),
            P("rep", "dom", None),
            P(),
            P(),
            P(),
            P(),
            P(),
            P(),
            P(),
            P(),
            P(),
            P(),
        ),
        check_vma=False,
    )
```

```python
import jax
import jax.numpy as jnp
from jax import lax
from jax.experimental import pallas as pl
from jax.experimental.pallas import tpu as pltpu
from jax.sharding import PartitionSpec as P

EPSILON = 1e-05
SCORE_CAP = 5.0
GELU_ROOT = 0.7978845608028654
GELU_CUBIC = 0.044715

ROWS = 128
WIDTH = 256
HEADS = 4
HEAD_DIM = 64
MATCH = 4
XY = 16
NEAR = 4
PIECE = 8
SHARE = PIECE // NEAR
MESH = pl.DeviceIdType.MESH
F32 = jnp.float32
B16 = jnp.bfloat16

CORE = 0
PLANE = 0
NEAR_OUT = 16
FAR_SUM = 20
NEAR_BACK = 24
PLANE_BACK = 32
CORE_BACK = 48
BLOCK = 64
SEND = 2 * BLOCK
RELAY = SEND + 5
RETURN = RELAY + 2
SEMS = RETURN + 4


def place():
    dom = lax.axis_index("dom")
    rep = lax.axis_index("rep")
    return dom // 8, (dom // 2) % 4, dom % 2, rep


def device(z, y, c, x):
    return {"dom": (z * 4 + y) * 2 + c, "rep": x}


def plane_peer(step):
    z, y, c, x = place()
    far_x = (x + step // 4) % 4
    far_y = (y + step % 4) % 4
    return far_x * 4 + far_y, device(z, far_y, c, far_x)


def near_peer(step):
    z, y, c, x = place()
    group = (z // NEAR) * NEAR
    other = (z % NEAR + step) % NEAR
    return other, device(group + other, y, c, x)


def far_peer(step):
    z, y, c, x = place()
    return device((z + NEAR * step) % 16, y, c, x)


def partner(matching):
    z, y, c, x = place()
    reach = 8 >> matching
    return device(z + reach - 2 * reach * ((z // reach) % 2), y, c, x)


def relay_target():
    z, y, c, x = place()
    high = z + 8 - 16 * ((z // 8) % 2)
    return device(high + 4 - 8 * ((z // 4) % 2), y, c, x)


def each(first, last, body):
    def step(index, carry):
        body(index)
        return carry

    lax.fori_loop(first, last, step, 0)


def enter():
    z, y, c, x = place()
    barrier = pltpu.get_barrier_semaphore()

    def greet(peer):
        pl.semaphore_signal(barrier, inc=1, device_id=peer, device_id_type=MESH)

    for step in range(1, 4):
        greet(far_peer(step))
        greet(near_peer(step)[1])
    greet(device(z, y, 1 - c, x))
    each(1, XY, lambda step: greet(plane_peer(step)[1]))
    pl.semaphore_wait(barrier, 3 + 3 + 1 + (XY - 1))


def remote(src, dst, sems, at, peer):
    return pltpu.make_async_remote_copy(
        src_ref=src,
        dst_ref=dst,
        send_sem=sems.at[0, at],
        recv_sem=sems.at[1, at],
        device_id=peer,
        device_id_type=MESH,
    )


def spread_small(total):
    row = lax.broadcasted_iota(jnp.int32, (8, 128), 0)
    high = total.astype(B16).astype(F32)
    low = pltpu.roll(total - high, 1, 0)
    return jnp.where(row == 5, low, total).astype(B16)


def join_small(parts):
    row = lax.broadcasted_iota(jnp.int32, (8, 128), 0)
    low = pltpu.roll(parts, 7, 0)
    return jnp.where(row == 4, parts + low, parts)


def resum(parts):
    return spread_small(join_small(parts))


def dot(left, right):
    return jnp.dot(left, right, preferred_element_type=F32)


def dot_back(left, right):
    return lax.dot_general(left, right, (((1,), (1,)), ((), ())), preferred_element_type=F32)


def dot_outer(left, right):
    return lax.dot_general(left, right, (((0,), (0,)), ((), ())), preferred_element_type=F32)


def gelu_parts(preact):
    square = preact * preact
    tangent = jnp.tanh(GELU_ROOT * (preact + GELU_CUBIC * square * preact))
    half = 0.5 * (1.0 + tangent)
    result = preact * half
    derivative = half + 0.5 * preact * (1.0 - tangent * tangent) * (
        GELU_ROOT + 3.0 * GELU_ROOT * GELU_CUBIC * square
    )
    return (result, derivative)


def norm_forward(matrix):
    center = jnp.mean(matrix, axis=-1, keepdims=True)
    shifted = matrix - center
    inverse = lax.rsqrt(jnp.mean(shifted * shifted, axis=-1, keepdims=True) + EPSILON)
    return (shifted * inverse, inverse)


def norm_backward(upstream, normed, inverse, gain):
    scaled_up = upstream * gain
    return inverse * (
        scaled_up
        - jnp.mean(scaled_up, axis=-1, keepdims=True)
        - normed * jnp.mean(scaled_up * normed, axis=-1, keepdims=True)
    )


def head_of_lane(shape, axis):
    return lax.broadcasted_iota(jnp.int32, shape, axis) >> 6


def head_sum(products, block_ones):
    high = products.astype(B16)
    low = (products - high.astype(F32)).astype(B16)
    return dot(high, block_ones) + dot(low, block_ones)


def put_units(stage, half, at, matrix):
    units = matrix.shape[0] // 8
    stage[half, at : at + units] = matrix.reshape(units, 8, 128).astype(B16)


def layer_kernel(*refs):
    sources, refs = refs[0:13], refs[13:]
    node_out_ref, grad_feats_ref, early_full, late_full, small_ref = refs[0:5]
    held, refs = refs[5:18], refs[18:]
    (
        feats_ref,
        up_ref,
        gain1_ref,
        wq_ref,
        wk_ref,
        wv_ref,
        wo_ref,
        gain2_ref,
        wup_ref,
        wdn_ref,
        local_ref,
        far_ref,
        perm_ref,
    ) = held
    far_in, back_out, back_in = refs[0:3]
    halves = (refs[3:11], refs[11:19])
    sems, load_sems = refs[19:21]
    early_stage, late_stage = halves[0][0], halves[1][0]

    def load(number):
        return pltpu.make_async_copy(sources[number], held[number], load_sems.at[number])

    for number in (0, 2, 3, 4, 5, 10, 11, 12, 1, 9, 6, 7, 8):
        load(number).start()
    z, y, c, x = place()
    sibling = device(z, y, 1 - c, x)
    mine = x * 4 + y
    enter()

    pieces = (pl.ds(0, ROWS // 2), pl.ds(ROWS // 2, ROWS // 2))

    def far_out(matching):
        return remote(
            sources[0], far_in.at[matching], sems, SEND + matching, partner(matching)
        )

    def far_piece(part):
        rows = pieces[part]
        return remote(
            sources[0].at[rows], far_in.at[1, rows], sems, SEND + part, partner(1)
        )

    def far_relay(part):
        rows = pieces[part]
        return remote(
            far_in.at[1, rows], far_in.at[0, rows], sems, RELAY + part, relay_target()
        )

    def far_back(matching):
        return remote(
            back_out.at[matching],
            back_in.at[matching],
            sems,
            RETURN + matching,
            partner(matching),
        )

    far_piece(0).start()
    far_piece(1).start()
    far_out(2).start()
    far_out(3).start()

    for number in (0, 2, 3, 4, 5, 10, 11, 12):
        load(number).wait()
    lane_head = head_of_lane((1, WIDTH), 1)
    masks = [jnp.where(lane_head == head, 1.0, 0.0) for head in range(HEADS)]
    masks16 = [mask.astype(B16) for mask in masks]
    ones_rows = head_of_lane((WIDTH, WIDTH), 0)
    ones_lanes = head_of_lane((WIDTH, WIDTH), 1)
    block_ones = jnp.where(ones_rows == ones_lanes, 1.0, 0.0).astype(B16)
    far_gain = sum(masks[head] * far_ref[head] for head in range(HEADS))

    def stacked(matrix):
        return jnp.concatenate([matrix * mask for mask in masks16], axis=0)

    gain1 = gain1_ref[...]
    wk = wk_ref[...]
    wv = wv_ref[...]
    features = feats_ref[...].astype(F32)
    normed1, inverse1 = norm_forward(features)
    hidden = (normed1 * gain1).astype(B16)
    query = dot(hidden, wq_ref[...]).astype(B16)
    key = dot(hidden, wk).astype(B16)
    value = dot(hidden, wv).astype(B16)
    query32 = query.astype(F32)
    query_stack = stacked(query)
    raw_all = dot_back(query_stack, key) * (1.0 / 8.0)
    raws, tangents, exps = [], [], []
    denominator = jnp.zeros((ROWS, WIDTH), F32)
    for head in range(HEADS):
        raw = raw_all[head * ROWS : (head + 1) * ROWS]
        tangent = jnp.tanh(raw * (local_ref[head] / SCORE_CAP))
        exped = jnp.exp(SCORE_CAP * tangent)
        denominator = denominator + masks[head] * jnp.sum(exped, axis=1, keepdims=True)
        raws.append(raw)
        tangents.append(tangent)
        exps.append(exped)
    for number in (1, 9, 6, 7, 8):
        load(number).wait()
    gain2 = gain2_ref[...]
    upstream = up_ref[...]
    grad_act = dot_back(upstream, wdn_ref[...])

    for part in range(2):
        far_piece(part).wait_recv()
        far_relay(part).start()
    one_hots, far_norms, far_hiddens, far_keys, far_values = {}, {}, {}, {}, {}
    far_raws, far_tangents, far_exps = {}, {}, {}
    rows = lax.broadcasted_iota(jnp.int32, (ROWS, ROWS), 0)
    for matching in reversed(range(MATCH)):
        one_hot = jnp.where(rows == perm_ref[matching : matching + 1, :], 1.0, 0.0)
        one_hots[matching] = one_hot.astype(B16)
        if matching >= 2:
            far_out(matching).wait_recv()
        elif matching == 0:
            far_relay(0).wait_recv()
            far_relay(1).wait_recv()
        picked = dot_outer(one_hots[matching], far_in[matching])
        normed, _ = norm_forward(picked)
        far_norms[matching] = normed
        far_hiddens[matching] = (normed * gain1).astype(B16)
        far_keys[matching] = dot(far_hiddens[matching], wk).astype(B16)
        far_values[matching] = dot(far_hiddens[matching], wv).astype(B16)
        raw = head_sum(query32 * far_keys[matching].astype(F32), block_ones) * (1.0 / 8.0)
        tangent = jnp.tanh(raw * (far_gain * (1.0 / SCORE_CAP)))
        exped = jnp.exp(SCORE_CAP * tangent)
        denominator = denominator + exped
        far_raws[matching] = raw
        far_tangents[matching] = tangent
        far_exps[matching] = exped

    inverse_den = 1.0 / denominator
    weights = [
        (exps[head] * inverse_den[:, head * HEAD_DIM : head * HEAD_DIM + 1]).astype(B16)
        for head in range(HEADS)
    ]
    weight_lanes = jnp.concatenate(weights, axis=1)
    attended32 = dot(weight_lanes, stacked(value))
    far_weights = {}
    for matching in range(MATCH):
        weight = (far_exps[matching] * inverse_den).astype(B16).astype(F32)
        far_weights[matching] = weight
        attended32 = attended32 + weight * far_values[matching].astype(F32)
    attended = attended32.astype(B16)

    mixed = (features + dot(attended, wo_ref[...])).astype(B16).astype(F32)
    normed2, inverse2 = norm_forward(mixed)
    hidden2 = (normed2 * gain2).astype(B16)
    activ, derivative = gelu_parts(dot(hidden2, wup_ref[...]))
    activ = activ.astype(B16)
    grad_pre = (grad_act * derivative).astype(B16)
    grad_hidden2 = dot_back(grad_pre, wup_ref[...])
    grad_mixed = upstream.astype(F32) + norm_backward(grad_hidden2, normed2, inverse2, gain2)
    grad_mixed16 = grad_mixed.astype(B16)
    grad_att = dot_back(grad_mixed16, wo_ref[...]).astype(B16)
    node_out_ref[...] = (mixed + dot(activ, wdn_ref[...])).astype(B16)
    grad_gain2 = jnp.sum(grad_hidden2 * normed2, axis=0, keepdims=True)

    def core_copy(half):
        stage, core_in = halves[half][0:2]
        return remote(stage.at[1 - c], core_in, sems, half * BLOCK + CORE, sibling)

    grad_down = dot_outer(activ, upstream)
    grad_up = dot_outer(hidden2, grad_pre)
    for part in range(2):
        put_units(early_stage, 0, part * 64, grad_down[:, part * 128 : part * 128 + 128])
    for part in range(4):
        put_units(early_stage, 1, part * 32, grad_up[:, part * 128 : part * 128 + 128])
    core_copy(0).start()
    grad_wout = dot_outer(attended, grad_mixed16)

    grad_att32 = grad_att.astype(F32)
    grad_stack = stacked(grad_att)
    delta = head_sum(grad_att32 * attended32, block_ones)
    far_gain_row = jnp.zeros((1, WIDTH), F32)
    grad_query32 = jnp.zeros((ROWS, WIDTH), F32)
    grad_gain1 = jnp.zeros((1, WIDTH), F32)
    key_terms, value_terms = {}, {}
    for matching in range(MATCH):
        weight = far_weights[matching]
        dots = head_sum(grad_att32 * far_values[matching].astype(F32), block_ones)
        dlogit = weight * (dots - delta)
        sloped = dlogit * (1.0 - far_tangents[matching] * far_tangents[matching])
        far_gain_row = far_gain_row + jnp.sum(
            sloped * far_raws[matching], axis=0, keepdims=True
        )
        dscore = (sloped * (far_gain * (1.0 / 8.0))).astype(B16).astype(F32)
        grad_query32 = grad_query32 + dscore * far_keys[matching].astype(F32)
        key_terms[matching] = (dscore * query32).astype(B16)
        value_terms[matching] = (weight * grad_att32).astype(B16)
        returned = dot_back(key_terms[matching], wk) + dot_back(value_terms[matching], wv)
        grad_gain1 = grad_gain1 + jnp.sum(
            returned * far_norms[matching], axis=0, keepdims=True
        )
        back_out[matching] = dot(one_hots[matching], returned.astype(B16)).astype(B16)
        far_back(matching).start()

    def plane_copy(half, step):
        mid, plane_in = halves[half][2:4]
        peer, where = plane_peer(step)
        return remote(
            mid.at[peer], plane_in.at[step], sems, half * BLOCK + PLANE + step, where
        )

    def near_copy(half, step):
        near_out, near_in = halves[half][4:6]
        peer, where = near_peer(step)
        return remote(
            near_out.at[peer], near_in.at[step], sems, half * BLOCK + NEAR_OUT + step, where
        )

    def far_copy(half, step):
        far_sum = halves[half][6]
        return remote(
            far_sum.at[0], far_sum.at[step], sems, half * BLOCK + FAR_SUM + step, far_peer(step)
        )

    def near_back(half, step):
        last = halves[half][7]
        return remote(
            last.at[z % NEAR],
            last.at[z % NEAR],
            sems,
            half * BLOCK + NEAR_BACK + step,
            near_peer(step)[1],
        )

    def plane_back(half, step):
        full = (early_full, late_full)[half]
        return remote(
            full.at[c, mine],
            full.at[c, mine],
            sems,
            half * BLOCK + PLANE_BACK + step,
            plane_peer(step)[1],
        )

    def core_back(half, step):
        full = (early_full, late_full)[half]
        origin = ((x + 4 - step // 4) % 4) * 4 + (y + 4 - step % 4) % 4
        return remote(
            full.at[c, origin],
            full.at[c, origin],
            sems,
            half * BLOCK + CORE_BACK + step,
            sibling,
        )

    def sum_core(half):
        stage, core_in, mid = halves[half][0:3]
        core_copy(half).wait_recv()
        if half == 1:
            small16 = resum(stage[0, XY * PIECE].astype(F32) + core_in[XY * PIECE].astype(F32))

        def add_pair(piece):
            units = pl.ds(piece * PIECE, PIECE)
            mid[piece, 0:PIECE] = (
                stage[c, units].astype(F32) + core_in[units].astype(F32)
            ).astype(B16)
            if half == 1:
                mid[piece, PIECE] = small16

        each(0, XY, add_pair)
        each(1, XY, lambda step: plane_copy(half, step).start())

    def sum_plane(half):
        mid, plane_in, near_out = halves[half][2:5]
        each(1, XY, lambda step: plane_copy(half, step).wait_recv())
        total = mid[mine].astype(F32)
        for step in range(1, XY):
            total = total + plane_in[step].astype(F32)
        for part in range(NEAR):
            near_out[part, 0:SHARE] = total[part * SHARE : (part + 1) * SHARE].astype(B16)
        if half == 1:
            small16 = resum(total[PIECE])
            for part in range(NEAR):
                near_out[part, SHARE] = small16
        for step in range(1, NEAR):
            near_copy(half, step).start()

    def sum_near(half):
        near_out, near_in, far_sum = halves[half][4:7]
        for step in range(1, NEAR):
            near_copy(half, step).wait_recv()
        total = near_out[z % NEAR].astype(F32)
        for step in range(1, NEAR):
            total = total + near_in[step].astype(F32)
        far_sum[0, 0:SHARE] = total[0:SHARE].astype(B16)
        if half == 1:
            far_sum[0, SHARE] = resum(total[SHARE])
        for step in range(1, NEAR):
            far_copy(half, step).start()

    def sum_far(half):
        far_sum, last = halves[half][6:8]
        for step in range(1, NEAR):
            far_copy(half, step).wait_recv()
        total = far_sum[0].astype(F32)
        for step in range(1, NEAR):
            total = total + far_sum[step].astype(F32)
        last[z % NEAR] = total[0:SHARE].astype(B16)
        if half == 1:
            small_ref[...] = join_small(total[SHARE])
        for step in range(1, NEAR):
            near_back(half, step).start()

    def give_plane(half):
        last = halves[half][7]
        full = (early_full, late_full)[half]
        for step in range(1, NEAR):
            near_back(half, step).wait_recv()
        for part in range(NEAR):
            full[c, mine, part * SHARE : (part + 1) * SHARE] = last[part]
        each(1, XY, lambda step: plane_back(half, step).start())
        core_back(half, 0).start()

    def give_core(half):
        def pass_on(step):
            plane_back(half, step).wait_recv()
            core_back(half, step).start()

        each(1, XY, pass_on)

    def finish(half):
        core_copy(half).wait_send()
        each(1, XY, lambda step: plane_copy(half, step).wait_send())
        for step in range(1, NEAR):
            near_copy(half, step).wait_send()
            far_copy(half, step).wait_send()
            near_back(half, step).wait_send()
        each(1, XY, lambda step: plane_back(half, step).wait_send())
        each(0, XY, lambda step: core_back(half, step).wait())

    sum_core(0)

    dots_all = dot_back(grad_stack, value)
    lane = lax.broadcasted_iota(jnp.int32, (1, 128), 1)
    gain_row = jnp.zeros((1, 128), F32)
    dscores = []
    for head in range(HEADS):
        dots = dots_all[head * ROWS : (head + 1) * ROWS]
        delta_column = delta[:, head * HEAD_DIM : head * HEAD_DIM + 1]
        dlogit = weights[head].astype(F32) * (dots - delta_column)
        sloped = dlogit * (1.0 - tangents[head] * tangents[head])
        local_sum = jnp.sum(
            jnp.sum(sloped * raws[head], axis=0, keepdims=True), axis=1, keepdims=True
        )
        far_sum = far_gain_row[:, head * HEAD_DIM : head * HEAD_DIM + 1]
        gain_row = jnp.where(lane == head, local_sum, gain_row)
        gain_row = jnp.where(lane == HEADS + head, far_sum, gain_row)
        dscores.append((sloped * (local_ref[head] / 8.0)).astype(B16))
    grad_query = (
        grad_query32 + dot(jnp.concatenate(dscores, axis=1), stacked(key))
    ).astype(B16)
    grad_key = dot_outer(jnp.concatenate(dscores, axis=0), query_stack).astype(B16)
    grad_value = dot_outer(jnp.concatenate(weights, axis=0), grad_stack).astype(B16)
    order = list(range(MATCH))
    all_hidden = jnp.concatenate([hidden] + [far_hiddens[m] for m in order], axis=0)
    grad_wq = dot_outer(hidden, grad_query)
    grad_wk = dot_outer(
        all_hidden, jnp.concatenate([grad_key] + [key_terms[m] for m in order], axis=0)
    )
    grad_wv = dot_outer(
        all_hidden, jnp.concatenate([grad_value] + [value_terms[m] for m in order], axis=0)
    )
    grad_hidden = (
        dot_back(grad_query, wq_ref[...]) + dot_back(grad_key, wk) + dot_back(grad_value, wv)
    )
    grad_gain1 = grad_gain1 + jnp.sum(grad_hidden * normed1, axis=0, keepdims=True)
    for number, grad in enumerate((grad_wq, grad_wk, grad_wv, grad_wout)):
        for part in range(2):
            put_units(late_stage, part, number * 32, grad[:, part * 128 : part * 128 + 128])
    small = jnp.concatenate(
        [
            grad_gain1[:, 0:128],
            grad_gain1[:, 128:256],
            grad_gain2[:, 0:128],
            grad_gain2[:, 128:256],
            gain_row,
            jnp.zeros((3, 128), F32),
        ],
        axis=0,
    )
    small16 = spread_small(small)
    late_stage[0, XY * PIECE] = small16
    late_stage[1, XY * PIECE] = small16
    core_copy(1).start()
    sum_core(1)
    sum_plane(0)
    sum_plane(1)
    sum_near(0)
    sum_near(1)

    for matching in reversed(range(MATCH)):
        far_back(matching).wait_recv()
        grad_hidden = grad_hidden + back_in[matching].astype(F32)
    grad_feats_ref[...] = (
        grad_mixed + norm_backward(grad_hidden, normed1, inverse1, gain1)
    ).astype(B16)

    sum_far(0)
    sum_far(1)
    give_plane(0)
    give_plane(1)
    give_core(0)
    give_core(1)
    finish(0)
    finish(1)
    for part in range(2):
        far_piece(part).wait_send()
        far_relay(part).wait_send()
    far_out(2).wait_send()
    far_out(3).wait_send()
    for matching in range(MATCH):
        far_back(matching).wait_send()


def half_scratch(extra):
    shapes = [
        (2, XY * PIECE + extra),
        (XY * PIECE + extra,),
        (XY, PIECE + extra),
        (XY, PIECE + extra),
        (NEAR, SHARE + extra),
        (NEAR, SHARE + extra),
        (NEAR, SHARE + extra),
        (NEAR, SHARE),
    ]
    return [pltpu.VMEM((*shape, 8, 128), B16) for shape in shapes]


def layer(*args):
    vmem = pl.BlockSpec(memory_space=pltpu.VMEM)
    hbm = pl.BlockSpec(memory_space=pltpu.HBM)
    held = [
        pltpu.SMEM(arg.shape, arg.dtype) if number in (10, 11) else pltpu.VMEM(arg.shape, arg.dtype)
        for number, arg in enumerate(args)
    ]
    return pl.pallas_call(
        layer_kernel,
        out_shape=[
            jax.ShapeDtypeStruct((ROWS, WIDTH), B16),
            jax.ShapeDtypeStruct((ROWS, WIDTH), B16),
            jax.ShapeDtypeStruct((2, XY, PIECE, 8, 128), B16),
            jax.ShapeDtypeStruct((2, XY, PIECE, 8, 128), B16),
            jax.ShapeDtypeStruct((8, 128), F32),
        ],
        in_specs=[hbm] * 13,
        out_specs=[vmem] * 5,
        scratch_shapes=held
        + [
            pltpu.VMEM((MATCH, ROWS, WIDTH), B16),
            pltpu.VMEM((MATCH, ROWS, WIDTH), B16),
            pltpu.VMEM((MATCH, ROWS, WIDTH), B16),
        ]
        + half_scratch(0)
        + half_scratch(1)
        + [
            pltpu.SemaphoreType.DMA((2, SEMS)),
            pltpu.SemaphoreType.DMA((13,)),
        ],
        compiler_params=pltpu.CompilerParams(
            collective_id=0, has_side_effects=True, vmem_limit_bytes=48 * 1024 * 1024
        ),
    )(*[pltpu.with_memory_space_constraint(arg, pltpu.HBM) for arg in args])


def write_kernel(node_ref, feats_ref, early_full, late_full, small, node_out, feats_out, *outs):
    node_out[...] = node_ref[...]
    feats_out[...] = feats_ref[...]
    gain1, wq, wk, wv, wout, gain2, up, down, near, far = outs
    for half in range(2):
        early = early_full[half].reshape(XY * PIECE, 8, 128)
        late = late_full[half].reshape(XY * PIECE, 8, 128)

        def take(units, at, count):
            return units[at : at + count].astype(F32).reshape(count * 8, 128)

        lanes = slice(half * 128, half * 128 + 128)
        for number, ref in enumerate((wq, wk, wv, wout)):
            ref[:, lanes] = take(late, number * 32, 32)
        if half == 0:
            for part in range(2):
                down[:, part * 128 : part * 128 + 128] = take(early, part * 64, 64)
        else:
            for part in range(4):
                up[:, part * 128 : part * 128 + 128] = take(early, part * 32, 32)
    gain1[:, 0:128] = small[0:1, :]
    gain1[:, 128:256] = small[1:2, :]
    gain2[:, 0:128] = small[2:3, :]
    gain2[:, 128:256] = small[3:4, :]
    near[...] = small[4:5, 0:HEADS]
    far[...] = small[4:5, HEADS : 2 * HEADS]


def write_out(*args):
    vmem = pl.BlockSpec(memory_space=pltpu.VMEM)
    shapes = [
        ((ROWS, WIDTH), B16),
        ((ROWS, WIDTH), B16),
        ((1, WIDTH), F32),
        ((WIDTH, WIDTH), F32),
        ((WIDTH, WIDTH), F32),
        ((WIDTH, WIDTH), F32),
        ((WIDTH, WIDTH), F32),
        ((1, WIDTH), F32),
        ((WIDTH, 2 * WIDTH), F32),
        ((2 * WIDTH, WIDTH), F32),
        ((1, HEADS), F32),
        ((1, HEADS), F32),
    ]
    return pl.pallas_call(
        write_kernel,
        out_shape=[jax.ShapeDtypeStruct(*shape) for shape in shapes],
        in_specs=[vmem] * 5,
        out_specs=[vmem] * len(shapes),
        compiler_params=pltpu.CompilerParams(vmem_limit_bytes=48 * 1024 * 1024),
    )(*args)


def local(
    node_feats,
    out_grad,
    norm1_gain,
    w_query,
    w_key,
    w_value,
    w_out,
    norm2_gain,
    w_up,
    w_down,
    local_gain,
    expander_gain,
    partner_perm,
    block_pairs,
    pair_count,
):
    summed = layer(
        node_feats[0],
        out_grad[0],
        norm1_gain[None],
        w_query,
        w_key,
        w_value,
        w_out,
        norm2_gain[None],
        w_up,
        w_down,
        local_gain,
        expander_gain,
        partner_perm[0, :, 0, :],
    )
    node_out, grad_feats, gain1, wq, wk, wv, wout, gain2, up, down, near, far = write_out(*summed)
    return (
        node_out[None],
        grad_feats[None],
        gain1[0],
        wq,
        wk,
        wv,
        wout,
        gain2[0],
        up,
        down,
        near[0],
        far[0],
    )


def solution(mesh):
    return jax.shard_map(
        local,
        mesh=mesh,
        in_specs=(
            P("rep", "dom", None),
            P("rep", "dom", None),
            P(),
            P(),
            P(),
            P(),
            P(),
            P(),
            P(),
            P(),
            P(),
            P(),
            P("rep", None, "dom", None),
            P("rep", "dom", None),
            P("rep", "dom"),
        ),
        out_specs=(
            P("rep", "dom", None),
            P("rep", "dom", None),
            P(),
            P(),
            P(),
            P(),
            P(),
            P(),
            P(),
            P(),
            P(),
            P(),
        ),
        check_vma=False,
    )
```

```python
import jax
import jax.numpy as jnp
from jax import lax
from jax.experimental import pallas as pl
from jax.experimental.pallas import tpu as pltpu
from jax.sharding import PartitionSpec as P

EPSILON = 1e-05
SCORE_CAP = 5.0
GELU_ROOT = 0.7978845608028654
GELU_CUBIC = 0.044715

ROWS = 128
WIDTH = 256
HEADS = 4
HEAD_DIM = 64
MATCH = 4
SIDE = 4
GROUP = 16
SHARE = 2
PIECE = GROUP * SHARE
HALF = SIDE * PIECE
MESH = pl.DeviceIdType.MESH
F32 = jnp.float32
B16 = jnp.bfloat16

CORE = 0
FIRST = 1
SECOND = 2
FAR_SUM = 3
SECOND_BACK = 4
FIRST_BACK = 5
CORE_BACK = 6
BLOCK = 7
SEND = 2 * BLOCK
RELAY = SEND + 4
RETURN = RELAY + 2
SEMS = RETURN + 1


def place():
    dom = lax.axis_index("dom")
    rep = lax.axis_index("rep")
    return dom // 8, (dom // 2) % 4, dom % 2, rep


def device(z, y, c, x):
    return {"dom": (z * 4 + y) * 2 + c, "rep": x}


def first_spot(half):
    z, y, c, x = place()
    return (x, y)[half]


def first_peer(half, step):
    z, y, c, x = place()
    other = (first_spot(half) + step) % SIDE
    return other, device(z, y, c, other) if half == 0 else device(z, other, c, x)


def second_spot(half):
    z, y, c, x = place()
    return (y, x)[half] * SIDE + z % SIDE


def second_peer(half, step):
    z, y, c, x = place()
    side = ((y, x)[half] + step // SIDE) % SIDE
    near = (z % SIDE + step % SIDE) % SIDE
    far_z = (z // SIDE) * SIDE + near
    where = device(far_z, side, c, x) if half == 0 else device(far_z, y, c, side)
    return side * SIDE + near, where


def far_peer(step):
    z, y, c, x = place()
    return device((z + SIDE * step) % 16, y, c, x)


def partner(matching):
    z, y, c, x = place()
    reach = 8 >> matching
    return device(z + reach - 2 * reach * ((z // reach) % 2), y, c, x)


def relay_target():
    z, y, c, x = place()
    high = z + 8 - 16 * ((z // 8) % 2)
    return device(high + 4 - 8 * ((z // 4) % 2), y, c, x)


def each(first, last, body):
    def step(index, carry):
        body(index)
        return carry

    lax.fori_loop(first, last, step, 0)


def enter():
    z, y, c, x = place()
    barrier = pltpu.get_barrier_semaphore()

    def greet(peer):
        pl.semaphore_signal(barrier, inc=1, device_id=peer, device_id_type=MESH)

    for step in range(1, SIDE):
        greet(far_peer(step))
    each(1, GROUP, lambda step: greet(second_peer(0, step)[1]))
    greet(device(z, y, 1 - c, x))

    def side(step):
        for near in range(SIDE):
            greet(second_peer(1, step * SIDE + near)[1])

    each(1, SIDE, side)
    pl.semaphore_wait(barrier, (SIDE - 1) + (GROUP - 1) + 1 + SIDE * (SIDE - 1))


def remote(src, dst, sems, at, peer):
    return pltpu.make_async_remote_copy(
        src_ref=src,
        dst_ref=dst,
        send_sem=sems.at[0, at],
        recv_sem=sems.at[1, at],
        device_id=peer,
        device_id_type=MESH,
    )


def spread_small(total):
    row = lax.broadcasted_iota(jnp.int32, (8, 128), 0)
    high = total.astype(B16).astype(F32)
    low = pltpu.roll(total - high, 1, 0)
    return jnp.where(row == 5, low, total).astype(B16)


def join_small(parts):
    row = lax.broadcasted_iota(jnp.int32, (8, 128), 0)
    low = pltpu.roll(parts, 7, 0)
    return jnp.where(row == 4, parts + low, parts)


def resum(parts):
    return spread_small(join_small(parts))


def dot(left, right):
    return jnp.dot(left, right, preferred_element_type=F32)


def dot_back(left, right):
    return lax.dot_general(left, right, (((1,), (1,)), ((), ())), preferred_element_type=F32)


def dot_outer(left, right):
    return lax.dot_general(left, right, (((0,), (0,)), ((), ())), preferred_element_type=F32)


def gelu_parts(preact):
    square = preact * preact
    tangent = jnp.tanh(GELU_ROOT * (preact + GELU_CUBIC * square * preact))
    half = 0.5 * (1.0 + tangent)
    result = preact * half
    derivative = half + 0.5 * preact * (1.0 - tangent * tangent) * (
        GELU_ROOT + 3.0 * GELU_ROOT * GELU_CUBIC * square
    )
    return (result, derivative)


def norm_forward(matrix):
    center = jnp.mean(matrix, axis=-1, keepdims=True)
    shifted = matrix - center
    inverse = lax.rsqrt(jnp.mean(shifted * shifted, axis=-1, keepdims=True) + EPSILON)
    return (shifted * inverse, inverse)


def norm_backward(upstream, normed, inverse, gain):
    scaled_up = upstream * gain
    return inverse * (
        scaled_up
        - jnp.mean(scaled_up, axis=-1, keepdims=True)
        - normed * jnp.mean(scaled_up * normed, axis=-1, keepdims=True)
    )


def head_of_lane(shape, axis):
    return lax.broadcasted_iota(jnp.int32, shape, axis) >> 6


def head_sum(products, block_ones):
    high = products.astype(B16)
    low = (products - high.astype(F32)).astype(B16)
    return dot(high, block_ones) + dot(low, block_ones)


def put_units(stage, half, at, matrix):
    units = matrix.shape[0] // 8
    stage[half, at : at + units] = matrix.reshape(units, 8, 128).astype(B16)


def layer_kernel(*refs):
    sources, refs = refs[0:13], refs[13:]
    node_out_ref, grad_feats_ref, early_full, late_full, small_ref = refs[0:5]
    held, refs = refs[5:18], refs[18:]
    (
        feats_ref,
        up_ref,
        gain1_ref,
        wq_ref,
        wk_ref,
        wv_ref,
        wo_ref,
        gain2_ref,
        wup_ref,
        wdn_ref,
        local_ref,
        far_ref,
        perm_ref,
    ) = held
    far_in, back_out, back_in = refs[0:3]
    halves = (refs[3:11], refs[11:19])
    sems, load_sems = refs[19:21]
    fulls = (early_full, late_full)
    early_stage, late_stage = halves[0][0], halves[1][0]

    def load(number):
        return pltpu.make_async_copy(sources[number], held[number], load_sems.at[number])

    for number in (0, 2, 3, 4, 5, 10, 11, 12, 1, 9, 6, 7, 8):
        load(number).start()
    z, y, c, x = place()
    sibling = device(z, y, 1 - c, x)
    enter()

    pieces = (pl.ds(0, ROWS // 2), pl.ds(ROWS // 2, ROWS // 2))

    def far_out(matching):
        return remote(
            sources[0], far_in.at[matching], sems, SEND + matching, partner(matching)
        )

    def far_piece(part):
        rows = pieces[part]
        return remote(
            sources[0].at[rows], far_in.at[1, rows], sems, SEND + part, partner(1)
        )

    def far_relay(part):
        rows = pieces[part]
        return remote(
            far_in.at[1, rows], far_in.at[0, rows], sems, RELAY + part, relay_target()
        )

    def far_back(matching):
        return remote(
            back_out.at[matching],
            back_in.at[matching],
            sems,
            RETURN,
            partner(matching),
        )

    far_piece(0).start()
    far_piece(1).start()
    far_out(2).start()
    far_out(3).start()

    for number in (0, 2, 3, 4, 5, 10, 11, 12):
        load(number).wait()
    lane_head = head_of_lane((1, WIDTH), 1)
    masks = [jnp.where(lane_head == head, 1.0, 0.0) for head in range(HEADS)]
    masks16 = [mask.astype(B16) for mask in masks]
    ones_rows = head_of_lane((WIDTH, WIDTH), 0)
    ones_lanes = head_of_lane((WIDTH, WIDTH), 1)
    block_ones = jnp.where(ones_rows == ones_lanes, 1.0, 0.0).astype(B16)
    far_gain = sum(masks[head] * far_ref[head] for head in range(HEADS))

    def stacked(matrix):
        return jnp.concatenate([matrix * mask for mask in masks16], axis=0)

    gain1 = gain1_ref[...]
    wk = wk_ref[...]
    wv = wv_ref[...]
    features = feats_ref[...].astype(F32)
    normed1, inverse1 = norm_forward(features)
    hidden = (normed1 * gain1).astype(B16)
    query = dot(hidden, wq_ref[...]).astype(B16)
    key = dot(hidden, wk).astype(B16)
    value = dot(hidden, wv).astype(B16)
    query32 = query.astype(F32)
    query_stack = stacked(query)
    raw_all = dot_back(query_stack, key) * (1.0 / 8.0)
    raws, tangents, exps = [], [], []
    denominator = jnp.zeros((ROWS, WIDTH), F32)
    for head in range(HEADS):
        raw = raw_all[head * ROWS : (head + 1) * ROWS]
        tangent = jnp.tanh(raw * (local_ref[head] / SCORE_CAP))
        exped = jnp.exp(SCORE_CAP * tangent)
        denominator = denominator + masks[head] * jnp.sum(exped, axis=1, keepdims=True)
        raws.append(raw)
        tangents.append(tangent)
        exps.append(exped)
    for number in (1, 9, 6, 7, 8):
        load(number).wait()
    gain2 = gain2_ref[...]
    upstream = up_ref[...]
    grad_act = dot_back(upstream, wdn_ref[...])

    for part in range(2):
        far_piece(part).wait_recv()
        far_relay(part).start()
    one_hots, far_norms, far_hiddens, far_keys, far_values = {}, {}, {}, {}, {}
    far_raws, far_tangents, far_exps = {}, {}, {}
    rows = lax.broadcasted_iota(jnp.int32, (ROWS, ROWS), 0)
    for matching in reversed(range(MATCH)):
        one_hot = jnp.where(rows == perm_ref[matching : matching + 1, :], 1.0, 0.0)
        one_hots[matching] = one_hot.astype(B16)
        if matching >= 2:
            far_out(matching).wait_recv()
        elif matching == 0:
            far_relay(0).wait_recv()
            far_relay(1).wait_recv()
        picked = dot_outer(one_hots[matching], far_in[matching])
        normed, _ = norm_forward(picked)
        far_norms[matching] = normed
        far_hiddens[matching] = (normed * gain1).astype(B16)
        far_keys[matching] = dot(far_hiddens[matching], wk).astype(B16)
        far_values[matching] = dot(far_hiddens[matching], wv).astype(B16)
        raw = head_sum(query32 * far_keys[matching].astype(F32), block_ones) * (1.0 / 8.0)
        tangent = jnp.tanh(raw * (far_gain * (1.0 / SCORE_CAP)))
        exped = jnp.exp(SCORE_CAP * tangent)
        denominator = denominator + exped
        far_raws[matching] = raw
        far_tangents[matching] = tangent
        far_exps[matching] = exped

    inverse_den = 1.0 / denominator
    weights = [
        (exps[head] * inverse_den[:, head * HEAD_DIM : head * HEAD_DIM + 1]).astype(B16)
        for head in range(HEADS)
    ]
    weight_lanes = jnp.concatenate(weights, axis=1)
    attended32 = dot(weight_lanes, stacked(value))
    far_weights = {}
    for matching in range(MATCH):
        weight = (far_exps[matching] * inverse_den).astype(B16).astype(F32)
        far_weights[matching] = weight
        attended32 = attended32 + weight * far_values[matching].astype(F32)
    attended = attended32.astype(B16)

    mixed = (features + dot(attended, wo_ref[...])).astype(B16).astype(F32)
    normed2, inverse2 = norm_forward(mixed)
    hidden2 = (normed2 * gain2).astype(B16)
    activ, derivative = gelu_parts(dot(hidden2, wup_ref[...]))
    activ = activ.astype(B16)
    grad_pre = (grad_act * derivative).astype(B16)
    grad_hidden2 = dot_back(grad_pre, wup_ref[...])
    grad_mixed = upstream.astype(F32) + norm_backward(grad_hidden2, normed2, inverse2, gain2)
    grad_mixed16 = grad_mixed.astype(B16)
    grad_att = dot_back(grad_mixed16, wo_ref[...]).astype(B16)
    node_out_ref[...] = (mixed + dot(activ, wdn_ref[...])).astype(B16)
    grad_gain2 = jnp.sum(grad_hidden2 * normed2, axis=0, keepdims=True)

    def core_copy(half):
        stage, core_in = halves[half][0:2]
        return remote(stage.at[1 - c], core_in, sems, half * BLOCK + CORE, sibling)

    grad_down = dot_outer(activ, upstream)
    grad_up = dot_outer(hidden2, grad_pre)
    for part in range(2):
        put_units(early_stage, 0, part * 64, grad_down[:, part * 128 : part * 128 + 128])
    for part in range(4):
        put_units(early_stage, 1, part * 32, grad_up[:, part * 128 : part * 128 + 128])
    core_copy(0).start()
    grad_wout = dot_outer(attended, grad_mixed16)

    grad_att32 = grad_att.astype(F32)
    grad_stack = stacked(grad_att)
    delta = head_sum(grad_att32 * attended32, block_ones)
    far_gain_row = jnp.zeros((1, WIDTH), F32)
    grad_query32 = jnp.zeros((ROWS, WIDTH), F32)
    grad_gain1 = jnp.zeros((1, WIDTH), F32)
    key_terms, value_terms = {}, {}
    for matching in range(MATCH):
        weight = far_weights[matching]
        dots = head_sum(grad_att32 * far_values[matching].astype(F32), block_ones)
        dlogit = weight * (dots - delta)
        sloped = dlogit * (1.0 - far_tangents[matching] * far_tangents[matching])
        far_gain_row = far_gain_row + jnp.sum(
            sloped * far_raws[matching], axis=0, keepdims=True
        )
        dscore = (sloped * (far_gain * (1.0 / 8.0))).astype(B16).astype(F32)
        grad_query32 = grad_query32 + dscore * far_keys[matching].astype(F32)
        key_terms[matching] = (dscore * query32).astype(B16)
        value_terms[matching] = (weight * grad_att32).astype(B16)
        returned = dot_back(key_terms[matching], wk) + dot_back(value_terms[matching], wv)
        grad_gain1 = grad_gain1 + jnp.sum(
            returned * far_norms[matching], axis=0, keepdims=True
        )
        back_out[matching] = dot(one_hots[matching], returned.astype(B16)).astype(B16)
        far_back(matching).start()

    def stage_copy(src, dst, half, stage, where):
        return remote(src, dst, sems, half * BLOCK + stage, where)

    def stage_wait(whole, half, stage):
        return stage_copy(whole, whole, half, stage, sibling)

    def first_copy(half, step):
        first_out, first_in = halves[half][2:4]
        peer, where = first_peer(half, step)
        return stage_copy(first_out.at[peer], first_in.at[step], half, FIRST, where)

    def second_copy(half, step):
        second_out, second_in = halves[half][4:6]
        peer, where = second_peer(half, step)
        return stage_copy(second_out.at[peer], second_in.at[step], half, SECOND, where)

    def far_copy(half, step):
        far_sum = halves[half][6]
        return stage_copy(far_sum.at[0], far_sum.at[step], half, FAR_SUM, far_peer(step))

    def second_back(half, step):
        slot = halves[half][7].at[second_spot(half)]
        return stage_copy(slot, slot, half, SECOND_BACK, second_peer(half, step)[1])

    def first_back(half, step):
        slot = fulls[half].at[c, first_spot(half)]
        return stage_copy(slot, slot, half, FIRST_BACK, first_peer(half, step)[1])

    def core_back(half):
        slot = fulls[half].at[c]
        return stage_copy(slot, slot, half, CORE_BACK, sibling)

    def first_wait(half):
        return stage_wait(halves[half][3].at[1:SIDE], half, FIRST)

    def second_wait(half):
        return stage_wait(halves[half][5].at[1:GROUP], half, SECOND)

    def far_wait(half):
        return stage_wait(halves[half][6].at[1:SIDE], half, FAR_SUM)

    def second_back_wait(half):
        return stage_wait(halves[half][7].at[1:GROUP], half, SECOND_BACK)

    def first_back_wait(half):
        return stage_wait(fulls[half].at[c, 1:SIDE], half, FIRST_BACK)

    def sum_core(half):
        stage, core_in, first_out = halves[half][0:3]
        core_copy(half).wait_recv()
        for piece in range(SIDE):
            units = pl.ds(piece * PIECE, PIECE)
            first_out[piece, 0:PIECE] = (
                stage[c, units].astype(F32) + core_in[units].astype(F32)
            ).astype(B16)
        if half == 1:
            small16 = resum(stage[0, HALF].astype(F32) + core_in[HALF].astype(F32))
            for piece in range(SIDE):
                first_out[piece, PIECE] = small16
        for step in range(1, SIDE):
            first_copy(half, step).start()

    def sum_first(half):
        first_out, first_in, second_out = halves[half][2:5]
        first_wait(half).wait_recv()
        total = first_out[first_spot(half)].astype(F32)
        for step in range(1, SIDE):
            total = total + first_in[step].astype(F32)
        second_out[:, 0:SHARE] = total[0:PIECE].astype(B16).reshape(GROUP, SHARE, 8, 128)
        if half == 1:
            small16 = resum(total[PIECE])
            for part in range(GROUP):
                second_out[part, SHARE] = small16
        each(1, GROUP, lambda step: second_copy(half, step).start())

    def sum_second(half):
        second_out, second_in, far_sum = halves[half][4:7]
        second_wait(half).wait_recv()
        total = second_out[second_spot(half)].astype(F32)
        for step in range(1, GROUP):
            total = total + second_in[step].astype(F32)
        far_sum[0, 0:SHARE] = total[0:SHARE].astype(B16)
        if half == 1:
            far_sum[0, SHARE] = resum(total[SHARE])
        for step in range(1, SIDE):
            far_copy(half, step).start()

    def sum_far(half):
        far_sum, last = halves[half][6:8]
        far_wait(half).wait_recv()
        total = far_sum[0].astype(F32)
        for step in range(1, SIDE):
            total = total + far_sum[step].astype(F32)
        last[second_spot(half)] = total[0:SHARE].astype(B16)
        each(1, GROUP, lambda step: second_back(half, step).start())
        if half == 1:
            small_ref[...] = join_small(total[SHARE])

    def give_first(half):
        second_back_wait(half).wait_recv()
        fulls[half][c, first_spot(half)] = halves[half][7][...].reshape(PIECE, 8, 128)
        for step in range(1, SIDE):
            first_back(half, step).start()

    def give_core(half):
        first_back_wait(half).wait_recv()
        core_back(half).start()

    def finish(half):
        core_copy(half).wait_send()
        first_wait(half).wait_send()
        second_wait(half).wait_send()
        far_wait(half).wait_send()
        second_back_wait(half).wait_send()
        first_back_wait(half).wait_send()
        core_back(half).wait()

    sum_core(0)

    dots_all = dot_back(grad_stack, value)
    lane = lax.broadcasted_iota(jnp.int32, (1, 128), 1)
    gain_row = jnp.zeros((1, 128), F32)
    dscores = []
    for head in range(HEADS):
        dots = dots_all[head * ROWS : (head + 1) * ROWS]
        delta_column = delta[:, head * HEAD_DIM : head * HEAD_DIM + 1]
        dlogit = weights[head].astype(F32) * (dots - delta_column)
        sloped = dlogit * (1.0 - tangents[head] * tangents[head])
        local_sum = jnp.sum(
            jnp.sum(sloped * raws[head], axis=0, keepdims=True), axis=1, keepdims=True
        )
        far_sum = far_gain_row[:, head * HEAD_DIM : head * HEAD_DIM + 1]
        gain_row = jnp.where(lane == head, local_sum, gain_row)
        gain_row = jnp.where(lane == HEADS + head, far_sum, gain_row)
        dscores.append((sloped * (local_ref[head] / 8.0)).astype(B16))
    grad_query = (
        grad_query32 + dot(jnp.concatenate(dscores, axis=1), stacked(key))
    ).astype(B16)
    grad_key = dot_outer(jnp.concatenate(dscores, axis=0), query_stack).astype(B16)
    grad_value = dot_outer(jnp.concatenate(weights, axis=0), grad_stack).astype(B16)
    order = list(range(MATCH))
    all_hidden = jnp.concatenate([hidden] + [far_hiddens[m] for m in order], axis=0)
    grad_wq = dot_outer(hidden, grad_query)
    grad_wk = dot_outer(
        all_hidden, jnp.concatenate([grad_key] + [key_terms[m] for m in order], axis=0)
    )
    grad_wv = dot_outer(
        all_hidden, jnp.concatenate([grad_value] + [value_terms[m] for m in order], axis=0)
    )
    grad_hidden = (
        dot_back(grad_query, wq_ref[...]) + dot_back(grad_key, wk) + dot_back(grad_value, wv)
    )
    grad_gain1 = grad_gain1 + jnp.sum(grad_hidden * normed1, axis=0, keepdims=True)
    for number, grad in enumerate((grad_wq, grad_wk, grad_wv, grad_wout)):
        for part in range(2):
            put_units(late_stage, part, number * 32, grad[:, part * 128 : part * 128 + 128])
    small = jnp.concatenate(
        [
            grad_gain1[:, 0:128],
            grad_gain1[:, 128:256],
            grad_gain2[:, 0:128],
            grad_gain2[:, 128:256],
            gain_row,
            jnp.zeros((3, 128), F32),
        ],
        axis=0,
    )
    small16 = spread_small(small)
    late_stage[0, HALF] = small16
    late_stage[1, HALF] = small16
    core_copy(1).start()
    sum_core(1)
    sum_first(0)
    sum_first(1)
    sum_second(0)
    sum_second(1)

    remote(back_out, back_in, sems, RETURN, sibling).wait_recv()
    for matching in range(MATCH):
        grad_hidden = grad_hidden + back_in[matching].astype(F32)
    grad_feats_ref[...] = (
        grad_mixed + norm_backward(grad_hidden, normed1, inverse1, gain1)
    ).astype(B16)

    sum_far(0)
    sum_far(1)
    give_first(0)
    give_first(1)
    give_core(0)
    give_core(1)
    finish(0)
    finish(1)
    for part in range(2):
        far_piece(part).wait_send()
        far_relay(part).wait_send()
    far_out(2).wait_send()
    far_out(3).wait_send()
    remote(back_out, back_in, sems, RETURN, sibling).wait_send()


def half_scratch(extra):
    shapes = [
        (2, HALF + extra),
        (HALF + extra,),
        (SIDE, PIECE + extra),
        (SIDE, PIECE + extra),
        (GROUP, SHARE + extra),
        (GROUP, SHARE + extra),
        (SIDE, SHARE + extra),
        (GROUP, SHARE),
    ]
    return [pltpu.VMEM((*shape, 8, 128), B16) for shape in shapes]


def layer(*args):
    vmem = pl.BlockSpec(memory_space=pltpu.VMEM)
    hbm = pl.BlockSpec(memory_space=pltpu.HBM)
    held = [
        pltpu.SMEM(arg.shape, arg.dtype) if number in (10, 11) else pltpu.VMEM(arg.shape, arg.dtype)
        for number, arg in enumerate(args)
    ]
    return pl.pallas_call(
        layer_kernel,
        out_shape=[
            jax.ShapeDtypeStruct((ROWS, WIDTH), B16),
            jax.ShapeDtypeStruct((ROWS, WIDTH), B16),
            jax.ShapeDtypeStruct((2, SIDE, PIECE, 8, 128), B16),
            jax.ShapeDtypeStruct((2, SIDE, PIECE, 8, 128), B16),
            jax.ShapeDtypeStruct((8, 128), F32),
        ],
        in_specs=[hbm] * 13,
        out_specs=[vmem] * 5,
        scratch_shapes=held
        + [
            pltpu.VMEM((MATCH, ROWS, WIDTH), B16),
            pltpu.VMEM((MATCH, ROWS, WIDTH), B16),
            pltpu.VMEM((MATCH, ROWS, WIDTH), B16),
        ]
        + half_scratch(0)
        + half_scratch(1)
        + [
            pltpu.SemaphoreType.DMA((2, SEMS)),
            pltpu.SemaphoreType.DMA((13,)),
        ],
        compiler_params=pltpu.CompilerParams(
            collective_id=0, has_side_effects=True, vmem_limit_bytes=48 * 1024 * 1024
        ),
    )(*[pltpu.with_memory_space_constraint(arg, pltpu.HBM) for arg in args])


def write_kernel(node_ref, feats_ref, early_full, late_full, small, node_out, feats_out, *outs):
    node_out[...] = node_ref[...]
    feats_out[...] = feats_ref[...]
    gain1, wq, wk, wv, wout, gain2, up, down, near, far = outs
    for half in range(2):
        early = early_full[half].reshape(HALF, 8, 128)
        late = late_full[half].reshape(HALF, 8, 128)

        def take(units, at, count):
            return units[at : at + count].astype(F32).reshape(count * 8, 128)

        lanes = slice(half * 128, half * 128 + 128)
        for number, ref in enumerate((wq, wk, wv, wout)):
            ref[:, lanes] = take(late, number * 32, 32)
        if half == 0:
            for part in range(2):
                down[:, part * 128 : part * 128 + 128] = take(early, part * 64, 64)
        else:
            for part in range(4):
                up[:, part * 128 : part * 128 + 128] = take(early, part * 32, 32)
    gain1[:, 0:128] = small[0:1, :]
    gain1[:, 128:256] = small[1:2, :]
    gain2[:, 0:128] = small[2:3, :]
    gain2[:, 128:256] = small[3:4, :]
    near[...] = small[4:5, 0:HEADS]
    far[...] = small[4:5, HEADS : 2 * HEADS]


def write_out(*args):
    vmem = pl.BlockSpec(memory_space=pltpu.VMEM)
    shapes = [
        ((ROWS, WIDTH), B16),
        ((ROWS, WIDTH), B16),
        ((1, WIDTH), F32),
        ((WIDTH, WIDTH), F32),
        ((WIDTH, WIDTH), F32),
        ((WIDTH, WIDTH), F32),
        ((WIDTH, WIDTH), F32),
        ((1, WIDTH), F32),
        ((WIDTH, 2 * WIDTH), F32),
        ((2 * WIDTH, WIDTH), F32),
        ((1, HEADS), F32),
        ((1, HEADS), F32),
    ]
    return pl.pallas_call(
        write_kernel,
        out_shape=[jax.ShapeDtypeStruct(*shape) for shape in shapes],
        in_specs=[vmem] * 5,
        out_specs=[vmem] * len(shapes),
        compiler_params=pltpu.CompilerParams(vmem_limit_bytes=48 * 1024 * 1024),
    )(*args)


def local(
    node_feats,
    out_grad,
    norm1_gain,
    w_query,
    w_key,
    w_value,
    w_out,
    norm2_gain,
    w_up,
    w_down,
    local_gain,
    expander_gain,
    partner_perm,
    block_pairs,
    pair_count,
):
    summed = layer(
        node_feats[0],
        out_grad[0],
        norm1_gain[None],
        w_query,
        w_key,
        w_value,
        w_out,
        norm2_gain[None],
        w_up,
        w_down,
        local_gain,
        expander_gain,
        partner_perm[0, :, 0, :],
    )
    node_out, grad_feats, gain1, wq, wk, wv, wout, gain2, up, down, near, far = write_out(*summed)
    return (
        node_out[None],
        grad_feats[None],
        gain1[0],
        wq,
        wk,
        wv,
        wout,
        gain2[0],
        up,
        down,
        near[0],
        far[0],
    )


def solution(mesh):
    return jax.shard_map(
        local,
        mesh=mesh,
        in_specs=(
            P("rep", "dom", None),
            P("rep", "dom", None),
            P(),
            P(),
            P(),
            P(),
            P(),
            P(),
            P(),
            P(),
            P(),
            P(),
            P("rep", None, "dom", None),
            P("rep", "dom", None),
            P("rep", "dom"),
        ),
        out_specs=(
            P("rep", "dom", None),
            P("rep", "dom", None),
            P(),
            P(),
            P(),
            P(),
            P(),
            P(),
            P(),
            P(),
            P(),
            P(),
        ),
        check_vma=False,
    )
```

```python
import jax
import jax.numpy as jnp
from jax import lax
from jax.experimental import pallas as pl
from jax.experimental.pallas import tpu as pltpu
from jax.sharding import PartitionSpec as P

EPSILON = 1e-05
SCORE_CAP = 5.0
GELU_ROOT = 0.7978845608028654
GELU_CUBIC = 0.044715

ROWS = 128
WIDTH = 256
HEADS = 4
HEAD_DIM = 64
MATCH = 4
PARTS = 4
NEAR = 4
PLANE = 16
SHARE = 2
PIECE = NEAR * SHARE
HALF = PLANE * PIECE
MESH = pl.DeviceIdType.MESH
F32 = jnp.float32
B16 = jnp.bfloat16

CORE = 0
PLANE_OUT = 1
NEAR_OUT = 2
FAR_SUM = 3
NEAR_BACK = 4
PLANE_BACK = 5
CORE_BACK = 6
BLOCK = 7
SEND = 2 * BLOCK
RELAY = SEND + PARTS + 2
RETURN = RELAY + PARTS
SEMS = RETURN + 1


def place():
    dom = lax.axis_index("dom")
    rep = lax.axis_index("rep")
    return dom // 8, (dom // 2) % 4, dom % 2, rep


def device(z, y, c, x):
    return {"dom": (z * 4 + y) * 2 + c, "rep": x}


def plane_spot():
    z, y, c, x = place()
    return x * 4 + y


def plane_peer(step):
    z, y, c, x = place()
    far_x = (x + step // 4) % 4
    far_y = (y + step % 4) % 4
    return far_x * 4 + far_y, device(z, far_y, c, far_x)


def near_spot():
    z, y, c, x = place()
    return z % NEAR


def near_peer(step):
    z, y, c, x = place()
    other = (z % NEAR + step) % NEAR
    return other, device((z // NEAR) * NEAR + other, y, c, x)


def far_peer(step):
    z, y, c, x = place()
    return device((z + NEAR * step) % 16, y, c, x)


def partner(matching):
    z, y, c, x = place()
    reach = 8 >> matching
    return device(z + reach - 2 * reach * ((z // reach) % 2), y, c, x)


def relay_target():
    z, y, c, x = place()
    high = z + 8 - 16 * ((z // 8) % 2)
    return device(high + 4 - 8 * ((z // 4) % 2), y, c, x)


def each(first, last, body):
    def step(index, carry):
        body(index)
        return carry

    lax.fori_loop(first, last, step, 0)


def enter():
    z, y, c, x = place()
    barrier = pltpu.get_barrier_semaphore()

    def greet(peer):
        pl.semaphore_signal(barrier, inc=1, device_id=peer, device_id_type=MESH)

    for step in range(1, NEAR):
        greet(far_peer(step))
        greet(near_peer(step)[1])
    greet(device(z, y, 1 - c, x))
    each(1, PLANE, lambda step: greet(plane_peer(step)[1]))
    pl.semaphore_wait(barrier, 2 * (NEAR - 1) + 1 + (PLANE - 1))


def remote(src, dst, sems, at, peer):
    return pltpu.make_async_remote_copy(
        src_ref=src,
        dst_ref=dst,
        send_sem=sems.at[0, at],
        recv_sem=sems.at[1, at],
        device_id=peer,
        device_id_type=MESH,
    )


def spread_small(total):
    row = lax.broadcasted_iota(jnp.int32, (8, 128), 0)
    high = total.astype(B16).astype(F32)
    low = pltpu.roll(total - high, 1, 0)
    return jnp.where(row == 5, low, total).astype(B16)


def join_small(parts):
    row = lax.broadcasted_iota(jnp.int32, (8, 128), 0)
    low = pltpu.roll(parts, 7, 0)
    return jnp.where(row == 4, parts + low, parts)


def resum(parts):
    return spread_small(join_small(parts))


def dot(left, right):
    return jnp.dot(left, right, preferred_element_type=F32)


def dot_back(left, right):
    return lax.dot_general(left, right, (((1,), (1,)), ((), ())), preferred_element_type=F32)


def dot_outer(left, right):
    return lax.dot_general(left, right, (((0,), (0,)), ((), ())), preferred_element_type=F32)


def gelu_parts(preact):
    square = preact * preact
    tangent = jnp.tanh(GELU_ROOT * (preact + GELU_CUBIC * square * preact))
    half = 0.5 * (1.0 + tangent)
    result = preact * half
    derivative = half + 0.5 * preact * (1.0 - tangent * tangent) * (
        GELU_ROOT + 3.0 * GELU_ROOT * GELU_CUBIC * square
    )
    return (result, derivative)


def norm_forward(matrix):
    center = jnp.mean(matrix, axis=-1, keepdims=True)
    shifted = matrix - center
    inverse = lax.rsqrt(jnp.mean(shifted * shifted, axis=-1, keepdims=True) + EPSILON)
    return (shifted * inverse, inverse)


def norm_backward(upstream, normed, inverse, gain):
    scaled_up = upstream * gain
    return inverse * (
        scaled_up
        - jnp.mean(scaled_up, axis=-1, keepdims=True)
        - normed * jnp.mean(scaled_up * normed, axis=-1, keepdims=True)
    )


def head_of_lane(shape, axis):
    return lax.broadcasted_iota(jnp.int32, shape, axis) >> 6


def head_sum(products, block_ones):
    high = products.astype(B16)
    low = (products - high.astype(F32)).astype(B16)
    return dot(high, block_ones) + dot(low, block_ones)


def put_units(stage, half, at, matrix):
    units = matrix.shape[0] // 8
    stage[half, at : at + units] = matrix.reshape(units, 8, 128).astype(B16)


def layer_kernel(*refs):
    sources, refs = refs[0:13], refs[13:]
    node_out_ref, grad_feats_ref, early_full, late_full, small_ref = refs[0:5]
    held, refs = refs[5:18], refs[18:]
    (
        feats_ref,
        up_ref,
        gain1_ref,
        wq_ref,
        wk_ref,
        wv_ref,
        wo_ref,
        gain2_ref,
        wup_ref,
        wdn_ref,
        local_ref,
        far_ref,
        perm_ref,
    ) = held
    far_in, back_out, back_in = refs[0:3]
    halves = (refs[3:11], refs[11:19])
    sems, load_sems = refs[19:21]
    fulls = (early_full, late_full)
    early_stage, late_stage = halves[0][0], halves[1][0]

    def load(number):
        return pltpu.make_async_copy(sources[number], held[number], load_sems.at[number])

    for number in (0, 2, 3, 4, 5, 10, 11, 12, 1, 9, 6, 7, 8):
        load(number).start()
    z, y, c, x = place()
    sibling = device(z, y, 1 - c, x)
    enter()

    pieces = [pl.ds(at, ROWS // PARTS) for at in range(0, ROWS, ROWS // PARTS)]

    def far_out(matching):
        return remote(
            sources[0], far_in.at[matching], sems, SEND + PARTS + matching - 2, partner(matching)
        )

    def far_piece(part):
        rows = pieces[part]
        return remote(
            sources[0].at[rows], far_in.at[1, rows], sems, SEND + part, partner(1)
        )

    def far_relay(part):
        rows = pieces[part]
        return remote(
            far_in.at[1, rows], far_in.at[0, rows], sems, RELAY + part, relay_target()
        )

    def far_back(matching):
        return remote(
            back_out.at[matching],
            back_in.at[matching],
            sems,
            RETURN,
            partner(matching),
        )

    for part in range(PARTS):
        far_piece(part).start()
    far_out(2).start()
    far_out(3).start()

    for number in (0, 2, 3, 4, 5, 10, 11, 12):
        load(number).wait()
    lane_head = head_of_lane((1, WIDTH), 1)
    masks = [jnp.where(lane_head == head, 1.0, 0.0) for head in range(HEADS)]
    masks16 = [mask.astype(B16) for mask in masks]
    ones_rows = head_of_lane((WIDTH, WIDTH), 0)
    ones_lanes = head_of_lane((WIDTH, WIDTH), 1)
    block_ones = jnp.where(ones_rows == ones_lanes, 1.0, 0.0).astype(B16)
    far_gain = sum(masks[head] * far_ref[head] for head in range(HEADS))

    def stacked(matrix):
        return jnp.concatenate([matrix * mask for mask in masks16], axis=0)

    gain1 = gain1_ref[...]
    wk = wk_ref[...]
    wv = wv_ref[...]
    features = feats_ref[...].astype(F32)
    normed1, inverse1 = norm_forward(features)
    hidden = (normed1 * gain1).astype(B16)
    query = dot(hidden, wq_ref[...]).astype(B16)
    key = dot(hidden, wk).astype(B16)
    value = dot(hidden, wv).astype(B16)
    query32 = query.astype(F32)
    query_stack = stacked(query)
    raw_all = dot_back(query_stack, key) * (1.0 / 8.0)
    raws, tangents, exps = [], [], []
    denominator = jnp.zeros((ROWS, WIDTH), F32)
    for head in range(HEADS):
        raw = raw_all[head * ROWS : (head + 1) * ROWS]
        tangent = jnp.tanh(raw * (local_ref[head] / SCORE_CAP))
        exped = jnp.exp(SCORE_CAP * tangent)
        denominator = denominator + masks[head] * jnp.sum(exped, axis=1, keepdims=True)
        raws.append(raw)
        tangents.append(tangent)
        exps.append(exped)
    for number in (1, 9, 6, 7, 8):
        load(number).wait()
    gain2 = gain2_ref[...]
    upstream = up_ref[...]
    grad_act = dot_back(upstream, wdn_ref[...])

    for part in range(PARTS):
        far_piece(part).wait_recv()
        far_relay(part).start()
    one_hots, far_norms, far_hiddens, far_keys, far_values = {}, {}, {}, {}, {}
    far_raws, far_tangents, far_exps = {}, {}, {}
    rows = lax.broadcasted_iota(jnp.int32, (ROWS, ROWS), 0)
    for matching in reversed(range(MATCH)):
        one_hot = jnp.where(rows == perm_ref[matching : matching + 1, :], 1.0, 0.0)
        one_hots[matching] = one_hot.astype(B16)
        if matching >= 2:
            far_out(matching).wait_recv()
        elif matching == 0:
            for part in range(PARTS):
                far_relay(part).wait_recv()
        picked = dot_outer(one_hots[matching], far_in[matching])
        normed, _ = norm_forward(picked)
        far_norms[matching] = normed
        far_hiddens[matching] = (normed * gain1).astype(B16)
        far_keys[matching] = dot(far_hiddens[matching], wk).astype(B16)
        far_values[matching] = dot(far_hiddens[matching], wv).astype(B16)
        raw = head_sum(query32 * far_keys[matching].astype(F32), block_ones) * (1.0 / 8.0)
        tangent = jnp.tanh(raw * (far_gain * (1.0 / SCORE_CAP)))
        exped = jnp.exp(SCORE_CAP * tangent)
        denominator = denominator + exped
        far_raws[matching] = raw
        far_tangents[matching] = tangent
        far_exps[matching] = exped

    inverse_den = 1.0 / denominator
    weights = [
        (exps[head] * inverse_den[:, head * HEAD_DIM : head * HEAD_DIM + 1]).astype(B16)
        for head in range(HEADS)
    ]
    weight_lanes = jnp.concatenate(weights, axis=1)
    attended32 = dot(weight_lanes, stacked(value))
    far_weights = {}
    for matching in range(MATCH):
        weight = (far_exps[matching] * inverse_den).astype(B16).astype(F32)
        far_weights[matching] = weight
        attended32 = attended32 + weight * far_values[matching].astype(F32)
    attended = attended32.astype(B16)

    mixed = (features + dot(attended, wo_ref[...])).astype(B16).astype(F32)
    normed2, inverse2 = norm_forward(mixed)
    hidden2 = (normed2 * gain2).astype(B16)
    activ, derivative = gelu_parts(dot(hidden2, wup_ref[...]))
    activ = activ.astype(B16)
    grad_pre = (grad_act * derivative).astype(B16)
    grad_hidden2 = dot_back(grad_pre, wup_ref[...])
    grad_mixed = upstream.astype(F32) + norm_backward(grad_hidden2, normed2, inverse2, gain2)
    grad_mixed16 = grad_mixed.astype(B16)
    grad_att = dot_back(grad_mixed16, wo_ref[...]).astype(B16)
    node_out_ref[...] = (mixed + dot(activ, wdn_ref[...])).astype(B16)
    grad_gain2 = jnp.sum(grad_hidden2 * normed2, axis=0, keepdims=True)

    def core_copy(half):
        stage, core_in = halves[half][0:2]
        return remote(stage.at[1 - c], core_in, sems, half * BLOCK + CORE, sibling)

    grad_down = dot_outer(activ, upstream)
    grad_up = dot_outer(hidden2, grad_pre)
    for part in range(2):
        put_units(early_stage, 0, part * 64, grad_down[:, part * 128 : part * 128 + 128])
    for part in range(4):
        put_units(early_stage, 1, part * 32, grad_up[:, part * 128 : part * 128 + 128])
    core_copy(0).start()
    grad_wout = dot_outer(attended, grad_mixed16)

    grad_att32 = grad_att.astype(F32)
    grad_stack = stacked(grad_att)
    delta = head_sum(grad_att32 * attended32, block_ones)
    far_gain_row = jnp.zeros((1, WIDTH), F32)
    grad_query32 = jnp.zeros((ROWS, WIDTH), F32)
    grad_gain1 = jnp.zeros((1, WIDTH), F32)
    key_terms, value_terms = {}, {}
    for matching in range(MATCH):
        weight = far_weights[matching]
        dots = head_sum(grad_att32 * far_values[matching].astype(F32), block_ones)
        dlogit = weight * (dots - delta)
        sloped = dlogit * (1.0 - far_tangents[matching] * far_tangents[matching])
        far_gain_row = far_gain_row + jnp.sum(
            sloped * far_raws[matching], axis=0, keepdims=True
        )
        dscore = (sloped * (far_gain * (1.0 / 8.0))).astype(B16).astype(F32)
        grad_query32 = grad_query32 + dscore * far_keys[matching].astype(F32)
        key_terms[matching] = (dscore * query32).astype(B16)
        value_terms[matching] = (weight * grad_att32).astype(B16)
        returned = dot_back(key_terms[matching], wk) + dot_back(value_terms[matching], wv)
        grad_gain1 = grad_gain1 + jnp.sum(
            returned * far_norms[matching], axis=0, keepdims=True
        )
        back_out[matching] = dot(one_hots[matching], returned.astype(B16)).astype(B16)
        far_back(matching).start()

    def stage_copy(src, dst, half, stage, where):
        return remote(src, dst, sems, half * BLOCK + stage, where)

    def stage_wait(whole, half, stage):
        return stage_copy(whole, whole, half, stage, sibling)

    def plane_copy(half, step):
        plane_out, plane_in = halves[half][2:4]
        peer, where = plane_peer(step)
        return stage_copy(plane_out.at[peer], plane_in.at[step], half, PLANE_OUT, where)

    def near_copy(half, step):
        near_out, near_in = halves[half][4:6]
        peer, where = near_peer(step)
        return stage_copy(near_out.at[peer], near_in.at[step], half, NEAR_OUT, where)

    def far_copy(half, step):
        far_sum = halves[half][6]
        return stage_copy(far_sum.at[0], far_sum.at[step], half, FAR_SUM, far_peer(step))

    def near_back(half, step):
        slot = halves[half][7].at[near_spot()]
        return stage_copy(slot, slot, half, NEAR_BACK, near_peer(step)[1])

    def plane_back(half, step):
        slot = fulls[half].at[c, plane_spot()]
        return stage_copy(slot, slot, half, PLANE_BACK, plane_peer(step)[1])

    def core_back(half):
        slot = fulls[half].at[c]
        return stage_copy(slot, slot, half, CORE_BACK, sibling)

    def plane_wait(half):
        return stage_wait(halves[half][3].at[1:PLANE], half, PLANE_OUT)

    def near_wait(half):
        return stage_wait(halves[half][5].at[1:NEAR], half, NEAR_OUT)

    def far_wait(half):
        return stage_wait(halves[half][6].at[1:NEAR], half, FAR_SUM)

    def near_back_wait(half):
        return stage_wait(halves[half][7].at[1:NEAR], half, NEAR_BACK)

    def plane_back_wait(half):
        return stage_wait(fulls[half].at[c, 1:PLANE], half, PLANE_BACK)

    def sum_core(half):
        stage, core_in, plane_out = halves[half][0:3]
        core_copy(half).wait_recv()
        plane_out[:, 0:PIECE] = (
            (stage[c, 0:HALF].astype(F32) + core_in[0:HALF].astype(F32))
            .astype(B16)
            .reshape(PLANE, PIECE, 8, 128)
        )
        if half == 1:
            small16 = resum(stage[0, HALF].astype(F32) + core_in[HALF].astype(F32))
            for piece in range(PLANE):
                plane_out[piece, PIECE] = small16
        each(1, PLANE, lambda step: plane_copy(half, step).start())

    def sum_plane(half):
        plane_out, plane_in, near_out = halves[half][2:5]
        plane_wait(half).wait_recv()
        total = plane_out[plane_spot()].astype(F32)
        for step in range(1, PLANE):
            total = total + plane_in[step].astype(F32)
        near_out[:, 0:SHARE] = total[0:PIECE].astype(B16).reshape(NEAR, SHARE, 8, 128)
        if half == 1:
            small16 = resum(total[PIECE])
            for part in range(NEAR):
                near_out[part, SHARE] = small16
        for step in range(1, NEAR):
            near_copy(half, step).start()

    def sum_near(half):
        near_out, near_in, far_sum = halves[half][4:7]
        near_wait(half).wait_recv()
        total = near_out[near_spot()].astype(F32)
        for step in range(1, NEAR):
            total = total + near_in[step].astype(F32)
        far_sum[0, 0:SHARE] = total[0:SHARE].astype(B16)
        if half == 1:
            far_sum[0, SHARE] = resum(total[SHARE])
        for step in range(1, NEAR):
            far_copy(half, step).start()

    def sum_far(half):
        far_sum, last = halves[half][6:8]
        far_wait(half).wait_recv()
        total = far_sum[0].astype(F32)
        for step in range(1, NEAR):
            total = total + far_sum[step].astype(F32)
        last[near_spot()] = total[0:SHARE].astype(B16)
        for step in range(1, NEAR):
            near_back(half, step).start()
        if half == 1:
            small_ref[...] = join_small(total[SHARE])

    def give_plane(half):
        near_back_wait(half).wait_recv()
        fulls[half][c, plane_spot()] = halves[half][7][...].reshape(PIECE, 8, 128)
        each(1, PLANE, lambda step: plane_back(half, step).start())

    def give_core(half):
        plane_back_wait(half).wait_recv()
        core_back(half).start()

    def finish(half):
        core_copy(half).wait_send()
        plane_wait(half).wait_send()
        near_wait(half).wait_send()
        far_wait(half).wait_send()
        near_back_wait(half).wait_send()
        plane_back_wait(half).wait_send()
        core_back(half).wait()

    dots_all = dot_back(grad_stack, value)
    lane = lax.broadcasted_iota(jnp.int32, (1, 128), 1)
    gain_row = jnp.zeros((1, 128), F32)
    dscores = []
    for head in range(HEADS):
        dots = dots_all[head * ROWS : (head + 1) * ROWS]
        delta_column = delta[:, head * HEAD_DIM : head * HEAD_DIM + 1]
        dlogit = weights[head].astype(F32) * (dots - delta_column)
        sloped = dlogit * (1.0 - tangents[head] * tangents[head])
        local_sum = jnp.sum(
            jnp.sum(sloped * raws[head], axis=0, keepdims=True), axis=1, keepdims=True
        )
        far_sum = far_gain_row[:, head * HEAD_DIM : head * HEAD_DIM + 1]
        gain_row = jnp.where(lane == head, local_sum, gain_row)
        gain_row = jnp.where(lane == HEADS + head, far_sum, gain_row)
        dscores.append((sloped * (local_ref[head] / 8.0)).astype(B16))
    grad_query = (
        grad_query32 + dot(jnp.concatenate(dscores, axis=1), stacked(key))
    ).astype(B16)
    grad_key = dot_outer(jnp.concatenate(dscores, axis=0), query_stack).astype(B16)
    grad_value = dot_outer(jnp.concatenate(weights, axis=0), grad_stack).astype(B16)
    order = list(range(MATCH))
    all_hidden = jnp.concatenate([hidden] + [far_hiddens[m] for m in order], axis=0)
    grad_wq = dot_outer(hidden, grad_query)
    grad_wk = dot_outer(
        all_hidden, jnp.concatenate([grad_key] + [key_terms[m] for m in order], axis=0)
    )
    grad_wv = dot_outer(
        all_hidden, jnp.concatenate([grad_value] + [value_terms[m] for m in order], axis=0)
    )
    grad_hidden = (
        dot_back(grad_query, wq_ref[...]) + dot_back(grad_key, wk) + dot_back(grad_value, wv)
    )
    grad_gain1 = grad_gain1 + jnp.sum(grad_hidden * normed1, axis=0, keepdims=True)
    for number, grad in enumerate((grad_wq, grad_wk, grad_wv, grad_wout)):
        for part in range(2):
            put_units(late_stage, part, number * 32, grad[:, part * 128 : part * 128 + 128])
    small = jnp.concatenate(
        [
            grad_gain1[:, 0:128],
            grad_gain1[:, 128:256],
            grad_gain2[:, 0:128],
            grad_gain2[:, 128:256],
            gain_row,
            jnp.zeros((3, 128), F32),
        ],
        axis=0,
    )
    small16 = spread_small(small)
    late_stage[0, HALF] = small16
    late_stage[1, HALF] = small16
    core_copy(1).start()
    sum_core(0)
    sum_core(1)
    sum_plane(0)
    sum_plane(1)
    sum_near(0)
    sum_near(1)

    remote(back_out, back_in, sems, RETURN, sibling).wait_recv()
    for matching in range(MATCH):
        grad_hidden = grad_hidden + back_in[matching].astype(F32)
    grad_feats_ref[...] = (
        grad_mixed + norm_backward(grad_hidden, normed1, inverse1, gain1)
    ).astype(B16)

    sum_far(0)
    sum_far(1)
    give_plane(0)
    give_plane(1)
    give_core(0)
    give_core(1)
    finish(0)
    finish(1)
    for part in range(PARTS):
        far_piece(part).wait_send()
        far_relay(part).wait_send()
    far_out(2).wait_send()
    far_out(3).wait_send()
    remote(back_out, back_in, sems, RETURN, sibling).wait_send()


def half_scratch(extra):
    shapes = [
        (2, HALF + extra),
        (HALF + extra,),
        (PLANE, PIECE + extra),
        (PLANE, PIECE + extra),
        (NEAR, SHARE + extra),
        (NEAR, SHARE + extra),
        (NEAR, SHARE + extra),
        (NEAR, SHARE),
    ]
    return [pltpu.VMEM((*shape, 8, 128), B16) for shape in shapes]


def layer(*args):
    vmem = pl.BlockSpec(memory_space=pltpu.VMEM)
    hbm = pl.BlockSpec(memory_space=pltpu.HBM)
    held = [
        pltpu.SMEM(arg.shape, arg.dtype) if number in (10, 11) else pltpu.VMEM(arg.shape, arg.dtype)
        for number, arg in enumerate(args)
    ]
    return pl.pallas_call(
        layer_kernel,
        out_shape=[
            jax.ShapeDtypeStruct((ROWS, WIDTH), B16),
            jax.ShapeDtypeStruct((ROWS, WIDTH), B16),
            jax.ShapeDtypeStruct((2, PLANE, PIECE, 8, 128), B16),
            jax.ShapeDtypeStruct((2, PLANE, PIECE, 8, 128), B16),
            jax.ShapeDtypeStruct((8, 128), F32),
        ],
        in_specs=[hbm] * 13,
        out_specs=[vmem] * 5,
        scratch_shapes=held
        + [
            pltpu.VMEM((MATCH, ROWS, WIDTH), B16),
            pltpu.VMEM((MATCH, ROWS, WIDTH), B16),
            pltpu.VMEM((MATCH, ROWS, WIDTH), B16),
        ]
        + half_scratch(0)
        + half_scratch(1)
        + [
            pltpu.SemaphoreType.DMA((2, SEMS)),
            pltpu.SemaphoreType.DMA((13,)),
        ],
        compiler_params=pltpu.CompilerParams(
            collective_id=0, has_side_effects=True, vmem_limit_bytes=48 * 1024 * 1024
        ),
    )(*[pltpu.with_memory_space_constraint(arg, pltpu.HBM) for arg in args])


WRITTEN = (
    ((1, WIDTH), F32),
    ((WIDTH, WIDTH), F32),
    ((WIDTH, WIDTH), F32),
    ((WIDTH, WIDTH), F32),
    ((WIDTH, WIDTH), F32),
    ((1, WIDTH), F32),
    ((WIDTH, 2 * WIDTH), F32),
    ((2 * WIDTH, WIDTH), F32),
    ((1, HEADS), F32),
    ((1, HEADS), F32),
)


def write_kernel(node_ref, feats_ref, early_full, late_full, small, *refs):
    outs, held, sems = refs[0:12], refs[12:22], refs[22]
    gain1, wq, wk, wv, wout, gain2, up, down, near, far = held

    def copy(number):
        source = (node_ref, feats_ref, *held)[number]
        return pltpu.make_async_copy(source, outs[number], sems.at[number])

    def take(full, half, at, count):
        pieces = full[half, at // PIECE : (at + count) // PIECE]
        return pieces.astype(F32).reshape(count * 8, 128)

    copy(0).start()
    copy(1).start()
    for part in range(2):
        down[:, part * 128 : part * 128 + 128] = take(early_full, 0, part * 64, 64)
    copy(9).start()
    for part in range(4):
        up[:, part * 128 : part * 128 + 128] = take(early_full, 1, part * 32, 32)
    copy(8).start()
    for number, ref in enumerate((wq, wk, wv, wout)):
        for half in range(2):
            ref[:, half * 128 : half * 128 + 128] = take(late_full, half, number * 32, 32)
        copy(3 + number).start()
    for part in range(2):
        gain1[:, part * 128 : part * 128 + 128] = small[part : part + 1, :]
        gain2[:, part * 128 : part * 128 + 128] = small[2 + part : 3 + part, :]
    near[...] = small[4:5, 0:HEADS]
    far[...] = small[4:5, HEADS : 2 * HEADS]
    for number in (2, 7, 10, 11):
        copy(number).start()
    for number in range(12):
        copy(number).wait()


def write_out(*args):
    vmem = pl.BlockSpec(memory_space=pltpu.VMEM)
    hbm = pl.BlockSpec(memory_space=pltpu.HBM)
    rows = ((ROWS, WIDTH), B16)
    return pl.pallas_call(
        write_kernel,
        out_shape=[jax.ShapeDtypeStruct(*shape) for shape in (rows, rows, *WRITTEN)],
        in_specs=[vmem] * 5,
        out_specs=[hbm] * 12,
        scratch_shapes=[pltpu.VMEM(*shape) for shape in WRITTEN]
        + [pltpu.SemaphoreType.DMA((12,))],
        compiler_params=pltpu.CompilerParams(vmem_limit_bytes=48 * 1024 * 1024),
    )(*args)


def local(
    node_feats,
    out_grad,
    norm1_gain,
    w_query,
    w_key,
    w_value,
    w_out,
    norm2_gain,
    w_up,
    w_down,
    local_gain,
    expander_gain,
    partner_perm,
    block_pairs,
    pair_count,
):
    summed = layer(
        node_feats[0],
        out_grad[0],
        norm1_gain[None],
        w_query,
        w_key,
        w_value,
        w_out,
        norm2_gain[None],
        w_up,
        w_down,
        local_gain,
        expander_gain,
        partner_perm[0, :, 0, :],
    )
    node_out, grad_feats, gain1, wq, wk, wv, wout, gain2, up, down, near, far = write_out(*summed)
    return (
        node_out[None],
        grad_feats[None],
        gain1[0],
        wq,
        wk,
        wv,
        wout,
        gain2[0],
        up,
        down,
        near[0],
        far[0],
    )


def solution(mesh):
    return jax.shard_map(
        local,
        mesh=mesh,
        in_specs=(
            P("rep", "dom", None),
            P("rep", "dom", None),
            P(),
            P(),
            P(),
            P(),
            P(),
            P(),
            P(),
            P(),
            P(),
            P(),
            P("rep", None, "dom", None),
            P("rep", "dom", None),
            P("rep", "dom"),
        ),
        out_specs=(
            P("rep", "dom", None),
            P("rep", "dom", None),
            P(),
            P(),
            P(),
            P(),
            P(),
            P(),
            P(),
            P(),
            P(),
            P(),
        ),
        check_vma=False,
    )
```

```python
import jax
import jax.numpy as jnp
from jax import lax
from jax.experimental import pallas as pl
from jax.experimental.pallas import tpu as pltpu
from jax.sharding import PartitionSpec as P

EPSILON = 1e-05
SCORE_CAP = 5.0
GELU_ROOT = 0.7978845608028654
GELU_CUBIC = 0.044715

ROWS = 128
WIDTH = 256
HEADS = 4
HEAD_DIM = 64
MATCH = 4
PARTS = 4
NEAR = 4
PLANE = 16
SHARE = 2
PIECE = NEAR * SHARE
HALF = PLANE * PIECE
MESH = pl.DeviceIdType.MESH
F32 = jnp.float32
B16 = jnp.bfloat16

CORE = 0
PLANE_OUT = 1
NEAR_OUT = 2
FAR_SUM = 3
NEAR_BACK = 4
PLANE_BACK = 5
CORE_BACK = 6
BLOCK = 7
SEND = 2 * BLOCK
RELAY = SEND + PARTS + 2
RETURN = RELAY + PARTS
SEMS = RETURN + 1


def place():
    dom = lax.axis_index("dom")
    rep = lax.axis_index("rep")
    return dom // 8, (dom // 2) % 4, dom % 2, rep


def device(z, y, c, x):
    return {"dom": (z * 4 + y) * 2 + c, "rep": x}


def plane_spot():
    z, y, c, x = place()
    return x * 4 + y


def plane_peer(step):
    z, y, c, x = place()
    far_x = (x + step // 4) % 4
    far_y = (y + step % 4) % 4
    return far_x * 4 + far_y, device(z, far_y, c, far_x)


def near_spot():
    z, y, c, x = place()
    return z % NEAR


def near_peer(step):
    z, y, c, x = place()
    other = (z % NEAR + step) % NEAR
    return other, device((z // NEAR) * NEAR + other, y, c, x)


def far_peer(step):
    z, y, c, x = place()
    return device((z + NEAR * step) % 16, y, c, x)


def partner(matching):
    z, y, c, x = place()
    reach = 8 >> matching
    return device(z + reach - 2 * reach * ((z // reach) % 2), y, c, x)


def relay_target():
    z, y, c, x = place()
    high = z + 8 - 16 * ((z // 8) % 2)
    return device(high + 4 - 8 * ((z // 4) % 2), y, c, x)


def each(first, last, body):
    def step(index, carry):
        body(index)
        return carry

    lax.fori_loop(first, last, step, 0)


def enter():
    z, y, c, x = place()
    barrier = pltpu.get_barrier_semaphore()

    def greet(peer):
        pl.semaphore_signal(barrier, inc=1, device_id=peer, device_id_type=MESH)

    for step in (1, 3):
        greet(far_peer(step))
    for step in range(1, NEAR):
        greet(near_peer(step)[1])
    greet(device(z, y, 1 - c, x))
    each(1, PLANE, lambda step: greet(plane_peer(step)[1]))
    pl.semaphore_wait(barrier, 2 + (NEAR - 1) + 1 + (PLANE - 1))


def remote(src, dst, sems, at, peer):
    return pltpu.make_async_remote_copy(
        src_ref=src,
        dst_ref=dst,
        send_sem=sems.at[0, at],
        recv_sem=sems.at[1, at],
        device_id=peer,
        device_id_type=MESH,
    )


def spread_small(total):
    row = lax.broadcasted_iota(jnp.int32, (8, 128), 0)
    high = total.astype(B16).astype(F32)
    low = pltpu.roll(total - high, 1, 0)
    return jnp.where(row == 5, low, total).astype(B16)


def join_small(parts):
    row = lax.broadcasted_iota(jnp.int32, (8, 128), 0)
    low = pltpu.roll(parts, 7, 0)
    return jnp.where(row == 4, parts + low, parts)


def resum(parts):
    return spread_small(join_small(parts))


def dot(left, right):
    return jnp.dot(left, right, preferred_element_type=F32)


def dot_back(left, right):
    return lax.dot_general(left, right, (((1,), (1,)), ((), ())), preferred_element_type=F32)


def dot_outer(left, right):
    return lax.dot_general(left, right, (((0,), (0,)), ((), ())), preferred_element_type=F32)


def gelu_parts(preact):
    square = preact * preact
    tangent = jnp.tanh(GELU_ROOT * (preact + GELU_CUBIC * square * preact))
    half = 0.5 * (1.0 + tangent)
    result = preact * half
    derivative = half + 0.5 * preact * (1.0 - tangent * tangent) * (
        GELU_ROOT + 3.0 * GELU_ROOT * GELU_CUBIC * square
    )
    return (result, derivative)


def norm_forward(matrix):
    center = jnp.mean(matrix, axis=-1, keepdims=True)
    shifted = matrix - center
    inverse = lax.rsqrt(jnp.mean(shifted * shifted, axis=-1, keepdims=True) + EPSILON)
    return (shifted * inverse, inverse)


def norm_backward(upstream, normed, inverse, gain):
    scaled_up = upstream * gain
    return inverse * (
        scaled_up
        - jnp.mean(scaled_up, axis=-1, keepdims=True)
        - normed * jnp.mean(scaled_up * normed, axis=-1, keepdims=True)
    )


def head_of_lane(shape, axis):
    return lax.broadcasted_iota(jnp.int32, shape, axis) >> 6


def head_sum(products, block_ones):
    high = products.astype(B16)
    low = (products - high.astype(F32)).astype(B16)
    return dot(high, block_ones) + dot(low, block_ones)


def put_units(stage, half, at, matrix):
    units = matrix.shape[0] // 8
    stage[half, at : at + units] = matrix.reshape(units, 8, 128).astype(B16)


def layer_kernel(*refs):
    sources, refs = refs[0:13], refs[13:]
    node_out_ref, grad_feats_ref, early_full, late_full, small_ref = refs[0:5]
    held, refs = refs[5:18], refs[18:]
    (
        feats_ref,
        up_ref,
        gain1_ref,
        wq_ref,
        wk_ref,
        wv_ref,
        wo_ref,
        gain2_ref,
        wup_ref,
        wdn_ref,
        local_ref,
        far_ref,
        perm_ref,
    ) = held
    far_in, back_out, back_in = refs[0:3]
    halves = (refs[3:11], refs[11:19])
    sems, load_sems = refs[19:21]
    fulls = (early_full, late_full)
    early_stage, late_stage = halves[0][0], halves[1][0]

    def load(number):
        return pltpu.make_async_copy(sources[number], held[number], load_sems.at[number])

    for number in (0, 2, 3, 4, 5, 10, 11, 12, 1, 9, 6, 7, 8):
        load(number).start()
    z, y, c, x = place()
    sibling = device(z, y, 1 - c, x)
    enter()

    pieces = [pl.ds(at, ROWS // PARTS) for at in range(0, ROWS, ROWS // PARTS)]

    def far_out(matching):
        return remote(
            sources[0], far_in.at[matching], sems, SEND + PARTS + matching - 2, partner(matching)
        )

    def far_piece(part):
        rows = pieces[part]
        return remote(
            sources[0].at[rows], far_in.at[1, rows], sems, SEND + part, partner(1)
        )

    def far_relay(part):
        rows = pieces[part]
        return remote(
            far_in.at[1, rows], far_in.at[0, rows], sems, RELAY + part, relay_target()
        )

    def far_back(matching):
        return remote(
            back_out.at[matching],
            back_in.at[matching],
            sems,
            RETURN,
            partner(matching),
        )

    for part in range(PARTS):
        far_piece(part).start()
    far_out(2).start()
    far_out(3).start()

    for number in (0, 2, 3, 4, 5, 10, 11, 12):
        load(number).wait()
    lane_head = head_of_lane((1, WIDTH), 1)
    masks = [jnp.where(lane_head == head, 1.0, 0.0) for head in range(HEADS)]
    masks16 = [mask.astype(B16) for mask in masks]
    ones_rows = head_of_lane((WIDTH, WIDTH), 0)
    ones_lanes = head_of_lane((WIDTH, WIDTH), 1)
    block_ones = jnp.where(ones_rows == ones_lanes, 1.0, 0.0).astype(B16)
    far_gain = sum(masks[head] * far_ref[head] for head in range(HEADS))

    def stacked(matrix):
        return jnp.concatenate([matrix * mask for mask in masks16], axis=0)

    gain1 = gain1_ref[...]
    wk = wk_ref[...]
    wv = wv_ref[...]
    features = feats_ref[...].astype(F32)
    normed1, inverse1 = norm_forward(features)
    hidden = (normed1 * gain1).astype(B16)
    query = dot(hidden, wq_ref[...]).astype(B16)
    key = dot(hidden, wk).astype(B16)
    value = dot(hidden, wv).astype(B16)
    query32 = query.astype(F32)
    query_stack = stacked(query)
    raw_all = dot_back(query_stack, key) * (1.0 / 8.0)
    raws, tangents, exps = [], [], []
    denominator = jnp.zeros((ROWS, WIDTH), F32)
    for head in range(HEADS):
        raw = raw_all[head * ROWS : (head + 1) * ROWS]
        tangent = jnp.tanh(raw * (local_ref[head] / SCORE_CAP))
        exped = jnp.exp(SCORE_CAP * tangent)
        denominator = denominator + masks[head] * jnp.sum(exped, axis=1, keepdims=True)
        raws.append(raw)
        tangents.append(tangent)
        exps.append(exped)
    for number in (1, 9, 6, 7, 8):
        load(number).wait()
    gain2 = gain2_ref[...]
    upstream = up_ref[...]
    grad_act = dot_back(upstream, wdn_ref[...])

    for part in range(PARTS):
        far_piece(part).wait_recv()
        far_relay(part).start()
    one_hots, far_norms, far_hiddens, far_keys, far_values = {}, {}, {}, {}, {}
    far_raws, far_tangents, far_exps = {}, {}, {}
    rows = lax.broadcasted_iota(jnp.int32, (ROWS, ROWS), 0)
    for matching in reversed(range(MATCH)):
        one_hot = jnp.where(rows == perm_ref[matching : matching + 1, :], 1.0, 0.0)
        one_hots[matching] = one_hot.astype(B16)
        if matching >= 2:
            far_out(matching).wait_recv()
        elif matching == 0:
            for part in range(PARTS):
                far_relay(part).wait_recv()
        picked = dot_outer(one_hots[matching], far_in[matching])
        normed, _ = norm_forward(picked)
        far_norms[matching] = normed
        far_hiddens[matching] = (normed * gain1).astype(B16)
        far_keys[matching] = dot(far_hiddens[matching], wk).astype(B16)
        far_values[matching] = dot(far_hiddens[matching], wv).astype(B16)
        raw = head_sum(query32 * far_keys[matching].astype(F32), block_ones) * (1.0 / 8.0)
        tangent = jnp.tanh(raw * (far_gain * (1.0 / SCORE_CAP)))
        exped = jnp.exp(SCORE_CAP * tangent)
        denominator = denominator + exped
        far_raws[matching] = raw
        far_tangents[matching] = tangent
        far_exps[matching] = exped

    inverse_den = 1.0 / denominator
    weights = [
        (exps[head] * inverse_den[:, head * HEAD_DIM : head * HEAD_DIM + 1]).astype(B16)
        for head in range(HEADS)
    ]
    weight_lanes = jnp.concatenate(weights, axis=1)
    attended32 = dot(weight_lanes, stacked(value))
    far_weights = {}
    for matching in range(MATCH):
        weight = (far_exps[matching] * inverse_den).astype(B16).astype(F32)
        far_weights[matching] = weight
        attended32 = attended32 + weight * far_values[matching].astype(F32)
    attended = attended32.astype(B16)

    mixed = (features + dot(attended, wo_ref[...])).astype(B16).astype(F32)
    normed2, inverse2 = norm_forward(mixed)
    hidden2 = (normed2 * gain2).astype(B16)
    activ, derivative = gelu_parts(dot(hidden2, wup_ref[...]))
    activ = activ.astype(B16)
    grad_pre = (grad_act * derivative).astype(B16)
    grad_hidden2 = dot_back(grad_pre, wup_ref[...])
    grad_mixed = upstream.astype(F32) + norm_backward(grad_hidden2, normed2, inverse2, gain2)
    grad_mixed16 = grad_mixed.astype(B16)
    grad_att = dot_back(grad_mixed16, wo_ref[...]).astype(B16)
    node_out_ref[...] = (mixed + dot(activ, wdn_ref[...])).astype(B16)
    grad_gain2 = jnp.sum(grad_hidden2 * normed2, axis=0, keepdims=True)

    def core_copy(half):
        stage, core_in = halves[half][0:2]
        return remote(stage.at[1 - c], core_in, sems, half * BLOCK + CORE, sibling)

    grad_down = dot_outer(activ, upstream)
    grad_up = dot_outer(hidden2, grad_pre)
    for part in range(2):
        put_units(early_stage, 0, part * 64, grad_down[:, part * 128 : part * 128 + 128])
    for part in range(4):
        put_units(early_stage, 1, part * 32, grad_up[:, part * 128 : part * 128 + 128])
    core_copy(0).start()
    grad_wout = dot_outer(attended, grad_mixed16)

    grad_att32 = grad_att.astype(F32)
    grad_stack = stacked(grad_att)
    delta = head_sum(grad_att32 * attended32, block_ones)
    far_gain_row = jnp.zeros((1, WIDTH), F32)
    grad_query32 = jnp.zeros((ROWS, WIDTH), F32)
    grad_gain1 = jnp.zeros((1, WIDTH), F32)
    key_terms, value_terms = {}, {}
    for matching in range(MATCH):
        weight = far_weights[matching]
        dots = head_sum(grad_att32 * far_values[matching].astype(F32), block_ones)
        dlogit = weight * (dots - delta)
        sloped = dlogit * (1.0 - far_tangents[matching] * far_tangents[matching])
        far_gain_row = far_gain_row + jnp.sum(
            sloped * far_raws[matching], axis=0, keepdims=True
        )
        dscore = (sloped * (far_gain * (1.0 / 8.0))).astype(B16).astype(F32)
        grad_query32 = grad_query32 + dscore * far_keys[matching].astype(F32)
        key_terms[matching] = (dscore * query32).astype(B16)
        value_terms[matching] = (weight * grad_att32).astype(B16)
        returned = dot_back(key_terms[matching], wk) + dot_back(value_terms[matching], wv)
        grad_gain1 = grad_gain1 + jnp.sum(
            returned * far_norms[matching], axis=0, keepdims=True
        )
        back_out[matching] = dot(one_hots[matching], returned.astype(B16)).astype(B16)
        far_back(matching).start()

    def stage_copy(src, dst, half, stage, where):
        return remote(src, dst, sems, half * BLOCK + stage, where)

    def stage_wait(whole, half, stage):
        return stage_copy(whole, whole, half, stage, sibling)

    def plane_copy(half, step):
        plane_out, plane_in = halves[half][2:4]
        peer, where = plane_peer(step)
        return stage_copy(plane_out.at[peer], plane_in.at[step], half, PLANE_OUT, where)

    def near_copy(half, step):
        near_out, near_in = halves[half][4:6]
        peer, where = near_peer(step)
        return stage_copy(near_out.at[peer], near_in.at[step], half, NEAR_OUT, where)

    def far_copy(half, step):
        far_sum = halves[half][6]
        return stage_copy(far_sum.at[0], far_sum.at[step], half, FAR_SUM, far_peer(step))

    def near_back(half, step):
        slot = halves[half][7].at[near_spot()]
        return stage_copy(slot, slot, half, NEAR_BACK, near_peer(step)[1])

    def plane_back(half, step):
        slot = fulls[half].at[c, plane_spot()]
        return stage_copy(slot, slot, half, PLANE_BACK, plane_peer(step)[1])

    def core_back(half):
        slot = fulls[half].at[c]
        return stage_copy(slot, slot, half, CORE_BACK, sibling)

    def plane_wait(half):
        return stage_wait(halves[half][3].at[1:PLANE], half, PLANE_OUT)

    def near_wait(half):
        return stage_wait(halves[half][5].at[1:NEAR], half, NEAR_OUT)

    def far_wait(half):
        return stage_wait(halves[half][6].at[1:NEAR], half, FAR_SUM)

    def near_back_wait(half):
        return stage_wait(halves[half][7].at[1:NEAR], half, NEAR_BACK)

    def plane_back_wait(half):
        return stage_wait(fulls[half].at[c, 1:PLANE], half, PLANE_BACK)

    def sum_core(half):
        stage, core_in, plane_out = halves[half][0:3]
        core_copy(half).wait_recv()
        plane_out[:, 0:PIECE] = (
            (stage[c, 0:HALF].astype(F32) + core_in[0:HALF].astype(F32))
            .astype(B16)
            .reshape(PLANE, PIECE, 8, 128)
        )
        if half == 1:
            small16 = resum(stage[0, HALF].astype(F32) + core_in[HALF].astype(F32))
            for piece in range(PLANE):
                plane_out[piece, PIECE] = small16
        each(1, PLANE, lambda step: plane_copy(half, step).start())

    def sum_plane(half):
        plane_out, plane_in, near_out = halves[half][2:5]
        plane_wait(half).wait_recv()
        total = plane_out[plane_spot()].astype(F32)
        for step in range(1, PLANE):
            total = total + plane_in[step].astype(F32)
        near_out[:, 0:SHARE] = total[0:PIECE].astype(B16).reshape(NEAR, SHARE, 8, 128)
        if half == 1:
            small16 = resum(total[PIECE])
            for part in range(NEAR):
                near_out[part, SHARE] = small16
        for step in range(1, NEAR):
            near_copy(half, step).start()

    def sum_near(half):
        near_out, near_in, far_sum = halves[half][4:7]
        near_wait(half).wait_recv()
        total = near_out[near_spot()].astype(F32)
        for step in range(1, NEAR):
            total = total + near_in[step].astype(F32)
        far_sum[0, 0:SHARE] = total[0:SHARE].astype(B16)
        if half == 1:
            far_sum[0, SHARE] = resum(total[SHARE])
        for step in range(1, NEAR):
            far_copy(half, step).start()

    def sum_far(half):
        far_sum, last = halves[half][6:8]
        far_wait(half).wait_recv()
        total = far_sum[0].astype(F32)
        for step in range(1, NEAR):
            total = total + far_sum[step].astype(F32)
        last[near_spot()] = total[0:SHARE].astype(B16)
        for step in range(1, NEAR):
            near_back(half, step).start()
        if half == 1:
            small_ref[...] = join_small(total[SHARE])

    def give_plane(half):
        near_back_wait(half).wait_recv()
        fulls[half][c, plane_spot()] = halves[half][7][...].reshape(PIECE, 8, 128)
        each(1, PLANE, lambda step: plane_back(half, step).start())

    def give_core(half):
        plane_back_wait(half).wait_recv()
        core_back(half).start()

    def finish(half):
        core_copy(half).wait_send()
        plane_wait(half).wait_send()
        near_wait(half).wait_send()
        far_wait(half).wait_send()
        near_back_wait(half).wait_send()
        plane_back_wait(half).wait_send()
        core_back(half).wait()

    dots_all = dot_back(grad_stack, value)
    lane = lax.broadcasted_iota(jnp.int32, (1, 128), 1)
    gain_row = jnp.zeros((1, 128), F32)
    dscores = []
    for head in range(HEADS):
        dots = dots_all[head * ROWS : (head + 1) * ROWS]
        delta_column = delta[:, head * HEAD_DIM : head * HEAD_DIM + 1]
        dlogit = weights[head].astype(F32) * (dots - delta_column)
        sloped = dlogit * (1.0 - tangents[head] * tangents[head])
        local_sum = jnp.sum(
            jnp.sum(sloped * raws[head], axis=0, keepdims=True), axis=1, keepdims=True
        )
        far_sum = far_gain_row[:, head * HEAD_DIM : head * HEAD_DIM + 1]
        gain_row = jnp.where(lane == head, local_sum, gain_row)
        gain_row = jnp.where(lane == HEADS + head, far_sum, gain_row)
        dscores.append((sloped * (local_ref[head] / 8.0)).astype(B16))
    grad_query = (
        grad_query32 + dot(jnp.concatenate(dscores, axis=1), stacked(key))
    ).astype(B16)
    grad_key = dot_outer(jnp.concatenate(dscores, axis=0), query_stack).astype(B16)
    grad_value = dot_outer(jnp.concatenate(weights, axis=0), grad_stack).astype(B16)
    order = list(range(MATCH))
    all_hidden = jnp.concatenate([hidden] + [far_hiddens[m] for m in order], axis=0)
    grad_wq = dot_outer(hidden, grad_query)
    grad_wk = dot_outer(
        all_hidden, jnp.concatenate([grad_key] + [key_terms[m] for m in order], axis=0)
    )
    grad_wv = dot_outer(
        all_hidden, jnp.concatenate([grad_value] + [value_terms[m] for m in order], axis=0)
    )
    grad_hidden = (
        dot_back(grad_query, wq_ref[...]) + dot_back(grad_key, wk) + dot_back(grad_value, wv)
    )
    grad_gain1 = grad_gain1 + jnp.sum(grad_hidden * normed1, axis=0, keepdims=True)
    for number, grad in enumerate((grad_wq, grad_wk, grad_wv, grad_wout)):
        for part in range(2):
            put_units(late_stage, part, number * 32, grad[:, part * 128 : part * 128 + 128])
    small = jnp.concatenate(
        [
            grad_gain1[:, 0:128],
            grad_gain1[:, 128:256],
            grad_gain2[:, 0:128],
            grad_gain2[:, 128:256],
            gain_row,
            jnp.zeros((3, 128), F32),
        ],
        axis=0,
    )
    small16 = spread_small(small)
    late_stage[0, HALF] = small16
    late_stage[1, HALF] = small16
    core_copy(1).start()
    sum_core(0)
    sum_core(1)
    sum_plane(0)
    sum_plane(1)
    sum_near(0)
    sum_near(1)

    remote(back_out, back_in, sems, RETURN, sibling).wait_recv()
    for matching in range(MATCH):
        grad_hidden = grad_hidden + back_in[matching].astype(F32)
    grad_feats_ref[...] = (
        grad_mixed + norm_backward(grad_hidden, normed1, inverse1, gain1)
    ).astype(B16)

    sum_far(0)
    sum_far(1)
    give_plane(0)
    give_plane(1)
    give_core(0)
    give_core(1)
    finish(0)
    finish(1)
    for part in range(PARTS):
        far_piece(part).wait_send()
        far_relay(part).wait_send()
    far_out(2).wait_send()
    far_out(3).wait_send()
    remote(back_out, back_in, sems, RETURN, sibling).wait_send()


def half_scratch(extra):
    shapes = [
        (2, HALF + extra),
        (HALF + extra,),
        (PLANE, PIECE + extra),
        (PLANE, PIECE + extra),
        (NEAR, SHARE + extra),
        (NEAR, SHARE + extra),
        (NEAR, SHARE + extra),
        (NEAR, SHARE),
    ]
    return [pltpu.VMEM((*shape, 8, 128), B16) for shape in shapes]


def layer(*args):
    vmem = pl.BlockSpec(memory_space=pltpu.VMEM)
    hbm = pl.BlockSpec(memory_space=pltpu.HBM)
    held = [
        pltpu.SMEM(arg.shape, arg.dtype) if number in (10, 11) else pltpu.VMEM(arg.shape, arg.dtype)
        for number, arg in enumerate(args)
    ]
    return pl.pallas_call(
        layer_kernel,
        out_shape=[
            jax.ShapeDtypeStruct((ROWS, WIDTH), B16),
            jax.ShapeDtypeStruct((ROWS, WIDTH), B16),
            jax.ShapeDtypeStruct((2, PLANE, PIECE, 8, 128), B16),
            jax.ShapeDtypeStruct((2, PLANE, PIECE, 8, 128), B16),
            jax.ShapeDtypeStruct((8, 128), F32),
        ],
        in_specs=[hbm] * 13,
        out_specs=[vmem] * 5,
        scratch_shapes=held
        + [
            pltpu.VMEM((MATCH, ROWS, WIDTH), B16),
            pltpu.VMEM((MATCH, ROWS, WIDTH), B16),
            pltpu.VMEM((MATCH, ROWS, WIDTH), B16),
        ]
        + half_scratch(0)
        + half_scratch(1)
        + [
            pltpu.SemaphoreType.DMA((2, SEMS)),
            pltpu.SemaphoreType.DMA((13,)),
        ],
        compiler_params=pltpu.CompilerParams(
            collective_id=0, has_side_effects=True, vmem_limit_bytes=48 * 1024 * 1024
        ),
    )(*[pltpu.with_memory_space_constraint(arg, pltpu.HBM) for arg in args])


WRITTEN = (
    ((1, WIDTH), F32),
    ((WIDTH, WIDTH), F32),
    ((WIDTH, WIDTH), F32),
    ((WIDTH, WIDTH), F32),
    ((WIDTH, WIDTH), F32),
    ((1, WIDTH), F32),
    ((WIDTH, 2 * WIDTH), F32),
    ((2 * WIDTH, WIDTH), F32),
    ((1, HEADS), F32),
    ((1, HEADS), F32),
)


def write_kernel(node_ref, feats_ref, early_full, late_full, small, *refs):
    outs, held, sems = refs[0:12], refs[12:22], refs[22]
    gain1, wq, wk, wv, wout, gain2, up, down, near, far = held

    def copy(number):
        source = (node_ref, feats_ref, *held)[number]
        return pltpu.make_async_copy(source, outs[number], sems.at[number])

    def take(full, half, at, count):
        pieces = full[half, at // PIECE : (at + count) // PIECE]
        return pieces.astype(F32).reshape(count * 8, 128)

    copy(0).start()
    copy(1).start()
    for part in range(2):
        down[:, part * 128 : part * 128 + 128] = take(early_full, 0, part * 64, 64)
    copy(9).start()
    for part in range(4):
        up[:, part * 128 : part * 128 + 128] = take(early_full, 1, part * 32, 32)
    copy(8).start()
    for number, ref in enumerate((wq, wk, wv, wout)):
        for half in range(2):
            ref[:, half * 128 : half * 128 + 128] = take(late_full, half, number * 32, 32)
        copy(3 + number).start()
    for part in range(2):
        gain1[:, part * 128 : part * 128 + 128] = small[part : part + 1, :]
        gain2[:, part * 128 : part * 128 + 128] = small[2 + part : 3 + part, :]
    near[...] = small[4:5, 0:HEADS]
    far[...] = small[4:5, HEADS : 2 * HEADS]
    for number in (2, 7, 10, 11):
        copy(number).start()
    for number in range(12):
        copy(number).wait()


def write_out(*args):
    vmem = pl.BlockSpec(memory_space=pltpu.VMEM)
    hbm = pl.BlockSpec(memory_space=pltpu.HBM)
    rows = ((ROWS, WIDTH), B16)
    return pl.pallas_call(
        write_kernel,
        out_shape=[jax.ShapeDtypeStruct(*shape) for shape in (rows, rows, *WRITTEN)],
        in_specs=[vmem] * 5,
        out_specs=[hbm] * 12,
        scratch_shapes=[pltpu.VMEM(*shape) for shape in WRITTEN]
        + [pltpu.SemaphoreType.DMA((12,))],
        compiler_params=pltpu.CompilerParams(vmem_limit_bytes=48 * 1024 * 1024),
    )(*args)


def local(
    node_feats,
    out_grad,
    norm1_gain,
    w_query,
    w_key,
    w_value,
    w_out,
    norm2_gain,
    w_up,
    w_down,
    local_gain,
    expander_gain,
    partner_perm,
    block_pairs,
    pair_count,
):
    summed = layer(
        node_feats[0],
        out_grad[0],
        norm1_gain[None],
        w_query,
        w_key,
        w_value,
        w_out,
        norm2_gain[None],
        w_up,
        w_down,
        local_gain,
        expander_gain,
        partner_perm[0, :, 0, :],
    )
    node_out, grad_feats, gain1, wq, wk, wv, wout, gain2, up, down, near, far = write_out(*summed)
    return (
        node_out[None],
        grad_feats[None],
        gain1[0],
        wq,
        wk,
        wv,
        wout,
        gain2[0],
        up,
        down,
        near[0],
        far[0],
    )


def solution(mesh):
    return jax.shard_map(
        local,
        mesh=mesh,
        in_specs=(
            P("rep", "dom", None),
            P("rep", "dom", None),
            P(),
            P(),
            P(),
            P(),
            P(),
            P(),
            P(),
            P(),
            P(),
            P(),
            P("rep", None, "dom", None),
            P("rep", "dom", None),
            P("rep", "dom"),
        ),
        out_specs=(
            P("rep", "dom", None),
            P("rep", "dom", None),
            P(),
            P(),
            P(),
            P(),
            P(),
            P(),
            P(),
            P(),
            P(),
            P(),
        ),
        check_vma=False,
    )
```

```python
import jax
import jax.numpy as jnp
from jax import lax
from jax.experimental import pallas as pl
from jax.experimental.pallas import tpu as pltpu
from jax.sharding import PartitionSpec as P

EPSILON = 1e-05
SCORE_CAP = 5.0
GELU_ROOT = 0.7978845608028654
GELU_CUBIC = 0.044715

ROWS = 128
WIDTH = 256
HEADS = 4
HEAD_DIM = 64
MATCH = 4
PARTS = 4
NEAR = 4
PLANE = 16
SHARE = 2
PIECE = NEAR * SHARE
HALF = PLANE * PIECE
MESH = pl.DeviceIdType.MESH
F32 = jnp.float32
B16 = jnp.bfloat16

CORE = 0
PLANE_OUT = 1
NEAR_OUT = 2
FAR_SUM = 3
NEAR_BACK = 4
PLANE_BACK = 5
CORE_BACK = 6
BLOCK = 7
SEND = 2 * BLOCK
RELAY = SEND + PARTS + 2
RETURN = RELAY + PARTS
SEMS = RETURN + 1


def place():
    dom = lax.axis_index("dom")
    rep = lax.axis_index("rep")
    return dom // 8, (dom // 2) % 4, dom % 2, rep


def device(z, y, c, x):
    return {"dom": (z * 4 + y) * 2 + c, "rep": x}


def plane_spot():
    z, y, c, x = place()
    return x * 4 + y


def plane_peer(step):
    z, y, c, x = place()
    far_x = (x + step // 4) % 4
    far_y = (y + step % 4) % 4
    return far_x * 4 + far_y, device(z, far_y, c, far_x)


def near_spot():
    z, y, c, x = place()
    return z % NEAR


def near_peer(step):
    z, y, c, x = place()
    other = (z % NEAR + step) % NEAR
    return other, device((z // NEAR) * NEAR + other, y, c, x)


def far_peer(step):
    z, y, c, x = place()
    return device((z + NEAR * step) % 16, y, c, x)


def partner(matching):
    z, y, c, x = place()
    reach = 8 >> matching
    return device(z + reach - 2 * reach * ((z // reach) % 2), y, c, x)


def relay_target():
    z, y, c, x = place()
    high = z + 8 - 16 * ((z // 8) % 2)
    return device(high + 4 - 8 * ((z // 4) % 2), y, c, x)


def each(first, last, body):
    def step(index, carry):
        body(index)
        return carry

    lax.fori_loop(first, last, step, 0)


def enter():
    z, y, c, x = place()
    barrier = pltpu.get_barrier_semaphore()

    def greet(peer):
        pl.semaphore_signal(barrier, inc=1, device_id=peer, device_id_type=MESH)

    for step in (1, 3):
        greet(far_peer(step))
    for step in range(1, NEAR):
        greet(near_peer(step)[1])
    greet(device(z, y, 1 - c, x))
    each(1, PLANE, lambda step: greet(plane_peer(step)[1]))
    pl.semaphore_wait(barrier, 2 + (NEAR - 1) + 1 + (PLANE - 1))


def remote(src, dst, sems, at, peer):
    return pltpu.make_async_remote_copy(
        src_ref=src,
        dst_ref=dst,
        send_sem=sems.at[0, at],
        recv_sem=sems.at[1, at],
        device_id=peer,
        device_id_type=MESH,
    )


def spread_small(total):
    row = lax.broadcasted_iota(jnp.int32, (8, 128), 0)
    high = total.astype(B16).astype(F32)
    low = pltpu.roll(total - high, 1, 0)
    return jnp.where(row == 5, low, total).astype(B16)


def join_small(parts):
    row = lax.broadcasted_iota(jnp.int32, (8, 128), 0)
    low = pltpu.roll(parts, 7, 0)
    return jnp.where(row == 4, parts + low, parts)


def resum(parts):
    return spread_small(join_small(parts))


def dot(left, right):
    return jnp.dot(left, right, preferred_element_type=F32)


def dot_back(left, right):
    return lax.dot_general(left, right, (((1,), (1,)), ((), ())), preferred_element_type=F32)


def dot_outer(left, right):
    return lax.dot_general(left, right, (((0,), (0,)), ((), ())), preferred_element_type=F32)


def gelu_parts(preact):
    square = preact * preact
    tangent = jnp.tanh(GELU_ROOT * (preact + GELU_CUBIC * square * preact))
    half = 0.5 * (1.0 + tangent)
    result = preact * half
    derivative = half + 0.5 * preact * (1.0 - tangent * tangent) * (
        GELU_ROOT + 3.0 * GELU_ROOT * GELU_CUBIC * square
    )
    return (result, derivative)


def norm_forward(matrix):
    center = jnp.mean(matrix, axis=-1, keepdims=True)
    shifted = matrix - center
    inverse = lax.rsqrt(jnp.mean(shifted * shifted, axis=-1, keepdims=True) + EPSILON)
    return (shifted * inverse, inverse)


def norm_backward(upstream, normed, inverse, gain):
    scaled_up = upstream * gain
    return inverse * (
        scaled_up
        - jnp.mean(scaled_up, axis=-1, keepdims=True)
        - normed * jnp.mean(scaled_up * normed, axis=-1, keepdims=True)
    )


def head_of_lane(shape, axis):
    return lax.broadcasted_iota(jnp.int32, shape, axis) >> 6


def head_sum(products, block_ones):
    high = products.astype(B16)
    low = (products - high.astype(F32)).astype(B16)
    return dot(high, block_ones) + dot(low, block_ones)


def put_units(stage, half, at, matrix):
    units = matrix.shape[0] // 8
    stage[half, at : at + units] = matrix.reshape(units, 8, 128).astype(B16)


def layer_kernel(*refs):
    sources, refs = refs[0:13], refs[13:]
    node_out_ref, grad_feats_ref, early_full, late_full, small_ref = refs[0:5]
    held, refs = refs[5:18], refs[18:]
    (
        feats_ref,
        up_ref,
        gain1_ref,
        wq_ref,
        wk_ref,
        wv_ref,
        wo_ref,
        gain2_ref,
        wup_ref,
        wdn_ref,
        local_ref,
        far_ref,
        perm_ref,
    ) = held
    far_in, back_out, back_in = refs[0:3]
    halves = (refs[3:11], refs[11:19])
    sems, load_sems = refs[19:21]
    fulls = (early_full, late_full)
    early_stage, late_stage = halves[0][0], halves[1][0]

    def load(number):
        return pltpu.make_async_copy(sources[number], held[number], load_sems.at[number])

    for number in (0, 2, 3, 4, 5, 10, 11, 12, 1, 9, 6, 7, 8):
        load(number).start()
    z, y, c, x = place()
    sibling = device(z, y, 1 - c, x)
    enter()

    pieces = [pl.ds(at, ROWS // PARTS) for at in range(0, ROWS, ROWS // PARTS)]

    def far_out(matching):
        return remote(
            sources[0], far_in.at[matching], sems, SEND + PARTS + matching - 2, partner(matching)
        )

    def far_piece(part):
        rows = pieces[part]
        return remote(
            sources[0].at[rows], far_in.at[1, rows], sems, SEND + part, partner(1)
        )

    def far_relay(part):
        rows = pieces[part]
        return remote(
            far_in.at[1, rows], far_in.at[0, rows], sems, RELAY + part, relay_target()
        )

    def far_back(matching):
        return remote(
            back_out.at[matching],
            back_in.at[matching],
            sems,
            RETURN,
            partner(matching),
        )

    for part in range(PARTS):
        far_piece(part).start()
    far_out(2).start()
    far_out(3).start()

    for number in (0, 2, 3, 4, 5, 10, 11, 12):
        load(number).wait()
    lane_head = head_of_lane((1, WIDTH), 1)
    masks = [jnp.where(lane_head == head, 1.0, 0.0) for head in range(HEADS)]
    masks16 = [mask.astype(B16) for mask in masks]
    ones_rows = head_of_lane((WIDTH, WIDTH), 0)
    ones_lanes = head_of_lane((WIDTH, WIDTH), 1)
    block_ones = jnp.where(ones_rows == ones_lanes, 1.0, 0.0).astype(B16)
    far_gain = sum(masks[head] * far_ref[head] for head in range(HEADS))

    def stacked(matrix):
        return jnp.concatenate([matrix * mask for mask in masks16], axis=0)

    gain1 = gain1_ref[...]
    wk = wk_ref[...]
    wv = wv_ref[...]
    features = feats_ref[...].astype(F32)
    normed1, inverse1 = norm_forward(features)
    hidden = (normed1 * gain1).astype(B16)
    query = dot(hidden, wq_ref[...]).astype(B16)
    key = dot(hidden, wk).astype(B16)
    value = dot(hidden, wv).astype(B16)
    query32 = query.astype(F32)
    query_stack = stacked(query)
    raw_all = dot_back(query_stack, key) * (1.0 / 8.0)
    raws, tangents, exps = [], [], []
    denominator = jnp.zeros((ROWS, WIDTH), F32)
    for head in range(HEADS):
        raw = raw_all[head * ROWS : (head + 1) * ROWS]
        tangent = jnp.tanh(raw * (local_ref[head] / SCORE_CAP))
        exped = jnp.exp(SCORE_CAP * tangent)
        denominator = denominator + masks[head] * jnp.sum(exped, axis=1, keepdims=True)
        raws.append(raw)
        tangents.append(tangent)
        exps.append(exped)
    for number in (1, 9, 6, 7, 8):
        load(number).wait()
    gain2 = gain2_ref[...]
    upstream = up_ref[...]
    grad_act = dot_back(upstream, wdn_ref[...])

    for part in range(PARTS):
        far_piece(part).wait_recv()
        far_relay(part).start()
    one_hots, far_norms, far_hiddens, far_keys, far_values = {}, {}, {}, {}, {}
    far_raws, far_tangents, far_exps = {}, {}, {}
    rows = lax.broadcasted_iota(jnp.int32, (ROWS, ROWS), 0)
    for matching in reversed(range(MATCH)):
        one_hot = jnp.where(rows == perm_ref[matching : matching + 1, :], 1.0, 0.0)
        one_hots[matching] = one_hot.astype(B16)
        if matching >= 2:
            far_out(matching).wait_recv()
        elif matching == 0:
            for part in range(PARTS):
                far_relay(part).wait_recv()
        picked = dot_outer(one_hots[matching], far_in[matching])
        normed, _ = norm_forward(picked)
        far_norms[matching] = normed
        far_hiddens[matching] = (normed * gain1).astype(B16)
        far_keys[matching] = dot(far_hiddens[matching], wk).astype(B16)
        far_values[matching] = dot(far_hiddens[matching], wv).astype(B16)
        raw = head_sum(query32 * far_keys[matching].astype(F32), block_ones) * (1.0 / 8.0)
        tangent = jnp.tanh(raw * (far_gain * (1.0 / SCORE_CAP)))
        exped = jnp.exp(SCORE_CAP * tangent)
        denominator = denominator + exped
        far_raws[matching] = raw
        far_tangents[matching] = tangent
        far_exps[matching] = exped

    inverse_den = 1.0 / denominator
    weights = [
        (exps[head] * inverse_den[:, head * HEAD_DIM : head * HEAD_DIM + 1]).astype(B16)
        for head in range(HEADS)
    ]
    weight_lanes = jnp.concatenate(weights, axis=1)
    attended32 = dot(weight_lanes, stacked(value))
    far_weights = {}
    for matching in range(MATCH):
        weight = (far_exps[matching] * inverse_den).astype(B16).astype(F32)
        far_weights[matching] = weight
        attended32 = attended32 + weight * far_values[matching].astype(F32)
    attended = attended32.astype(B16)

    mixed = (features + dot(attended, wo_ref[...])).astype(B16).astype(F32)
    normed2, inverse2 = norm_forward(mixed)
    hidden2 = (normed2 * gain2).astype(B16)
    activ, derivative = gelu_parts(dot(hidden2, wup_ref[...]))
    activ = activ.astype(B16)
    grad_pre = (grad_act * derivative).astype(B16)
    grad_hidden2 = dot_back(grad_pre, wup_ref[...])
    grad_mixed = upstream.astype(F32) + norm_backward(grad_hidden2, normed2, inverse2, gain2)
    grad_mixed16 = grad_mixed.astype(B16)
    grad_att = dot_back(grad_mixed16, wo_ref[...]).astype(B16)
    node_out_ref[...] = (mixed + dot(activ, wdn_ref[...])).astype(B16)
    grad_gain2 = jnp.sum(grad_hidden2 * normed2, axis=0, keepdims=True)

    def core_copy(half):
        stage, core_in = halves[half][0:2]
        return remote(stage.at[1 - c], core_in, sems, half * BLOCK + CORE, sibling)

    grad_down = dot_outer(activ, upstream)
    grad_up = dot_outer(hidden2, grad_pre)
    for part in range(2):
        put_units(early_stage, 0, part * 64, grad_down[:, part * 128 : part * 128 + 128])
    for part in range(4):
        put_units(early_stage, 1, part * 32, grad_up[:, part * 128 : part * 128 + 128])
    core_copy(0).start()
    grad_wout = dot_outer(attended, grad_mixed16)

    grad_att32 = grad_att.astype(F32)
    grad_stack = stacked(grad_att)
    delta = head_sum(grad_att32 * attended32, block_ones)
    far_gain_row = jnp.zeros((1, WIDTH), F32)
    grad_query32 = jnp.zeros((ROWS, WIDTH), F32)
    grad_gain1 = jnp.zeros((1, WIDTH), F32)
    key_terms, value_terms = {}, {}
    for matching in range(MATCH):
        weight = far_weights[matching]
        dots = head_sum(grad_att32 * far_values[matching].astype(F32), block_ones)
        dlogit = weight * (dots - delta)
        sloped = dlogit * (1.0 - far_tangents[matching] * far_tangents[matching])
        far_gain_row = far_gain_row + jnp.sum(
            sloped * far_raws[matching], axis=0, keepdims=True
        )
        dscore = (sloped * (far_gain * (1.0 / 8.0))).astype(B16).astype(F32)
        grad_query32 = grad_query32 + dscore * far_keys[matching].astype(F32)
        key_terms[matching] = (dscore * query32).astype(B16)
        value_terms[matching] = (weight * grad_att32).astype(B16)
        returned = dot_back(key_terms[matching], wk) + dot_back(value_terms[matching], wv)
        grad_gain1 = grad_gain1 + jnp.sum(
            returned * far_norms[matching], axis=0, keepdims=True
        )
        back_out[matching] = dot(one_hots[matching], returned.astype(B16)).astype(B16)
        far_back(matching).start()

    def stage_copy(src, dst, half, stage, where):
        return remote(src, dst, sems, half * BLOCK + stage, where)

    def stage_wait(whole, half, stage):
        return stage_copy(whole, whole, half, stage, sibling)

    def plane_copy(half, step):
        plane_out, plane_in = halves[half][2:4]
        peer, where = plane_peer(step)
        return stage_copy(plane_out.at[peer], plane_in.at[step], half, PLANE_OUT, where)

    def near_copy(half, step):
        near_out, near_in = halves[half][4:6]
        peer, where = near_peer(step)
        return stage_copy(near_out.at[peer], near_in.at[step], half, NEAR_OUT, where)

    def far_copy(half, step):
        far_sum = halves[half][6]
        return stage_copy(far_sum.at[0], far_sum.at[step], half, FAR_SUM, far_peer(step))

    def near_back(half, step):
        slot = halves[half][7].at[near_spot()]
        return stage_copy(slot, slot, half, NEAR_BACK, near_peer(step)[1])

    def plane_back(half, step):
        slot = fulls[half].at[c, plane_spot()]
        return stage_copy(slot, slot, half, PLANE_BACK, plane_peer(step)[1])

    def core_back(half):
        slot = fulls[half].at[c]
        return stage_copy(slot, slot, half, CORE_BACK, sibling)

    def plane_wait(half):
        return stage_wait(halves[half][3].at[1:PLANE], half, PLANE_OUT)

    def near_wait(half):
        return stage_wait(halves[half][5].at[1:NEAR], half, NEAR_OUT)

    def far_wait(half):
        return stage_wait(halves[half][6].at[1:NEAR], half, FAR_SUM)

    def near_back_wait(half):
        return stage_wait(halves[half][7].at[1:NEAR], half, NEAR_BACK)

    def plane_back_wait(half):
        return stage_wait(fulls[half].at[c, 1:PLANE], half, PLANE_BACK)

    def sum_core(half):
        stage, core_in, plane_out = halves[half][0:3]
        core_copy(half).wait_recv()
        plane_out[:, 0:PIECE] = (
            (stage[c, 0:HALF].astype(F32) + core_in[0:HALF].astype(F32))
            .astype(B16)
            .reshape(PLANE, PIECE, 8, 128)
        )
        if half == 1:
            small16 = resum(stage[0, HALF].astype(F32) + core_in[HALF].astype(F32))
            for piece in range(PLANE):
                plane_out[piece, PIECE] = small16
        each(1, PLANE, lambda step: plane_copy(half, (step * 7) % PLANE).start())

    def sum_plane(half):
        plane_out, plane_in, near_out = halves[half][2:5]
        plane_wait(half).wait_recv()
        total = plane_out[plane_spot()].astype(F32)
        for step in range(1, PLANE):
            total = total + plane_in[step].astype(F32)
        near_out[:, 0:SHARE] = total[0:PIECE].astype(B16).reshape(NEAR, SHARE, 8, 128)
        if half == 1:
            small16 = resum(total[PIECE])
            for part in range(NEAR):
                near_out[part, SHARE] = small16
        for step in range(1, NEAR):
            near_copy(half, step).start()

    def sum_near(half):
        near_out, near_in, far_sum = halves[half][4:7]
        near_wait(half).wait_recv()
        total = near_out[near_spot()].astype(F32)
        for step in range(1, NEAR):
            total = total + near_in[step].astype(F32)
        far_sum[0, 0:SHARE] = total[0:SHARE].astype(B16)
        if half == 1:
            far_sum[0, SHARE] = resum(total[SHARE])
        for step in range(1, NEAR):
            far_copy(half, step).start()

    def sum_far(half):
        far_sum, last = halves[half][6:8]
        far_wait(half).wait_recv()
        total = far_sum[0].astype(F32)
        for step in range(1, NEAR):
            total = total + far_sum[step].astype(F32)
        last[near_spot()] = total[0:SHARE].astype(B16)
        for step in range(1, NEAR):
            near_back(half, step).start()
        if half == 1:
            small_ref[...] = join_small(total[SHARE])

    def give_plane(half):
        near_back_wait(half).wait_recv()
        fulls[half][c, plane_spot()] = halves[half][7][...].reshape(PIECE, 8, 128)
        each(1, PLANE, lambda step: plane_back(half, (step * 7) % PLANE).start())

    def give_core(half):
        plane_back_wait(half).wait_recv()
        core_back(half).start()

    def finish(half):
        core_copy(half).wait_send()
        plane_wait(half).wait_send()
        near_wait(half).wait_send()
        far_wait(half).wait_send()
        near_back_wait(half).wait_send()
        plane_back_wait(half).wait_send()
        core_back(half).wait()

    dots_all = dot_back(grad_stack, value)
    lane = lax.broadcasted_iota(jnp.int32, (1, 128), 1)
    gain_row = jnp.zeros((1, 128), F32)
    dscores = []
    for head in range(HEADS):
        dots = dots_all[head * ROWS : (head + 1) * ROWS]
        delta_column = delta[:, head * HEAD_DIM : head * HEAD_DIM + 1]
        dlogit = weights[head].astype(F32) * (dots - delta_column)
        sloped = dlogit * (1.0 - tangents[head] * tangents[head])
        local_sum = jnp.sum(
            jnp.sum(sloped * raws[head], axis=0, keepdims=True), axis=1, keepdims=True
        )
        far_sum = far_gain_row[:, head * HEAD_DIM : head * HEAD_DIM + 1]
        gain_row = jnp.where(lane == head, local_sum, gain_row)
        gain_row = jnp.where(lane == HEADS + head, far_sum, gain_row)
        dscores.append((sloped * (local_ref[head] / 8.0)).astype(B16))
    grad_query = (
        grad_query32 + dot(jnp.concatenate(dscores, axis=1), stacked(key))
    ).astype(B16)
    grad_key = dot_outer(jnp.concatenate(dscores, axis=0), query_stack).astype(B16)
    grad_value = dot_outer(jnp.concatenate(weights, axis=0), grad_stack).astype(B16)
    order = list(range(MATCH))
    all_hidden = jnp.concatenate([hidden] + [far_hiddens[m] for m in order], axis=0)
    grad_wq = dot_outer(hidden, grad_query)
    grad_wk = dot_outer(
        all_hidden, jnp.concatenate([grad_key] + [key_terms[m] for m in order], axis=0)
    )
    grad_wv = dot_outer(
        all_hidden, jnp.concatenate([grad_value] + [value_terms[m] for m in order], axis=0)
    )
    grad_hidden = (
        dot_back(grad_query, wq_ref[...]) + dot_back(grad_key, wk) + dot_back(grad_value, wv)
    )
    grad_gain1 = grad_gain1 + jnp.sum(grad_hidden * normed1, axis=0, keepdims=True)
    for number, grad in enumerate((grad_wq, grad_wk, grad_wv, grad_wout)):
        for part in range(2):
            put_units(late_stage, part, number * 32, grad[:, part * 128 : part * 128 + 128])
    small = jnp.concatenate(
        [
            grad_gain1[:, 0:128],
            grad_gain1[:, 128:256],
            grad_gain2[:, 0:128],
            grad_gain2[:, 128:256],
            gain_row,
            jnp.zeros((3, 128), F32),
        ],
        axis=0,
    )
    small16 = spread_small(small)
    late_stage[0, HALF] = small16
    late_stage[1, HALF] = small16
    core_copy(1).start()
    sum_core(0)
    sum_core(1)
    sum_plane(0)
    sum_plane(1)
    sum_near(0)
    sum_near(1)

    remote(back_out, back_in, sems, RETURN, sibling).wait_recv()
    for matching in range(MATCH):
        grad_hidden = grad_hidden + back_in[matching].astype(F32)
    grad_feats_ref[...] = (
        grad_mixed + norm_backward(grad_hidden, normed1, inverse1, gain1)
    ).astype(B16)

    sum_far(0)
    sum_far(1)
    give_plane(0)
    give_plane(1)
    give_core(0)
    give_core(1)
    finish(0)
    finish(1)
    for part in range(PARTS):
        far_piece(part).wait_send()
        far_relay(part).wait_send()
    far_out(2).wait_send()
    far_out(3).wait_send()
    remote(back_out, back_in, sems, RETURN, sibling).wait_send()


def half_scratch(extra):
    shapes = [
        (2, HALF + extra),
        (HALF + extra,),
        (PLANE, PIECE + extra),
        (PLANE, PIECE + extra),
        (NEAR, SHARE + extra),
        (NEAR, SHARE + extra),
        (NEAR, SHARE + extra),
        (NEAR, SHARE),
    ]
    return [pltpu.VMEM((*shape, 8, 128), B16) for shape in shapes]


def layer(*args):
    vmem = pl.BlockSpec(memory_space=pltpu.VMEM)
    hbm = pl.BlockSpec(memory_space=pltpu.HBM)
    held = [
        pltpu.SMEM(arg.shape, arg.dtype) if number in (10, 11) else pltpu.VMEM(arg.shape, arg.dtype)
        for number, arg in enumerate(args)
    ]
    return pl.pallas_call(
        layer_kernel,
        out_shape=[
            jax.ShapeDtypeStruct((ROWS, WIDTH), B16),
            jax.ShapeDtypeStruct((ROWS, WIDTH), B16),
            jax.ShapeDtypeStruct((2, PLANE, PIECE, 8, 128), B16),
            jax.ShapeDtypeStruct((2, PLANE, PIECE, 8, 128), B16),
            jax.ShapeDtypeStruct((8, 128), F32),
        ],
        in_specs=[hbm] * 13,
        out_specs=[vmem] * 5,
        scratch_shapes=held
        + [
            pltpu.VMEM((MATCH, ROWS, WIDTH), B16),
            pltpu.VMEM((MATCH, ROWS, WIDTH), B16),
            pltpu.VMEM((MATCH, ROWS, WIDTH), B16),
        ]
        + half_scratch(0)
        + half_scratch(1)
        + [
            pltpu.SemaphoreType.DMA((2, SEMS)),
            pltpu.SemaphoreType.DMA((13,)),
        ],
        compiler_params=pltpu.CompilerParams(
            collective_id=0, has_side_effects=True, vmem_limit_bytes=48 * 1024 * 1024
        ),
    )(*[pltpu.with_memory_space_constraint(arg, pltpu.HBM) for arg in args])


WRITTEN = (
    ((1, WIDTH), F32),
    ((WIDTH, WIDTH), F32),
    ((WIDTH, WIDTH), F32),
    ((WIDTH, WIDTH), F32),
    ((WIDTH, WIDTH), F32),
    ((1, WIDTH), F32),
    ((WIDTH, 2 * WIDTH), F32),
    ((2 * WIDTH, WIDTH), F32),
    ((1, HEADS), F32),
    ((1, HEADS), F32),
)


def write_kernel(node_ref, feats_ref, early_full, late_full, small, *refs):
    outs, held, sems = refs[0:12], refs[12:22], refs[22]
    gain1, wq, wk, wv, wout, gain2, up, down, near, far = held

    def copy(number):
        source = (node_ref, feats_ref, *held)[number]
        return pltpu.make_async_copy(source, outs[number], sems.at[number])

    def take(full, half, at, count):
        pieces = full[half, at // PIECE : (at + count) // PIECE]
        return pieces.astype(F32).reshape(count * 8, 128)

    copy(0).start()
    copy(1).start()
    for part in range(2):
        down[:, part * 128 : part * 128 + 128] = take(early_full, 0, part * 64, 64)
    copy(9).start()
    for part in range(4):
        up[:, part * 128 : part * 128 + 128] = take(early_full, 1, part * 32, 32)
    copy(8).start()
    for number, ref in enumerate((wq, wk, wv, wout)):
        for half in range(2):
            ref[:, half * 128 : half * 128 + 128] = take(late_full, half, number * 32, 32)
        copy(3 + number).start()
    for part in range(2):
        gain1[:, part * 128 : part * 128 + 128] = small[part : part + 1, :]
        gain2[:, part * 128 : part * 128 + 128] = small[2 + part : 3 + part, :]
    near[...] = small[4:5, 0:HEADS]
    far[...] = small[4:5, HEADS : 2 * HEADS]
    for number in (2, 7, 10, 11):
        copy(number).start()
    for number in range(12):
        copy(number).wait()


def write_out(*args):
    vmem = pl.BlockSpec(memory_space=pltpu.VMEM)
    hbm = pl.BlockSpec(memory_space=pltpu.HBM)
    rows = ((ROWS, WIDTH), B16)
    return pl.pallas_call(
        write_kernel,
        out_shape=[jax.ShapeDtypeStruct(*shape) for shape in (rows, rows, *WRITTEN)],
        in_specs=[vmem] * 5,
        out_specs=[hbm] * 12,
        scratch_shapes=[pltpu.VMEM(*shape) for shape in WRITTEN]
        + [pltpu.SemaphoreType.DMA((12,))],
        compiler_params=pltpu.CompilerParams(vmem_limit_bytes=48 * 1024 * 1024),
    )(*args)


def local(
    node_feats,
    out_grad,
    norm1_gain,
    w_query,
    w_key,
    w_value,
    w_out,
    norm2_gain,
    w_up,
    w_down,
    local_gain,
    expander_gain,
    partner_perm,
    block_pairs,
    pair_count,
):
    summed = layer(
        node_feats[0],
        out_grad[0],
        norm1_gain[None],
        w_query,
        w_key,
        w_value,
        w_out,
        norm2_gain[None],
        w_up,
        w_down,
        local_gain,
        expander_gain,
        partner_perm[0, :, 0, :],
    )
    node_out, grad_feats, gain1, wq, wk, wv, wout, gain2, up, down, near, far = write_out(*summed)
    return (
        node_out[None],
        grad_feats[None],
        gain1[0],
        wq,
        wk,
        wv,
        wout,
        gain2[0],
        up,
        down,
        near[0],
        far[0],
    )


def solution(mesh):
    return jax.shard_map(
        local,
        mesh=mesh,
        in_specs=(
            P("rep", "dom", None),
            P("rep", "dom", None),
            P(),
            P(),
            P(),
            P(),
            P(),
            P(),
            P(),
            P(),
            P(),
            P(),
            P("rep", None, "dom", None),
            P("rep", "dom", None),
            P("rep", "dom"),
        ),
        out_specs=(
            P("rep", "dom", None),
            P("rep", "dom", None),
            P(),
            P(),
            P(),
            P(),
            P(),
            P(),
            P(),
            P(),
            P(),
            P(),
        ),
        check_vma=False,
    )
```
